512 devices in a mesh: ab: 32 (over z, x), cd: 16 (over y, core).
Axes of the slice: x: 4, y: 8, z: 8, core: 2. Of those that a mesh axis runs over, the one named last changes fastest.
Arguments:
- amplitudes: float32 [512, 8192], P('ab', 'cd'), may hold values from -6 to 6
- integrals: float32 [65536, 8192], P('ab', 'cd'), may hold values from -0.125 to 0.125
- ij_pairs: int32 [512, 2], P('cd'), may hold values from 0 to 127
- ab_pairs: int32 [65536, 2], P('ab'), may hold values from 0 to 1535
- eps_occ: float32 [128], replicated, may hold values from -1.5 to -0.3
- eps_vir: float32 [1536], replicated, may hold values from 0.1 to 2.5
Outputs:
- ladder: float32 [512, 65536], P('cd', 'ab')
- update: float32 [512, 65536], P('cd', 'ab')
The draws below stay inside these ranges and needn't reach their ends.
All inputs are finite; a program needn't handle non-finite values.
Results may differ from the reference program's by a relative error of at most 0.00015.
Values sent between devices are 32-bit elements; how exact they have to be, the bound alone decides.
A program may use at most 64 MiB of HBM per device.

```python
import jax
import jax.numpy as jnp
from jax import lax

NO = 128
NV = 1536
CD = 8192
IJ = 512
AB = 65536


def place_ends(result, own_key, smallest, top_value):
    longest = result.shape.index(max(result.shape))
    spots = []
    for shift in (0, 1):
        where = [jax.random.randint(jax.random.fold_in(own_key, axis), (), 0, length) for axis, length in enumerate(result.shape)]
        where[longest] = (where[longest] + shift) % result.shape[longest]
        spots.append(tuple(where))
    return result.at[spots[0]].set(smallest).at[spots[1]].set(top_value)


def strengthened(values, own_key, source, target, parts, factor):
    owner, partner = [(jnp.arange(values.shape[axis_at]) // (values.shape[axis_at] // parts)).reshape([-1 if axis == axis_at else 1 for axis in range(values.ndim)]) for axis_at in (source, target)]
    chosen = jax.random.permutation(own_key, parts)[partner]
    strong = (owner == chosen) | (owner == (partner + parts // 2) % parts)
    return jnp.where(strong, factor * values, values)


def block_levels(rng, dims, split, low, largest):
    level, own = 1.0, jax.random.fold_in(rng, 6)
    for dim, shards_of in split:
        draws = jnp.exp(jax.random.uniform(jax.random.fold_in(own, dim), (shards_of,), jnp.float32, low / len(split), largest / len(split)))
        level = level * jnp.repeat(draws, dims[dim] // shards_of).reshape([-1 if axis == dim else 1 for axis in range(len(dims))])
    return level


def scatter_about(key, shape, deviation, reach, split=(), dtype=jnp.bfloat16):
    values = deviation * jax.random.normal(key, shape, jnp.float32)
    if split:
        values = values * block_levels(key, shape, split, -0.22, 0.18)
    return jnp.clip(values, -reach, reach).astype(dtype)


def heavy_noise(key, dims, spread, most, shards, heavy, held_as=jnp.bfloat16):
    entries = spread * jax.random.normal(key, dims, jnp.float32)
    if shards:
        entries = entries * block_levels(key, dims, shards, -0.22, 0.18)
    return jnp.clip(strengthened(entries, jax.random.fold_in(key, 3), *heavy), -most, most).astype(held_as)


def setup_inputs(seed: int = 0) -> dict:
    keys = jax.random.split(jax.random.key(seed), 7)
    amplitudes = heavy_noise(keys[0], (IJ, CD), 1.0, 6.0, ((0, 32), (1, 16)), (1, 0, 32, 2.75), jnp.float32)
    integrals = scatter_about(keys[1], (AB, CD), (CD // 4) ** -0.5, 0.125, ((0, 32), (1, 16)), jnp.float32)
    ij_pairs = place_ends(jax.random.randint(keys[2], (IJ, 2), 0, NO), jax.random.fold_in(keys[2], 1), 0, NO - 1).astype(jnp.int32)
    ab_pairs = place_ends(jax.random.randint(keys[3], (AB, 2), 0, NV), jax.random.fold_in(keys[3], 1), 0, NV - 1).astype(jnp.int32)
    eps_occ = jnp.clip(jax.random.uniform(keys[4], (NO,), jnp.float32, -1.5, -0.3), -1.5, -0.3)
    eps_vir = jnp.clip(jax.random.uniform(keys[5], (NV,), jnp.float32, 0.1, 2.5), 0.1, 2.5)
    return dict(amplitudes=amplitudes, integrals=integrals, ij_pairs=ij_pairs, ab_pairs=ab_pairs, eps_occ=eps_occ, eps_vir=eps_vir)


def reference(amplitudes, integrals, ij_pairs, ab_pairs, eps_occ, eps_vir):
    ladder = lax.dot_general(amplitudes, integrals, (((1,), (1,)), ((), ())), precision=lax.Precision.HIGHEST, preferred_element_type=jnp.float32)
    first_occ = eps_occ[ij_pairs[:, 0]][:, None]
    second_occ = eps_occ[ij_pairs[:, 1]][:, None]
    first_vir = eps_vir[ab_pairs[:, 0]][None, :]
    second_vir = eps_vir[ab_pairs[:, 1]][None, :]
    denominator = first_occ + second_occ - first_vir - second_vir
    update = ladder / denominator
    return ladder, update
```

```python
import functools

import jax
import jax.numpy as jnp
from jax import lax
from jax.experimental import pallas as pl
from jax.experimental.pallas import tpu as pltpu
from jax.sharding import PartitionSpec as P

MESH = pl.DeviceIdType.MESH


def lookup_energy(indices, energies):
    positions = lax.broadcasted_iota(jnp.int32, (indices.shape[0], energies.shape[0]), 1)
    picked = jnp.where(indices[:, None] == positions, energies[None, :], jnp.float32(0.0))
    return jnp.sum(picked, axis=1)


def contract_rows(row_block, col_block):
    return lax.dot_general(
        row_block,
        col_block,
        (((1,), (1,)), ((), ())),
        precision=lax.Precision.HIGHEST,
        preferred_element_type=jnp.float32,
    )


def gather_kernel(n, amp_ref, out_ref, held, send_sems, recv_sems):
    me = lax.axis_index("ab")
    cd = lax.axis_index("cd")
    rows = amp_ref.shape[0]

    barrier = pltpu.get_barrier_semaphore()

    def greet(i, carry):
        peer = lax.rem(me + i, n)
        pl.semaphore_signal(barrier, inc=1, device_id=(peer, cd), device_id_type=MESH)
        return carry

    lax.fori_loop(1, n, greet, 0)
    pl.semaphore_wait(barrier, n - 1)

    mine = pl.ds(pl.multiple_of(me * rows, rows), rows)

    def copy_to(peer):
        return pltpu.make_async_remote_copy(
            src_ref=amp_ref,
            dst_ref=held.at[mine],
            send_sem=send_sems.at[peer],
            recv_sem=recv_sems.at[me],
            device_id=(peer, cd),
            device_id_type=MESH,
        )

    def copy_from(peer):
        theirs = pl.ds(pl.multiple_of(peer * rows, rows), rows)
        return pltpu.make_async_remote_copy(
            src_ref=amp_ref,
            dst_ref=held.at[theirs],
            send_sem=send_sems.at[peer],
            recv_sem=recv_sems.at[peer],
            device_id=(peer, cd),
            device_id_type=MESH,
        )

    def send(i, carry):
        copy_to(lax.rem(me + i, n)).start()
        return carry

    lax.fori_loop(1, n, send, 0)
    held[mine, :] = amp_ref[...]

    def finish(i, carry):
        copy_to(lax.rem(me + i, n)).wait_send()
        copy_from(lax.rem(me + n - i, n)).wait_recv()
        return carry

    lax.fori_loop(1, n, finish, 0)
    out_ref[...] = held[...]


def gather_rows(amplitudes, n):
    rows, cols = amplitudes.shape
    return pl.pallas_call(
        functools.partial(gather_kernel, n),
        out_shape=jax.ShapeDtypeStruct((rows * n, cols), amplitudes.dtype),
        in_specs=[pl.BlockSpec(memory_space=pltpu.VMEM)],
        out_specs=pl.BlockSpec(memory_space=pltpu.VMEM),
        scratch_shapes=[
            pltpu.VMEM((rows * n, cols), amplitudes.dtype),
            pltpu.SemaphoreType.DMA((n,)),
            pltpu.SemaphoreType.DMA((n,)),
        ],
        compiler_params=pltpu.CompilerParams(collective_id=0, has_side_effects=True),
    )(amplitudes)


def on_device(n_ab, amplitudes, integrals, ij_pairs, ab_pairs, eps_occ, eps_vir):
    partial_value = contract_rows(gather_rows(amplitudes, n_ab), integrals)
    ladder = lax.psum_scatter(partial_value, "cd", scatter_dimension=0, tiled=True)
    first_occ = lookup_energy(ij_pairs[:, 0], eps_occ)[:, None]
    second_occ = lookup_energy(ij_pairs[:, 1], eps_occ)[:, None]
    first_vir = lookup_energy(ab_pairs[:, 0], eps_vir)[None, :]
    second_vir = lookup_energy(ab_pairs[:, 1], eps_vir)[None, :]
    denominator = first_occ + second_occ - first_vir - second_vir
    update = ladder / denominator
    return (ladder, update)


def solution(mesh):
    in_specs = (P("ab", "cd"), P("ab", "cd"), P("cd", None), P("ab", None), P(), P())
    out_specs = (P("cd", "ab"), P("cd", "ab"))
    return jax.shard_map(
        functools.partial(on_device, mesh.shape["ab"]),
        mesh=mesh,
        in_specs=in_specs,
        out_specs=out_specs,
        check_vma=False,
    )
```

```python
import functools

import jax
import jax.numpy as jnp
from jax import lax
from jax.experimental import pallas as pl
from jax.experimental.pallas import tpu as pltpu
from jax.sharding import PartitionSpec as P

MESH = pl.DeviceIdType.MESH


def lookup_energy(indices, energies):
    positions = lax.broadcasted_iota(jnp.int32, (indices.shape[0], energies.shape[0]), 1)
    picked = jnp.where(indices[:, None] == positions, energies[None, :], jnp.float32(0.0))
    return jnp.sum(picked, axis=1)


def contract_rows(row_block, col_block):
    return lax.dot_general(
        row_block,
        col_block,
        (((1,), (1,)), ((), ())),
        precision=lax.Precision.HIGHEST,
        preferred_element_type=jnp.float32,
    )


def gather_kernel(n, amp_ref, out_ref, held, send_sems, recv_sems):
    me = lax.axis_index("ab")
    cd = lax.axis_index("cd")
    rows = amp_ref.shape[0]

    barrier = pltpu.get_barrier_semaphore()

    def greet(i, carry):
        peer = lax.rem(me + i, n)
        pl.semaphore_signal(barrier, inc=1, device_id=(peer, cd), device_id_type=MESH)
        return carry

    lax.fori_loop(1, n, greet, 0)
    pl.semaphore_wait(barrier, n - 1)

    mine = pl.ds(pl.multiple_of(me * rows, rows), rows)

    def copy_to(peer):
        return pltpu.make_async_remote_copy(
            src_ref=amp_ref,
            dst_ref=held.at[mine],
            send_sem=send_sems.at[peer],
            recv_sem=recv_sems.at[me],
            device_id=(peer, cd),
            device_id_type=MESH,
        )

    def copy_from(peer):
        theirs = pl.ds(pl.multiple_of(peer * rows, rows), rows)
        return pltpu.make_async_remote_copy(
            src_ref=amp_ref,
            dst_ref=held.at[theirs],
            send_sem=send_sems.at[peer],
            recv_sem=recv_sems.at[peer],
            device_id=(peer, cd),
            device_id_type=MESH,
        )

    def send(i, carry):
        copy_to(lax.rem(me + i, n)).start()
        return carry

    lax.fori_loop(1, n, send, 0)
    held[mine, :] = amp_ref[...]

    def finish(i, carry):
        copy_to(lax.rem(me + i, n)).wait_send()
        copy_from(lax.rem(me + n - i, n)).wait_recv()
        return carry

    lax.fori_loop(1, n, finish, 0)
    out_ref[...] = held[...]


def gather_rows(amplitudes, n):
    rows, cols = amplitudes.shape
    return pl.pallas_call(
        functools.partial(gather_kernel, n),
        out_shape=jax.ShapeDtypeStruct((rows * n, cols), amplitudes.dtype),
        in_specs=[pl.BlockSpec(memory_space=pltpu.VMEM)],
        out_specs=pl.BlockSpec(memory_space=pltpu.VMEM),
        scratch_shapes=[
            pltpu.VMEM((rows * n, cols), amplitudes.dtype),
            pltpu.SemaphoreType.DMA((n,)),
            pltpu.SemaphoreType.DMA((n,)),
        ],
        compiler_params=pltpu.CompilerParams(collective_id=0, has_side_effects=True),
    )(amplitudes)


def scatter_kernel(n_y, part_ref, out_ref, pair, send_r, recv_r, send_l, recv_l,
                   pair_send, pair_recv, ring_send, ring_recv):
    ab = lax.axis_index("ab")
    cd = lax.axis_index("cd")
    y, core = cd // 2, lax.rem(cd, 2)
    other = 1 - core
    right = lax.rem(y + 1, n_y) * 2 + core
    left = lax.rem(y + n_y - 1, n_y) * 2 + core
    partner = y * 2 + other
    half = out_ref.shape[1] // 2

    barrier = pltpu.get_barrier_semaphore()
    for peer in (partner, right, left):
        pl.semaphore_signal(barrier, inc=1, device_id=(ab, peer), device_id_type=MESH)
    pl.semaphore_wait(barrier, 3)

    order = []
    for k in list(range(1, n_y // 2 + 1)) + [0]:
        for sign in (1, -1):
            if (sign * k) % n_y not in [j % n_y for j in order]:
                order.append(sign * k)

    def pair_copy(k):
        b = lax.rem(y + k + n_y, n_y)
        return pltpu.make_async_remote_copy(
            src_ref=part_ref.at[b, other],
            dst_ref=pair.at[b],
            send_sem=pair_send.at[b],
            recv_sem=pair_recv.at[b],
            device_id=(ab, partner),
            device_id_type=MESH,
        )

    for k in order:
        pair_copy(k).start()

    def own(k, cols):
        b = lax.rem(y + k + n_y, n_y)
        return part_ref[b, core, :, cols] + pair[b, :, cols]

    lo, hi = slice(0, half), slice(half, 2 * half)

    def ring_copy(d, s):
        src, dst = (send_r, recv_r) if d == 0 else (send_l, recv_l)
        return pltpu.make_async_remote_copy(
            src_ref=src.at[s],
            dst_ref=dst.at[s],
            send_sem=ring_send.at[d, s],
            recv_sem=ring_recv.at[d, s],
            device_id=(ab, right if d == 0 else left),
            device_id_type=MESH,
        )

    waited = set()

    def need(k):
        k = k % n_y
        if k not in waited:
            waited.add(k)
            pair_copy(k if k <= n_y // 2 else k - n_y).wait_recv()

    for s in range(n_y - 1):
        need(-(s + 1))
        need(s + 1)
        if s == 0:
            send_r[s] = own(-1, lo)
            send_l[s] = own(1, hi)
        else:
            ring_copy(0, s - 1).wait_recv()
            send_r[s] = recv_r[s - 1] + own(-(s + 1), lo)
            ring_copy(1, s - 1).wait_recv()
            send_l[s] = recv_l[s - 1] + own(s + 1, hi)
        ring_copy(0, s).start()
        ring_copy(1, s).start()
    need(0)
    ring_copy(0, n_y - 2).wait_recv()
    out_ref[:, lo] = recv_r[n_y - 2] + own(0, lo)
    ring_copy(1, n_y - 2).wait_recv()
    out_ref[:, hi] = recv_l[n_y - 2] + own(0, hi)
    for k in order:
        pair_copy(k).wait_send()
    for s in range(n_y - 1):
        ring_copy(0, s).wait_send()
        ring_copy(1, s).wait_send()


def scatter_rows(partial_value, n_cd):
    n_y = n_cd // 2
    total_rows, cols = partial_value.shape
    rows = total_rows // n_cd
    blocks = partial_value.reshape(n_y, 2, rows, cols)
    half = cols // 2
    return pl.pallas_call(
        functools.partial(scatter_kernel, n_y),
        out_shape=jax.ShapeDtypeStruct((rows, cols), partial_value.dtype),
        in_specs=[pl.BlockSpec(memory_space=pltpu.VMEM)],
        out_specs=pl.BlockSpec(memory_space=pltpu.VMEM),
        scratch_shapes=[
            pltpu.VMEM((n_y, rows, cols), jnp.float32),
            pltpu.VMEM((n_y - 1, rows, half), jnp.float32),
            pltpu.VMEM((n_y - 1, rows, half), jnp.float32),
            pltpu.VMEM((n_y - 1, rows, half), jnp.float32),
            pltpu.VMEM((n_y - 1, rows, half), jnp.float32),
            pltpu.SemaphoreType.DMA((n_y,)),
            pltpu.SemaphoreType.DMA((n_y,)),
            pltpu.SemaphoreType.DMA((2, n_y - 1)),
            pltpu.SemaphoreType.DMA((2, n_y - 1)),
        ],
        compiler_params=pltpu.CompilerParams(collective_id=1, has_side_effects=True),
    )(blocks)


def on_device(n_ab, n_cd, amplitudes, integrals, ij_pairs, ab_pairs, eps_occ, eps_vir):
    partial_value = contract_rows(gather_rows(amplitudes, n_ab), integrals)
    ladder = scatter_rows(partial_value, n_cd)
    first_occ = lookup_energy(ij_pairs[:, 0], eps_occ)[:, None]
    second_occ = lookup_energy(ij_pairs[:, 1], eps_occ)[:, None]
    first_vir = lookup_energy(ab_pairs[:, 0], eps_vir)[None, :]
    second_vir = lookup_energy(ab_pairs[:, 1], eps_vir)[None, :]
    denominator = first_occ + second_occ - first_vir - second_vir
    update = ladder / denominator
    return (ladder, update)


def solution(mesh):
    in_specs = (P("ab", "cd"), P("ab", "cd"), P("cd", None), P("ab", None), P(), P())
    out_specs = (P("cd", "ab"), P("cd", "ab"))
    return jax.shard_map(
        functools.partial(on_device, mesh.shape["ab"], mesh.shape["cd"]),
        mesh=mesh,
        in_specs=in_specs,
        out_specs=out_specs,
        check_vma=False,
    )
```

```python
import functools

import jax
import jax.numpy as jnp
from jax import lax
from jax.experimental import pallas as pl
from jax.experimental.pallas import tpu as pltpu
from jax.sharding import PartitionSpec as P

MESH = pl.DeviceIdType.MESH


def lookup_energy(indices, energies):
    positions = lax.broadcasted_iota(jnp.int32, (indices.shape[0], energies.shape[0]), 1)
    picked = jnp.where(indices[:, None] == positions, energies[None, :], jnp.float32(0.0))
    return jnp.sum(picked, axis=1)


def contract_rows(row_block, col_block):
    return lax.dot_general(
        row_block,
        col_block,
        (((1,), (1,)), ((), ())),
        precision=lax.Precision.HIGH,
        preferred_element_type=jnp.float32,
    )


def gather_kernel(n, amp_ref, out_ref, held, send_sems, recv_sems):
    me = lax.axis_index("ab")
    cd = lax.axis_index("cd")
    rows = amp_ref.shape[0]

    barrier = pltpu.get_barrier_semaphore()

    def greet(i, carry):
        peer = lax.rem(me + i, n)
        pl.semaphore_signal(barrier, inc=1, device_id=(peer, cd), device_id_type=MESH)
        return carry

    lax.fori_loop(1, n, greet, 0)
    pl.semaphore_wait(barrier, n - 1)

    mine = pl.ds(pl.multiple_of(me * rows, rows), rows)

    def copy_to(peer):
        return pltpu.make_async_remote_copy(
            src_ref=amp_ref,
            dst_ref=held.at[mine],
            send_sem=send_sems.at[peer],
            recv_sem=recv_sems.at[me],
            device_id=(peer, cd),
            device_id_type=MESH,
        )

    def copy_from(peer):
        theirs = pl.ds(pl.multiple_of(peer * rows, rows), rows)
        return pltpu.make_async_remote_copy(
            src_ref=amp_ref,
            dst_ref=held.at[theirs],
            send_sem=send_sems.at[peer],
            recv_sem=recv_sems.at[peer],
            device_id=(peer, cd),
            device_id_type=MESH,
        )

    def send(i, carry):
        copy_to(lax.rem(me + i, n)).start()
        return carry

    lax.fori_loop(1, n, send, 0)
    held[mine, :] = amp_ref[...]

    def finish(i, carry):
        copy_to(lax.rem(me + i, n)).wait_send()
        copy_from(lax.rem(me + n - i, n)).wait_recv()
        return carry

    lax.fori_loop(1, n, finish, 0)
    out_ref[...] = held[...]


def gather_rows(amplitudes, n):
    rows, cols = amplitudes.shape
    return pl.pallas_call(
        functools.partial(gather_kernel, n),
        out_shape=jax.ShapeDtypeStruct((rows * n, cols), amplitudes.dtype),
        in_specs=[pl.BlockSpec(memory_space=pltpu.VMEM)],
        out_specs=pl.BlockSpec(memory_space=pltpu.VMEM),
        scratch_shapes=[
            pltpu.VMEM((rows * n, cols), amplitudes.dtype),
            pltpu.SemaphoreType.DMA((n,)),
            pltpu.SemaphoreType.DMA((n,)),
        ],
        compiler_params=pltpu.CompilerParams(collective_id=0, has_side_effects=True),
    )(amplitudes)


def scatter_kernel(n_y, part_ref, out_ref, pair, send_r, recv_r, send_l, recv_l,
                   pair_send, pair_recv, ring_send, ring_recv):
    ab = lax.axis_index("ab")
    cd = lax.axis_index("cd")
    y, core = cd // 2, lax.rem(cd, 2)
    other = 1 - core
    right = lax.rem(y + 1, n_y) * 2 + core
    left = lax.rem(y + n_y - 1, n_y) * 2 + core
    partner = y * 2 + other
    half = out_ref.shape[1] // 2

    barrier = pltpu.get_barrier_semaphore()
    for peer in (partner, right, left):
        pl.semaphore_signal(barrier, inc=1, device_id=(ab, peer), device_id_type=MESH)
    pl.semaphore_wait(barrier, 3)

    order = []
    for k in list(range(1, n_y // 2 + 1)) + [0]:
        for sign in (1, -1):
            if (sign * k) % n_y not in [j % n_y for j in order]:
                order.append(sign * k)

    def pair_copy(k):
        b = lax.rem(y + k + n_y, n_y)
        return pltpu.make_async_remote_copy(
            src_ref=part_ref.at[b, other],
            dst_ref=pair.at[b],
            send_sem=pair_send.at[b],
            recv_sem=pair_recv.at[b],
            device_id=(ab, partner),
            device_id_type=MESH,
        )

    for k in order:
        pair_copy(k).start()

    def own(k, cols):
        b = lax.rem(y + k + n_y, n_y)
        return part_ref[b, core, :, cols] + pair[b, :, cols]

    lo, hi = slice(0, half), slice(half, 2 * half)

    def ring_copy(d, s):
        src, dst = (send_r, recv_r) if d == 0 else (send_l, recv_l)
        return pltpu.make_async_remote_copy(
            src_ref=src.at[s],
            dst_ref=dst.at[s],
            send_sem=ring_send.at[d, s],
            recv_sem=ring_recv.at[d, s],
            device_id=(ab, right if d == 0 else left),
            device_id_type=MESH,
        )

    waited = set()

    def need(k):
        k = k % n_y
        if k not in waited:
            waited.add(k)
            pair_copy(k if k <= n_y // 2 else k - n_y).wait_recv()

    for s in range(n_y - 1):
        need(-(s + 1))
        need(s + 1)
        if s == 0:
            send_r[s] = own(-1, lo)
            send_l[s] = own(1, hi)
        else:
            ring_copy(0, s - 1).wait_recv()
            send_r[s] = recv_r[s - 1] + own(-(s + 1), lo)
            ring_copy(1, s - 1).wait_recv()
            send_l[s] = recv_l[s - 1] + own(s + 1, hi)
        ring_copy(0, s).start()
        ring_copy(1, s).start()
    need(0)
    ring_copy(0, n_y - 2).wait_recv()
    out_ref[:, lo] = recv_r[n_y - 2] + own(0, lo)
    ring_copy(1, n_y - 2).wait_recv()
    out_ref[:, hi] = recv_l[n_y - 2] + own(0, hi)
    for k in order:
        pair_copy(k).wait_send()
    for s in range(n_y - 1):
        ring_copy(0, s).wait_send()
        ring_copy(1, s).wait_send()


def scatter_rows(partial_value, n_cd):
    n_y = n_cd // 2
    total_rows, cols = partial_value.shape
    rows = total_rows // n_cd
    blocks = partial_value.reshape(n_y, 2, rows, cols)
    half = cols // 2
    return pl.pallas_call(
        functools.partial(scatter_kernel, n_y),
        out_shape=jax.ShapeDtypeStruct((rows, cols), partial_value.dtype),
        in_specs=[pl.BlockSpec(memory_space=pltpu.VMEM)],
        out_specs=pl.BlockSpec(memory_space=pltpu.VMEM),
        scratch_shapes=[
            pltpu.VMEM((n_y, rows, cols), jnp.float32),
            pltpu.VMEM((n_y - 1, rows, half), jnp.float32),
            pltpu.VMEM((n_y - 1, rows, half), jnp.float32),
            pltpu.VMEM((n_y - 1, rows, half), jnp.float32),
            pltpu.VMEM((n_y - 1, rows, half), jnp.float32),
            pltpu.SemaphoreType.DMA((n_y,)),
            pltpu.SemaphoreType.DMA((n_y,)),
            pltpu.SemaphoreType.DMA((2, n_y - 1)),
            pltpu.SemaphoreType.DMA((2, n_y - 1)),
        ],
        compiler_params=pltpu.CompilerParams(collective_id=1, has_side_effects=True),
    )(blocks)


def on_device(n_ab, n_cd, amplitudes, integrals, ij_pairs, ab_pairs, eps_occ, eps_vir):
    partial_value = contract_rows(gather_rows(amplitudes, n_ab), integrals)
    ladder = scatter_rows(partial_value, n_cd)
    first_occ = eps_occ[ij_pairs[:, 0]][:, None]
    second_occ = eps_occ[ij_pairs[:, 1]][:, None]
    first_vir = eps_vir[ab_pairs[:, 0]][None, :]
    second_vir = eps_vir[ab_pairs[:, 1]][None, :]
    denominator = first_occ + second_occ - first_vir - second_vir
    update = ladder / denominator
    return (ladder, update)


def solution(mesh):
    in_specs = (P("ab", "cd"), P("ab", "cd"), P("cd", None), P("ab", None), P(), P())
    out_specs = (P("cd", "ab"), P("cd", "ab"))
    return jax.shard_map(
        functools.partial(on_device, mesh.shape["ab"], mesh.shape["cd"]),
        mesh=mesh,
        in_specs=in_specs,
        out_specs=out_specs,
        check_vma=False,
    )
```

```python
import functools

import jax
import jax.numpy as jnp
from jax import lax
from jax.experimental import pallas as pl
from jax.experimental.pallas import tpu as pltpu
from jax.sharding import PartitionSpec as P

MESH = pl.DeviceIdType.MESH


def lookup_energy(indices, energies):
    lanes = 128
    groups = -(-energies.shape[0] // lanes)
    table = jnp.pad(energies, (0, groups * lanes - energies.shape[0])).reshape(groups, lanes)
    low = lax.rem(indices, lanes)
    high = indices // lanes
    one_hot = (low[:, None] == lax.broadcasted_iota(jnp.int32, (indices.shape[0], lanes), 1)).astype(jnp.float32)
    by_group = lax.dot_general(
        one_hot, table, (((1,), (1,)), ((), ())),
        precision=lax.Precision.HIGHEST, preferred_element_type=jnp.float32,
    )
    chosen = high[:, None] == lax.broadcasted_iota(jnp.int32, by_group.shape, 1)
    return jnp.sum(jnp.where(chosen, by_group, jnp.float32(0.0)), axis=1)


def contract_rows(row_block, col_block):
    return lax.dot_general(
        row_block,
        col_block,
        (((1,), (1,)), ((), ())),
        precision=lax.Precision.HIGH,
        preferred_element_type=jnp.float32,
    )


def gather_kernel(n, amp_ref, out_ref, held, send_sems, recv_sems):
    me = lax.axis_index("ab")
    cd = lax.axis_index("cd")
    rows = amp_ref.shape[0]

    barrier = pltpu.get_barrier_semaphore()

    def greet(i, carry):
        peer = lax.rem(me + i, n)
        pl.semaphore_signal(barrier, inc=1, device_id=(peer, cd), device_id_type=MESH)
        return carry

    lax.fori_loop(1, n, greet, 0)
    pl.semaphore_wait(barrier, n - 1)

    mine = pl.ds(pl.multiple_of(me * rows, rows), rows)

    def copy_to(peer):
        return pltpu.make_async_remote_copy(
            src_ref=amp_ref,
            dst_ref=held.at[mine],
            send_sem=send_sems.at[peer],
            recv_sem=recv_sems.at[me],
            device_id=(peer, cd),
            device_id_type=MESH,
        )

    def copy_from(peer):
        theirs = pl.ds(pl.multiple_of(peer * rows, rows), rows)
        return pltpu.make_async_remote_copy(
            src_ref=amp_ref,
            dst_ref=held.at[theirs],
            send_sem=send_sems.at[peer],
            recv_sem=recv_sems.at[peer],
            device_id=(peer, cd),
            device_id_type=MESH,
        )

    def send(i, carry):
        copy_to(lax.rem(me + i, n)).start()
        return carry

    lax.fori_loop(1, n, send, 0)
    held[mine, :] = amp_ref[...]

    def finish(i, carry):
        copy_to(lax.rem(me + i, n)).wait_send()
        copy_from(lax.rem(me + n - i, n)).wait_recv()
        return carry

    lax.fori_loop(1, n, finish, 0)
    out_ref[...] = held[...]


def gather_rows(amplitudes, n):
    rows, cols = amplitudes.shape
    return pl.pallas_call(
        functools.partial(gather_kernel, n),
        out_shape=jax.ShapeDtypeStruct((rows * n, cols), amplitudes.dtype),
        in_specs=[pl.BlockSpec(memory_space=pltpu.VMEM)],
        out_specs=pl.BlockSpec(memory_space=pltpu.VMEM),
        scratch_shapes=[
            pltpu.VMEM((rows * n, cols), amplitudes.dtype),
            pltpu.SemaphoreType.DMA((n,)),
            pltpu.SemaphoreType.DMA((n,)),
        ],
        compiler_params=pltpu.CompilerParams(collective_id=0, has_side_effects=True),
    )(amplitudes)


def scatter_kernel(n_y, part_ref, out_ref, pair, send_r, recv_r, send_l, recv_l,
                   pair_send, pair_recv, ring_send, ring_recv):
    ab = lax.axis_index("ab")
    cd = lax.axis_index("cd")
    y, core = cd // 2, lax.rem(cd, 2)
    other = 1 - core
    right = lax.rem(y + 1, n_y) * 2 + core
    left = lax.rem(y + n_y - 1, n_y) * 2 + core
    partner = y * 2 + other
    half = out_ref.shape[1] // 2

    barrier = pltpu.get_barrier_semaphore()
    for peer in (partner, right, left):
        pl.semaphore_signal(barrier, inc=1, device_id=(ab, peer), device_id_type=MESH)
    pl.semaphore_wait(barrier, 3)

    order = []
    for k in list(range(1, n_y // 2 + 1)) + [0]:
        for sign in (1, -1):
            if (sign * k) % n_y not in [j % n_y for j in order]:
                order.append(sign * k)

    def pair_copy(k):
        b = lax.rem(y + k + n_y, n_y)
        return pltpu.make_async_remote_copy(
            src_ref=part_ref.at[b, other],
            dst_ref=pair.at[b],
            send_sem=pair_send.at[b],
            recv_sem=pair_recv.at[b],
            device_id=(ab, partner),
            device_id_type=MESH,
        )

    for k in order:
        pair_copy(k).start()

    def own(k, cols):
        b = lax.rem(y + k + n_y, n_y)
        return part_ref[b, core, :, cols] + pair[b, :, cols]

    lo, hi = slice(0, half), slice(half, 2 * half)

    def ring_copy(d, s):
        src, dst = (send_r, recv_r) if d == 0 else (send_l, recv_l)
        return pltpu.make_async_remote_copy(
            src_ref=src.at[s],
            dst_ref=dst.at[s],
            send_sem=ring_send.at[d, s],
            recv_sem=ring_recv.at[d, s],
            device_id=(ab, right if d == 0 else left),
            device_id_type=MESH,
        )

    waited = set()

    def need(k):
        k = k % n_y
        if k not in waited:
            waited.add(k)
            pair_copy(k if k <= n_y // 2 else k - n_y).wait_recv()

    for s in range(n_y - 1):
        need(-(s + 1))
        need(s + 1)
        if s == 0:
            send_r[s] = own(-1, lo)
            send_l[s] = own(1, hi)
        else:
            ring_copy(0, s - 1).wait_recv()
            send_r[s] = recv_r[s - 1] + own(-(s + 1), lo)
            ring_copy(1, s - 1).wait_recv()
            send_l[s] = recv_l[s - 1] + own(s + 1, hi)
        ring_copy(0, s).start()
        ring_copy(1, s).start()
    need(0)
    ring_copy(0, n_y - 2).wait_recv()
    out_ref[:, lo] = recv_r[n_y - 2] + own(0, lo)
    ring_copy(1, n_y - 2).wait_recv()
    out_ref[:, hi] = recv_l[n_y - 2] + own(0, hi)
    for k in order:
        pair_copy(k).wait_send()
    for s in range(n_y - 1):
        ring_copy(0, s).wait_send()
        ring_copy(1, s).wait_send()


def scatter_rows(partial_value, n_cd):
    n_y = n_cd // 2
    total_rows, cols = partial_value.shape
    rows = total_rows // n_cd
    blocks = partial_value.reshape(n_y, 2, rows, cols)
    half = cols // 2
    return pl.pallas_call(
        functools.partial(scatter_kernel, n_y),
        out_shape=jax.ShapeDtypeStruct((rows, cols), partial_value.dtype),
        in_specs=[pl.BlockSpec(memory_space=pltpu.VMEM)],
        out_specs=pl.BlockSpec(memory_space=pltpu.VMEM),
        scratch_shapes=[
            pltpu.VMEM((n_y, rows, cols), jnp.float32),
            pltpu.VMEM((n_y - 1, rows, half), jnp.float32),
            pltpu.VMEM((n_y - 1, rows, half), jnp.float32),
            pltpu.VMEM((n_y - 1, rows, half), jnp.float32),
            pltpu.VMEM((n_y - 1, rows, half), jnp.float32),
            pltpu.SemaphoreType.DMA((n_y,)),
            pltpu.SemaphoreType.DMA((n_y,)),
            pltpu.SemaphoreType.DMA((2, n_y - 1)),
            pltpu.SemaphoreType.DMA((2, n_y - 1)),
        ],
        compiler_params=pltpu.CompilerParams(collective_id=1, has_side_effects=True),
    )(blocks)


def on_device(n_ab, n_cd, amplitudes, integrals, ij_pairs, ab_pairs, eps_occ, eps_vir):
    partial_value = contract_rows(gather_rows(amplitudes, n_ab), integrals)
    ladder = scatter_rows(partial_value, n_cd)
    first_occ = lookup_energy(ij_pairs[:, 0], eps_occ)[:, None]
    second_occ = lookup_energy(ij_pairs[:, 1], eps_occ)[:, None]
    first_vir = lookup_energy(ab_pairs[:, 0], eps_vir)[None, :]
    second_vir = lookup_energy(ab_pairs[:, 1], eps_vir)[None, :]
    denominator = first_occ + second_occ - first_vir - second_vir
    update = ladder / denominator
    return (ladder, update)


def solution(mesh):
    in_specs = (P("ab", "cd"), P("ab", "cd"), P("cd", None), P("ab", None), P(), P())
    out_specs = (P("cd", "ab"), P("cd", "ab"))
    return jax.shard_map(
        functools.partial(on_device, mesh.shape["ab"], mesh.shape["cd"]),
        mesh=mesh,
        in_specs=in_specs,
        out_specs=out_specs,
        check_vma=False,
    )
```

```python
import functools

import jax
import jax.numpy as jnp
from jax import lax
from jax.experimental import pallas as pl
from jax.experimental.pallas import tpu as pltpu
from jax.sharding import PartitionSpec as P

MESH = pl.DeviceIdType.MESH


def lookup_energy(indices, energies):
    lanes = 128
    groups = -(-energies.shape[0] // lanes)
    table = jnp.pad(energies, (0, groups * lanes - energies.shape[0])).reshape(groups, lanes)
    low = lax.rem(indices, lanes)
    high = indices // lanes
    one_hot = (low[:, None] == lax.broadcasted_iota(jnp.int32, (indices.shape[0], lanes), 1)).astype(jnp.float32)
    by_group = lax.dot_general(
        one_hot, table, (((1,), (1,)), ((), ())),
        precision=lax.Precision.HIGHEST, preferred_element_type=jnp.float32,
    )
    chosen = high[:, None] == lax.broadcasted_iota(jnp.int32, by_group.shape, 1)
    return jnp.sum(jnp.where(chosen, by_group, jnp.float32(0.0)), axis=1)


def contract_rows(row_block, col_block):
    return lax.dot_general(
        row_block,
        col_block,
        (((1,), (1,)), ((), ())),
        precision=lax.Precision.HIGH,
        preferred_element_type=jnp.float32,
    )


def gather_kernel(n, amp_ref, out_ref, held, send_sems, recv_sems):
    me = lax.axis_index("ab")
    cd = lax.axis_index("cd")
    rows = amp_ref.shape[0]

    barrier = pltpu.get_barrier_semaphore()

    def greet(i, carry):
        peer = lax.rem(me + i, n)
        pl.semaphore_signal(barrier, inc=1, device_id=(peer, cd), device_id_type=MESH)
        return carry

    lax.fori_loop(1, n, greet, 0)
    pl.semaphore_wait(barrier, n - 1)

    mine = pl.ds(pl.multiple_of(me * rows, rows), rows)

    def copy_to(peer):
        return pltpu.make_async_remote_copy(
            src_ref=amp_ref,
            dst_ref=held.at[mine],
            send_sem=send_sems.at[peer],
            recv_sem=recv_sems.at[me],
            device_id=(peer, cd),
            device_id_type=MESH,
        )

    def copy_from(peer):
        theirs = pl.ds(pl.multiple_of(peer * rows, rows), rows)
        return pltpu.make_async_remote_copy(
            src_ref=amp_ref,
            dst_ref=held.at[theirs],
            send_sem=send_sems.at[peer],
            recv_sem=recv_sems.at[peer],
            device_id=(peer, cd),
            device_id_type=MESH,
        )

    def send(i, carry):
        copy_to(lax.rem(me + i, n)).start()
        return carry

    lax.fori_loop(1, n, send, 0)
    held[mine, :] = amp_ref[...]

    def finish(i, carry):
        copy_to(lax.rem(me + i, n)).wait_send()
        copy_from(lax.rem(me + n - i, n)).wait_recv()
        return carry

    lax.fori_loop(1, n, finish, 0)
    out_ref[...] = held[...]


def gather_rows(amplitudes, n):
    rows, cols = amplitudes.shape
    return pl.pallas_call(
        functools.partial(gather_kernel, n),
        out_shape=jax.ShapeDtypeStruct((rows * n, cols), amplitudes.dtype),
        in_specs=[pl.BlockSpec(memory_space=pltpu.VMEM)],
        out_specs=pl.BlockSpec(memory_space=pltpu.VMEM),
        scratch_shapes=[
            pltpu.VMEM((rows * n, cols), amplitudes.dtype),
            pltpu.SemaphoreType.DMA((n,)),
            pltpu.SemaphoreType.DMA((n,)),
        ],
        compiler_params=pltpu.CompilerParams(collective_id=0, has_side_effects=True),
    )(amplitudes)


def scatter_kernel(n_y, n_chunks, part_ref, out_ref, pair, send_r, recv_r, send_l, recv_l,
                   pair_send, pair_recv, ring_send, ring_recv):
    ab = lax.axis_index("ab")
    cd = lax.axis_index("cd")
    y, core = cd // 2, lax.rem(cd, 2)
    other = 1 - core
    right = lax.rem(y + 1, n_y) * 2 + core
    left = lax.rem(y + n_y - 1, n_y) * 2 + core
    partner = y * 2 + other
    half = out_ref.shape[1] // 2
    width = half // n_chunks

    barrier = pltpu.get_barrier_semaphore()
    for peer in (partner, right, left):
        pl.semaphore_signal(barrier, inc=1, device_id=(ab, peer), device_id_type=MESH)
    pl.semaphore_wait(barrier, 3)

    order = []
    for k in list(range(1, n_y // 2 + 1)) + [0]:
        for sign in (1, -1):
            if (sign * k) % n_y not in [j % n_y for j in order]:
                order.append(sign * k)

    def pair_copy(k):
        b = lax.rem(y + k + n_y, n_y)
        return pltpu.make_async_remote_copy(
            src_ref=part_ref.at[b, other],
            dst_ref=pair.at[b],
            send_sem=pair_send.at[b],
            recv_sem=pair_recv.at[b],
            device_id=(ab, partner),
            device_id_type=MESH,
        )

    for k in order:
        pair_copy(k).start()

    def own(k, cols):
        b = lax.rem(y + k + n_y, n_y)
        return part_ref[b, core, :, cols] + pair[b, :, cols]

    def columns(d, q):
        start = d * half + q * width
        return slice(start, start + width)

    sends = (send_r, send_l)
    recvs = (recv_r, recv_l)

    def ring_copy(d, s, q):
        return pltpu.make_async_remote_copy(
            src_ref=sends[d].at[s, q],
            dst_ref=recvs[d].at[s, q],
            send_sem=ring_send.at[d, s, q],
            recv_sem=ring_recv.at[d, s, q],
            device_id=(ab, right if d == 0 else left),
            device_id_type=MESH,
        )

    waited = set()

    def need(k):
        k = k % n_y
        if k not in waited:
            waited.add(k)
            pair_copy(k if k <= n_y // 2 else k - n_y).wait_recv()

    for s in range(n_y - 1):
        need(-(s + 1))
        need(s + 1)
        for q in range(n_chunks):
            for d in (0, 1):
                k = -(s + 1) if d == 0 else s + 1
                if s == 0:
                    sends[d][s, q] = own(k, columns(d, q))
                else:
                    ring_copy(d, s - 1, q).wait_recv()
                    sends[d][s, q] = recvs[d][s - 1, q] + own(k, columns(d, q))
                ring_copy(d, s, q).start()
    need(0)
    for q in range(n_chunks):
        for d in (0, 1):
            ring_copy(d, n_y - 2, q).wait_recv()
            out_ref[:, columns(d, q)] = recvs[d][n_y - 2, q] + own(0, columns(d, q))
    for k in order:
        pair_copy(k).wait_send()
    for s in range(n_y - 1):
        for q in range(n_chunks):
            ring_copy(0, s, q).wait_send()
            ring_copy(1, s, q).wait_send()


def scatter_rows(partial_value, n_cd, n_chunks=4):
    n_y = n_cd // 2
    total_rows, cols = partial_value.shape
    rows = total_rows // n_cd
    blocks = partial_value.reshape(n_y, 2, rows, cols)
    width = cols // 2 // n_chunks
    slots = pltpu.VMEM((n_y - 1, n_chunks, rows, width), jnp.float32)
    return pl.pallas_call(
        functools.partial(scatter_kernel, n_y, n_chunks),
        out_shape=jax.ShapeDtypeStruct((rows, cols), partial_value.dtype),
        in_specs=[pl.BlockSpec(memory_space=pltpu.VMEM)],
        out_specs=pl.BlockSpec(memory_space=pltpu.VMEM),
        scratch_shapes=[
            pltpu.VMEM((n_y, rows, cols), jnp.float32),
            slots,
            slots,
            slots,
            slots,
            pltpu.SemaphoreType.DMA((n_y,)),
            pltpu.SemaphoreType.DMA((n_y,)),
            pltpu.SemaphoreType.DMA((2, n_y - 1, n_chunks)),
            pltpu.SemaphoreType.DMA((2, n_y - 1, n_chunks)),
        ],
        compiler_params=pltpu.CompilerParams(collective_id=1, has_side_effects=True),
    )(blocks)


def on_device(n_ab, n_cd, amplitudes, integrals, ij_pairs, ab_pairs, eps_occ, eps_vir):
    partial_value = contract_rows(gather_rows(amplitudes, n_ab), integrals)
    ladder = scatter_rows(partial_value, n_cd)
    first_occ = lookup_energy(ij_pairs[:, 0], eps_occ)[:, None]
    second_occ = lookup_energy(ij_pairs[:, 1], eps_occ)[:, None]
    first_vir = lookup_energy(ab_pairs[:, 0], eps_vir)[None, :]
    second_vir = lookup_energy(ab_pairs[:, 1], eps_vir)[None, :]
    denominator = first_occ + second_occ - first_vir - second_vir
    update = ladder / denominator
    return (ladder, update)


def solution(mesh):
    in_specs = (P("ab", "cd"), P("ab", "cd"), P("cd", None), P("ab", None), P(), P())
    out_specs = (P("cd", "ab"), P("cd", "ab"))
    return jax.shard_map(
        functools.partial(on_device, mesh.shape["ab"], mesh.shape["cd"]),
        mesh=mesh,
        in_specs=in_specs,
        out_specs=out_specs,
        check_vma=False,
    )
```

```python
import functools

import jax
import jax.numpy as jnp
from jax import lax
from jax.experimental import pallas as pl
from jax.experimental.pallas import tpu as pltpu
from jax.sharding import PartitionSpec as P

MESH = pl.DeviceIdType.MESH


def lookup_energy(indices, energies):
    lanes = 128
    groups = -(-energies.shape[0] // lanes)
    table = jnp.pad(energies, (0, groups * lanes - energies.shape[0])).reshape(groups, lanes)
    low = lax.rem(indices, lanes)
    high = indices // lanes
    one_hot = (low[:, None] == lax.broadcasted_iota(jnp.int32, (indices.shape[0], lanes), 1)).astype(jnp.float32)
    by_group = lax.dot_general(
        one_hot, table, (((1,), (1,)), ((), ())),
        precision=lax.Precision.HIGHEST, preferred_element_type=jnp.float32,
    )
    chosen = high[:, None] == lax.broadcasted_iota(jnp.int32, by_group.shape, 1)
    return jnp.sum(jnp.where(chosen, by_group, jnp.float32(0.0)), axis=1)


def contract_rows(row_block, col_block):
    return lax.dot_general(
        row_block,
        col_block,
        (((1,), (1,)), ((), ())),
        precision=lax.Precision.HIGH,
        preferred_element_type=jnp.float32,
    )


def gather_kernel(n_x, n_z, amp_ref, out_ref, held, local_sem, x_send, x_recv, z_send, z_recv):
    ab = lax.axis_index("ab")
    cd = lax.axis_index("cd")
    z, x = ab // n_x, lax.rem(ab, n_x)
    rows = amp_ref.shape[0]
    group = rows * n_x
    cols = amp_ref.shape[1]
    up = lax.rem(z + 1, n_z) * n_x + x
    down = lax.rem(z + n_z - 1, n_z) * n_x + x

    barrier = pltpu.get_barrier_semaphore()
    for i in range(1, n_x):
        pl.semaphore_signal(barrier, inc=1, device_id=(z * n_x + lax.rem(x + i, n_x), cd), device_id_type=MESH)
    pl.semaphore_signal(barrier, inc=1, device_id=(up, cd), device_id_type=MESH)
    pl.semaphore_signal(barrier, inc=1, device_id=(down, cd), device_id_type=MESH)
    pl.semaphore_wait(barrier, n_x + 1)

    def block_rows(a_index):
        return pl.ds(pl.multiple_of(a_index * rows, rows), rows)

    def x_copy(i, receiving):
        sender = lax.rem(x + n_x - i, n_x) if receiving else x
        target = lax.rem(x + i, n_x)
        return pltpu.make_async_remote_copy(
            src_ref=amp_ref,
            dst_ref=held.at[block_rows(z * n_x + sender)],
            send_sem=x_send.at[target],
            recv_sem=x_recv.at[sender],
            device_id=(z * n_x + target, cd),
            device_id_type=MESH,
        )

    for i in range(1, n_x):
        x_copy(i, False).start()
    local = pltpu.make_async_copy(amp_ref, held.at[block_rows(ab)], local_sem)
    local.start()
    local.wait()
    for i in range(1, n_x):
        x_copy(i, True).wait_recv()

    steps = n_z // 2

    def z_copy(d, t, q):
        source_z = lax.rem(z + n_z - t, n_z) if d == 0 else lax.rem(z + t, n_z)
        cols_here = slice(0, cols)
        if t == steps - 1:
            cols_here = slice(0, cols // 2) if d == 0 else slice(cols // 2, cols)
        src = held.at[block_rows(source_z * n_x + q), cols_here]
        return pltpu.make_async_remote_copy(
            src_ref=src,
            dst_ref=src,
            send_sem=z_send.at[d, t, q],
            recv_sem=z_recv.at[d, t, q],
            device_id=(up if d == 0 else down, cd),
            device_id_type=MESH,
        )

    def z_arrival(d, t, q):
        source_z = lax.rem(z + n_z - t - 1, n_z) if d == 0 else lax.rem(z + t + 1, n_z)
        cols_here = slice(0, cols)
        if t == steps - 1:
            cols_here = slice(0, cols // 2) if d == 0 else slice(cols // 2, cols)
        dst = held.at[block_rows(source_z * n_x + q), cols_here]
        return pltpu.make_async_remote_copy(
            src_ref=dst,
            dst_ref=dst,
            send_sem=z_send.at[d, t, q],
            recv_sem=z_recv.at[d, t, q],
            device_id=(up if d == 0 else down, cd),
            device_id_type=MESH,
        )

    for t in range(steps):
        for q in range(n_x):
            for d in (0, 1):
                if t > 0:
                    z_arrival(d, t - 1, q).wait_recv()
                z_copy(d, t, q).start()
    for q in range(n_x):
        for d in (0, 1):
            z_arrival(d, steps - 1, q).wait_recv()
    for i in range(1, n_x):
        x_copy(i, False).wait_send()
    for t in range(steps):
        for q in range(n_x):
            for d in (0, 1):
                z_copy(d, t, q).wait_send()
    out_ref[...] = held[...]


def gather_rows(amplitudes, n_x, n_z):
    rows, cols = amplitudes.shape
    steps = n_z // 2
    return pl.pallas_call(
        functools.partial(gather_kernel, n_x, n_z),
        out_shape=jax.ShapeDtypeStruct((rows * n_x * n_z, cols), amplitudes.dtype),
        in_specs=[pl.BlockSpec(memory_space=pltpu.VMEM)],
        out_specs=pl.BlockSpec(memory_space=pltpu.VMEM),
        scratch_shapes=[
            pltpu.VMEM((rows * n_x * n_z, cols), amplitudes.dtype),
            pltpu.SemaphoreType.DMA(()),
            pltpu.SemaphoreType.DMA((n_x,)),
            pltpu.SemaphoreType.DMA((n_x,)),
            pltpu.SemaphoreType.DMA((2, steps, n_x)),
            pltpu.SemaphoreType.DMA((2, steps, n_x)),
        ],
        compiler_params=pltpu.CompilerParams(collective_id=0, has_side_effects=True),
    )(amplitudes)


def x_extent(mesh):
    first = mesh.devices.reshape(mesh.shape["ab"], -1)[:, 0]
    try:
        return len({d.coords[0] for d in first})
    except AttributeError:
        return 2


def scatter_kernel(n_y, n_chunks, part_ref, out_ref, pair, send_r, recv_r, send_l, recv_l,
                   pair_send, pair_recv, ring_send, ring_recv):
    ab = lax.axis_index("ab")
    cd = lax.axis_index("cd")
    y, core = cd // 2, lax.rem(cd, 2)
    other = 1 - core
    right = lax.rem(y + 1, n_y) * 2 + core
    left = lax.rem(y + n_y - 1, n_y) * 2 + core
    partner = y * 2 + other
    half = out_ref.shape[1] // 2
    width = half // n_chunks

    barrier = pltpu.get_barrier_semaphore()
    for peer in (partner, right, left):
        pl.semaphore_signal(barrier, inc=1, device_id=(ab, peer), device_id_type=MESH)
    pl.semaphore_wait(barrier, 3)

    order = []
    for k in list(range(1, n_y // 2 + 1)) + [0]:
        for sign in (1, -1):
            if (sign * k) % n_y not in [j % n_y for j in order]:
                order.append(sign * k)

    def pair_copy(k):
        b = lax.rem(y + k + n_y, n_y)
        return pltpu.make_async_remote_copy(
            src_ref=part_ref.at[b, other],
            dst_ref=pair.at[b],
            send_sem=pair_send.at[b],
            recv_sem=pair_recv.at[b],
            device_id=(ab, partner),
            device_id_type=MESH,
        )

    for k in order:
        pair_copy(k).start()

    def own(k, cols):
        b = lax.rem(y + k + n_y, n_y)
        return part_ref[b, core, :, cols] + pair[b, :, cols]

    def columns(d, q):
        start = d * half + q * width
        return slice(start, start + width)

    sends = (send_r, send_l)
    recvs = (recv_r, recv_l)

    def ring_copy(d, s, q):
        return pltpu.make_async_remote_copy(
            src_ref=sends[d].at[s, q],
            dst_ref=recvs[d].at[s, q],
            send_sem=ring_send.at[d, s, q],
            recv_sem=ring_recv.at[d, s, q],
            device_id=(ab, right if d == 0 else left),
            device_id_type=MESH,
        )

    waited = set()

    def need(k):
        k = k % n_y
        if k not in waited:
            waited.add(k)
            pair_copy(k if k <= n_y // 2 else k - n_y).wait_recv()

    for s in range(n_y - 1):
        need(-(s + 1))
        need(s + 1)
        for q in range(n_chunks):
            for d in (0, 1):
                k = -(s + 1) if d == 0 else s + 1
                if s == 0:
                    sends[d][s, q] = own(k, columns(d, q))
                else:
                    ring_copy(d, s - 1, q).wait_recv()
                    sends[d][s, q] = recvs[d][s - 1, q] + own(k, columns(d, q))
                ring_copy(d, s, q).start()
    need(0)
    for q in range(n_chunks):
        for d in (0, 1):
            ring_copy(d, n_y - 2, q).wait_recv()
            out_ref[:, columns(d, q)] = recvs[d][n_y - 2, q] + own(0, columns(d, q))
    for k in order:
        pair_copy(k).wait_send()
    for s in range(n_y - 1):
        for q in range(n_chunks):
            ring_copy(0, s, q).wait_send()
            ring_copy(1, s, q).wait_send()


def scatter_rows(partial_value, n_cd, n_chunks=4):
    n_y = n_cd // 2
    total_rows, cols = partial_value.shape
    rows = total_rows // n_cd
    blocks = partial_value.reshape(n_y, 2, rows, cols)
    width = cols // 2 // n_chunks
    slots = pltpu.VMEM((n_y - 1, n_chunks, rows, width), jnp.float32)
    return pl.pallas_call(
        functools.partial(scatter_kernel, n_y, n_chunks),
        out_shape=jax.ShapeDtypeStruct((rows, cols), partial_value.dtype),
        in_specs=[pl.BlockSpec(memory_space=pltpu.VMEM)],
        out_specs=pl.BlockSpec(memory_space=pltpu.VMEM),
        scratch_shapes=[
            pltpu.VMEM((n_y, rows, cols), jnp.float32),
            slots,
            slots,
            slots,
            slots,
            pltpu.SemaphoreType.DMA((n_y,)),
            pltpu.SemaphoreType.DMA((n_y,)),
            pltpu.SemaphoreType.DMA((2, n_y - 1, n_chunks)),
            pltpu.SemaphoreType.DMA((2, n_y - 1, n_chunks)),
        ],
        compiler_params=pltpu.CompilerParams(collective_id=1, has_side_effects=True),
    )(blocks)


def on_device(n_x, n_z, n_cd, amplitudes, integrals, ij_pairs, ab_pairs, eps_occ, eps_vir):
    partial_value = contract_rows(gather_rows(amplitudes, n_x, n_z), integrals)
    ladder = scatter_rows(partial_value, n_cd)
    first_occ = lookup_energy(ij_pairs[:, 0], eps_occ)[:, None]
    second_occ = lookup_energy(ij_pairs[:, 1], eps_occ)[:, None]
    first_vir = lookup_energy(ab_pairs[:, 0], eps_vir)[None, :]
    second_vir = lookup_energy(ab_pairs[:, 1], eps_vir)[None, :]
    denominator = first_occ + second_occ - first_vir - second_vir
    update = ladder / denominator
    return (ladder, update)


def solution(mesh):
    in_specs = (P("ab", "cd"), P("ab", "cd"), P("cd", None), P("ab", None), P(), P())
    out_specs = (P("cd", "ab"), P("cd", "ab"))
    return jax.shard_map(
        functools.partial(on_device, x_extent(mesh), mesh.shape["ab"] // x_extent(mesh), mesh.shape["cd"]),
        mesh=mesh,
        in_specs=in_specs,
        out_specs=out_specs,
        check_vma=False,
    )
```

```python
import functools

import jax
import jax.numpy as jnp
from jax import lax
from jax.experimental import pallas as pl
from jax.experimental.pallas import tpu as pltpu
from jax.sharding import PartitionSpec as P

MESH = pl.DeviceIdType.MESH


def lookup_energy(indices, energies):
    lanes = 128
    groups = -(-energies.shape[0] // lanes)
    table = jnp.pad(energies, (0, groups * lanes - energies.shape[0])).reshape(groups, lanes)
    low = lax.rem(indices, lanes)
    high = indices // lanes
    one_hot = (low[:, None] == lax.broadcasted_iota(jnp.int32, (indices.shape[0], lanes), 1)).astype(jnp.float32)
    by_group = lax.dot_general(
        one_hot, table, (((1,), (1,)), ((), ())),
        precision=lax.Precision.HIGHEST, preferred_element_type=jnp.float32,
    )
    chosen = high[:, None] == lax.broadcasted_iota(jnp.int32, by_group.shape, 1)
    return jnp.sum(jnp.where(chosen, by_group, jnp.float32(0.0)), axis=1)


def contract_rows(row_block, col_block):
    return lax.dot_general(
        row_block,
        col_block,
        (((1,), (1,)), ((), ())),
        precision=lax.Precision.HIGH,
        preferred_element_type=jnp.float32,
    )


def gather_kernel(n_x, n_z, amp_ref, out_ref, held, local_sem, x_send, x_recv, z_send, z_recv):
    ab = lax.axis_index("ab")
    cd = lax.axis_index("cd")
    z, x = ab // n_x, lax.rem(ab, n_x)
    rows = amp_ref.shape[0]
    group = rows * n_x
    cols = amp_ref.shape[1]
    up = lax.rem(z + 1, n_z) * n_x + x
    down = lax.rem(z + n_z - 1, n_z) * n_x + x

    barrier = pltpu.get_barrier_semaphore()
    for i in range(1, n_x):
        pl.semaphore_signal(barrier, inc=1, device_id=(z * n_x + lax.rem(x + i, n_x), cd), device_id_type=MESH)
    pl.semaphore_signal(barrier, inc=1, device_id=(up, cd), device_id_type=MESH)
    pl.semaphore_signal(barrier, inc=1, device_id=(down, cd), device_id_type=MESH)
    pl.semaphore_wait(barrier, n_x + 1)

    def block_rows(a_index):
        return pl.ds(pl.multiple_of(a_index * rows, rows), rows)

    def x_copy(i, receiving):
        sender = lax.rem(x + n_x - i, n_x) if receiving else x
        target = lax.rem(x + i, n_x)
        return pltpu.make_async_remote_copy(
            src_ref=amp_ref,
            dst_ref=held.at[block_rows(z * n_x + sender)],
            send_sem=x_send.at[target],
            recv_sem=x_recv.at[sender],
            device_id=(z * n_x + target, cd),
            device_id_type=MESH,
        )

    for i in range(1, n_x):
        x_copy(i, False).start()
    local = pltpu.make_async_copy(amp_ref, held.at[block_rows(ab)], local_sem)
    local.start()
    local.wait()
    for i in range(1, n_x):
        x_copy(i, True).wait_recv()

    steps = n_z // 2

    def z_copy(d, t, q):
        source_z = lax.rem(z + n_z - t, n_z) if d == 0 else lax.rem(z + t, n_z)
        cols_here = slice(0, cols)
        if t == steps - 1:
            cols_here = slice(0, cols // 2) if d == 0 else slice(cols // 2, cols)
        src = held.at[block_rows(source_z * n_x + q), cols_here]
        return pltpu.make_async_remote_copy(
            src_ref=src,
            dst_ref=src,
            send_sem=z_send.at[d, t, q],
            recv_sem=z_recv.at[d, t, q],
            device_id=(up if d == 0 else down, cd),
            device_id_type=MESH,
        )

    def z_arrival(d, t, q):
        source_z = lax.rem(z + n_z - t - 1, n_z) if d == 0 else lax.rem(z + t + 1, n_z)
        cols_here = slice(0, cols)
        if t == steps - 1:
            cols_here = slice(0, cols // 2) if d == 0 else slice(cols // 2, cols)
        dst = held.at[block_rows(source_z * n_x + q), cols_here]
        return pltpu.make_async_remote_copy(
            src_ref=dst,
            dst_ref=dst,
            send_sem=z_send.at[d, t, q],
            recv_sem=z_recv.at[d, t, q],
            device_id=(up if d == 0 else down, cd),
            device_id_type=MESH,
        )

    for t in range(steps):
        for q in range(n_x):
            for d in (0, 1):
                if t > 0:
                    z_arrival(d, t - 1, q).wait_recv()
                z_copy(d, t, q).start()
    for q in range(n_x):
        for d in (0, 1):
            z_arrival(d, steps - 1, q).wait_recv()
    for i in range(1, n_x):
        x_copy(i, False).wait_send()
    for t in range(steps):
        for q in range(n_x):
            for d in (0, 1):
                z_copy(d, t, q).wait_send()
    out_ref[...] = held[...]


def gather_rows(amplitudes, n_x, n_z):
    rows, cols = amplitudes.shape
    steps = n_z // 2
    return pl.pallas_call(
        functools.partial(gather_kernel, n_x, n_z),
        out_shape=jax.ShapeDtypeStruct((rows * n_x * n_z, cols), amplitudes.dtype),
        in_specs=[pl.BlockSpec(memory_space=pltpu.VMEM)],
        out_specs=pl.BlockSpec(memory_space=pltpu.VMEM),
        scratch_shapes=[
            pltpu.VMEM((rows * n_x * n_z, cols), amplitudes.dtype),
            pltpu.SemaphoreType.DMA(()),
            pltpu.SemaphoreType.DMA((n_x,)),
            pltpu.SemaphoreType.DMA((n_x,)),
            pltpu.SemaphoreType.DMA((2, steps, n_x)),
            pltpu.SemaphoreType.DMA((2, steps, n_x)),
        ],
        compiler_params=pltpu.CompilerParams(collective_id=0, has_side_effects=True),
    )(amplitudes)


def x_extent(mesh):
    first = mesh.devices.reshape(mesh.shape["ab"], -1)[:, 0]
    try:
        return len({d.coords[0] for d in first})
    except AttributeError:
        return 2


def scatter_kernel(n_y, n_chunks, part_ref, out_ref, pair, send_r, recv_r, send_l, recv_l,
                   pair_send, pair_recv, ring_send, ring_recv):
    ab = lax.axis_index("ab")
    cd = lax.axis_index("cd")
    y, core = cd // 2, lax.rem(cd, 2)
    other = 1 - core
    right = lax.rem(y + 1, n_y) * 2 + core
    left = lax.rem(y + n_y - 1, n_y) * 2 + core
    partner = y * 2 + other
    half = out_ref.shape[1] // 2
    width = half // n_chunks

    barrier = pltpu.get_barrier_semaphore()
    for peer in (partner, right, left):
        pl.semaphore_signal(barrier, inc=1, device_id=(ab, peer), device_id_type=MESH)
    pl.semaphore_wait(barrier, 3)

    order = []
    for k in list(range(1, n_y // 2 + 1)) + [0]:
        for sign in (1, -1):
            if (sign * k) % n_y not in [j % n_y for j in order]:
                order.append(sign * k)

    def pair_copy(k):
        b = lax.rem(y + k + n_y, n_y)
        return pltpu.make_async_remote_copy(
            src_ref=part_ref.at[b, other],
            dst_ref=pair.at[b],
            send_sem=pair_send.at[b],
            recv_sem=pair_recv.at[b],
            device_id=(ab, partner),
            device_id_type=MESH,
        )

    for k in order:
        pair_copy(k).start()

    def own(k, cols):
        b = lax.rem(y + k + n_y, n_y)
        return part_ref[b, core, :, cols] + pair[b, :, cols]

    def columns(d, q):
        start = d * half + q * width
        return slice(start, start + width)

    sends = (send_r, send_l)
    recvs = (recv_r, recv_l)

    def ring_copy(d, s, q):
        return pltpu.make_async_remote_copy(
            src_ref=sends[d].at[s, q],
            dst_ref=recvs[d].at[s, q],
            send_sem=ring_send.at[d, s, q],
            recv_sem=ring_recv.at[d, s, q],
            device_id=(ab, right if d == 0 else left),
            device_id_type=MESH,
        )

    waited = set()

    def need(k):
        k = k % n_y
        if k not in waited:
            waited.add(k)
            pair_copy(k if k <= n_y // 2 else k - n_y).wait_recv()

    for s in range(n_y - 1):
        need(-(s + 1))
        need(s + 1)
        for q in range(n_chunks):
            for d in (0, 1):
                k = -(s + 1) if d == 0 else s + 1
                if s == 0:
                    sends[d][s, q] = own(k, columns(d, q))
                else:
                    ring_copy(d, s - 1, q).wait_recv()
                    sends[d][s, q] = recvs[d][s - 1, q] + own(k, columns(d, q))
                ring_copy(d, s, q).start()
    need(0)
    for q in range(n_chunks):
        for d in (0, 1):
            ring_copy(d, n_y - 2, q).wait_recv()
            out_ref[:, columns(d, q)] = recvs[d][n_y - 2, q] + own(0, columns(d, q))
    for k in order:
        pair_copy(k).wait_send()
    for s in range(n_y - 1):
        for q in range(n_chunks):
            ring_copy(0, s, q).wait_send()
            ring_copy(1, s, q).wait_send()


def scatter_rows(partial_value, n_cd, n_chunks=8):
    n_y = n_cd // 2
    total_rows, cols = partial_value.shape
    rows = total_rows // n_cd
    blocks = partial_value.reshape(n_y, 2, rows, cols)
    width = cols // 2 // n_chunks
    slots = pltpu.VMEM((n_y - 1, n_chunks, rows, width), jnp.float32)
    return pl.pallas_call(
        functools.partial(scatter_kernel, n_y, n_chunks),
        out_shape=jax.ShapeDtypeStruct((rows, cols), partial_value.dtype),
        in_specs=[pl.BlockSpec(memory_space=pltpu.VMEM)],
        out_specs=pl.BlockSpec(memory_space=pltpu.VMEM),
        scratch_shapes=[
            pltpu.VMEM((n_y, rows, cols), jnp.float32),
            slots,
            slots,
            slots,
            slots,
            pltpu.SemaphoreType.DMA((n_y,)),
            pltpu.SemaphoreType.DMA((n_y,)),
            pltpu.SemaphoreType.DMA((2, n_y - 1, n_chunks)),
            pltpu.SemaphoreType.DMA((2, n_y - 1, n_chunks)),
        ],
        compiler_params=pltpu.CompilerParams(collective_id=1, has_side_effects=True),
    )(blocks)


def on_device(n_x, n_z, n_cd, amplitudes, integrals, ij_pairs, ab_pairs, eps_occ, eps_vir):
    partial_value = contract_rows(gather_rows(amplitudes, n_x, n_z), integrals)
    ladder = scatter_rows(partial_value, n_cd)
    first_occ = lookup_energy(ij_pairs[:, 0], eps_occ)[:, None]
    second_occ = lookup_energy(ij_pairs[:, 1], eps_occ)[:, None]
    first_vir = lookup_energy(ab_pairs[:, 0], eps_vir)[None, :]
    second_vir = lookup_energy(ab_pairs[:, 1], eps_vir)[None, :]
    denominator = first_occ + second_occ - first_vir - second_vir
    update = ladder / denominator
    return (ladder, update)


def solution(mesh):
    in_specs = (P("ab", "cd"), P("ab", "cd"), P("cd", None), P("ab", None), P(), P())
    out_specs = (P("cd", "ab"), P("cd", "ab"))
    return jax.shard_map(
        functools.partial(on_device, x_extent(mesh), mesh.shape["ab"] // x_extent(mesh), mesh.shape["cd"]),
        mesh=mesh,
        in_specs=in_specs,
        out_specs=out_specs,
        check_vma=False,
    )
```

```python
import functools

import jax
import jax.numpy as jnp
from jax import lax
from jax.experimental import pallas as pl
from jax.experimental.pallas import tpu as pltpu
from jax.sharding import PartitionSpec as P

MESH = pl.DeviceIdType.MESH


def lookup_energy(indices, energies):
    lanes = 128
    groups = -(-energies.shape[0] // lanes)
    table = jnp.pad(energies, (0, groups * lanes - energies.shape[0])).reshape(groups, lanes)
    low = lax.rem(indices, lanes)
    high = indices // lanes
    one_hot = (low[:, None] == lax.broadcasted_iota(jnp.int32, (indices.shape[0], lanes), 1)).astype(jnp.float32)
    by_group = lax.dot_general(
        one_hot, table, (((1,), (1,)), ((), ())),
        precision=lax.Precision.HIGHEST, preferred_element_type=jnp.float32,
    )
    chosen = high[:, None] == lax.broadcasted_iota(jnp.int32, by_group.shape, 1)
    return jnp.sum(jnp.where(chosen, by_group, jnp.float32(0.0)), axis=1)


def contract_rows(row_block, col_block):
    return lax.dot_general(
        row_block,
        col_block,
        (((1,), (1,)), ((), ())),
        precision=lax.Precision.HIGH,
        preferred_element_type=jnp.float32,
    )


def gather_kernel(n_x, n_z, amp_ref, out_ref, held, local_sem, x_send, x_recv, z_send, z_recv):
    ab = lax.axis_index("ab")
    cd = lax.axis_index("cd")
    z, x = ab // n_x, lax.rem(ab, n_x)
    rows = amp_ref.shape[0]
    group = rows * n_x
    cols = amp_ref.shape[1]
    up = lax.rem(z + 1, n_z) * n_x + x
    down = lax.rem(z + n_z - 1, n_z) * n_x + x

    barrier = pltpu.get_barrier_semaphore()
    for i in range(1, n_x):
        pl.semaphore_signal(barrier, inc=1, device_id=(z * n_x + lax.rem(x + i, n_x), cd), device_id_type=MESH)
    pl.semaphore_signal(barrier, inc=1, device_id=(up, cd), device_id_type=MESH)
    pl.semaphore_signal(barrier, inc=1, device_id=(down, cd), device_id_type=MESH)
    pl.semaphore_wait(barrier, n_x + 1)

    def block_rows(a_index):
        return pl.ds(pl.multiple_of(a_index * rows, rows), rows)

    def x_copy(i, receiving):
        sender = lax.rem(x + n_x - i, n_x) if receiving else x
        target = lax.rem(x + i, n_x)
        return pltpu.make_async_remote_copy(
            src_ref=amp_ref,
            dst_ref=held.at[block_rows(z * n_x + sender)],
            send_sem=x_send.at[target],
            recv_sem=x_recv.at[sender],
            device_id=(z * n_x + target, cd),
            device_id_type=MESH,
        )

    for i in range(1, n_x):
        x_copy(i, False).start()
    local = pltpu.make_async_copy(amp_ref, held.at[block_rows(ab)], local_sem)
    local.start()
    local.wait()
    for i in range(1, n_x):
        x_copy(i, True).wait_recv()

    steps = n_z // 2

    def z_copy(d, t, q):
        source_z = lax.rem(z + n_z - t, n_z) if d == 0 else lax.rem(z + t, n_z)
        cols_here = slice(0, cols)
        if t == steps - 1:
            cols_here = slice(0, cols // 2) if d == 0 else slice(cols // 2, cols)
        src = held.at[block_rows(source_z * n_x + q), cols_here]
        return pltpu.make_async_remote_copy(
            src_ref=src,
            dst_ref=src,
            send_sem=z_send.at[d, t, q],
            recv_sem=z_recv.at[d, t, q],
            device_id=(up if d == 0 else down, cd),
            device_id_type=MESH,
        )

    def z_arrival(d, t, q):
        source_z = lax.rem(z + n_z - t - 1, n_z) if d == 0 else lax.rem(z + t + 1, n_z)
        cols_here = slice(0, cols)
        if t == steps - 1:
            cols_here = slice(0, cols // 2) if d == 0 else slice(cols // 2, cols)
        dst = held.at[block_rows(source_z * n_x + q), cols_here]
        return pltpu.make_async_remote_copy(
            src_ref=dst,
            dst_ref=dst,
            send_sem=z_send.at[d, t, q],
            recv_sem=z_recv.at[d, t, q],
            device_id=(up if d == 0 else down, cd),
            device_id_type=MESH,
        )

    for t in range(steps):
        for q in range(n_x):
            for d in (0, 1):
                if t > 0:
                    z_arrival(d, t - 1, q).wait_recv()
                z_copy(d, t, q).start()
    for q in range(n_x):
        for d in (0, 1):
            z_arrival(d, steps - 1, q).wait_recv()
    for i in range(1, n_x):
        x_copy(i, False).wait_send()
    for t in range(steps):
        for q in range(n_x):
            for d in (0, 1):
                z_copy(d, t, q).wait_send()
    out_ref[...] = held[...]


def gather_rows(amplitudes, n_x, n_z):
    rows, cols = amplitudes.shape
    steps = n_z // 2
    return pl.pallas_call(
        functools.partial(gather_kernel, n_x, n_z),
        out_shape=jax.ShapeDtypeStruct((rows * n_x * n_z, cols), amplitudes.dtype),
        in_specs=[pl.BlockSpec(memory_space=pltpu.VMEM)],
        out_specs=pl.BlockSpec(memory_space=pltpu.VMEM),
        scratch_shapes=[
            pltpu.VMEM((rows * n_x * n_z, cols), amplitudes.dtype),
            pltpu.SemaphoreType.DMA(()),
            pltpu.SemaphoreType.DMA((n_x,)),
            pltpu.SemaphoreType.DMA((n_x,)),
            pltpu.SemaphoreType.DMA((2, steps, n_x)),
            pltpu.SemaphoreType.DMA((2, steps, n_x)),
        ],
        compiler_params=pltpu.CompilerParams(collective_id=0, has_side_effects=True),
    )(amplitudes)


def x_extent(mesh):
    first = mesh.devices.reshape(mesh.shape["ab"], -1)[:, 0]
    try:
        return len({d.coords[0] for d in first})
    except AttributeError:
        return 2


def scatter_kernel(n_y, n_chunks, part_ref, out_ref, pair, send_r, recv_r, send_l, recv_l,
                   pair_send, pair_recv, ring_send, ring_recv):
    ab = lax.axis_index("ab")
    cd = lax.axis_index("cd")
    y, core = cd // 2, lax.rem(cd, 2)
    other = 1 - core
    right = lax.rem(y + 1, n_y) * 2 + core
    left = lax.rem(y + n_y - 1, n_y) * 2 + core
    partner = y * 2 + other
    half = out_ref.shape[1] // 2
    width = half // n_chunks

    barrier = pltpu.get_barrier_semaphore()
    for peer in (partner, right, left):
        pl.semaphore_signal(barrier, inc=1, device_id=(ab, peer), device_id_type=MESH)
    pl.semaphore_wait(barrier, 3)

    order = [item for s in range(n_y - 1) for item in ((-(s + 1), 0), (s + 1, 1))] + [(0, 0), (0, 1)]

    def pair_copy(k, d):
        b = lax.rem(y + k + n_y * n_y, n_y)
        cols = slice(d * half, (d + 1) * half)
        return pltpu.make_async_remote_copy(
            src_ref=part_ref.at[b, other, :, cols],
            dst_ref=pair.at[b, :, cols],
            send_sem=pair_send.at[b, d],
            recv_sem=pair_recv.at[b, d],
            device_id=(ab, partner),
            device_id_type=MESH,
        )

    for k, d in order:
        pair_copy(k, d).start()

    def own(k, cols):
        b = lax.rem(y + k + n_y, n_y)
        return part_ref[b, core, :, cols] + pair[b, :, cols]

    def columns(d, q):
        start = d * half + q * width
        return slice(start, start + width)

    sends = (send_r, send_l)
    recvs = (recv_r, recv_l)

    def ring_copy(d, s, q):
        return pltpu.make_async_remote_copy(
            src_ref=sends[d].at[s, q],
            dst_ref=recvs[d].at[s, q],
            send_sem=ring_send.at[d, s, q],
            recv_sem=ring_recv.at[d, s, q],
            device_id=(ab, right if d == 0 else left),
            device_id_type=MESH,
        )

    for s in range(n_y - 1):
        pair_copy(-(s + 1), 0).wait_recv()
        pair_copy(s + 1, 1).wait_recv()
        for q in range(n_chunks):
            for d in (0, 1):
                k = -(s + 1) if d == 0 else s + 1
                if s == 0:
                    sends[d][s, q] = own(k, columns(d, q))
                else:
                    ring_copy(d, s - 1, q).wait_recv()
                    sends[d][s, q] = recvs[d][s - 1, q] + own(k, columns(d, q))
                ring_copy(d, s, q).start()
    pair_copy(0, 0).wait_recv()
    pair_copy(0, 1).wait_recv()
    for q in range(n_chunks):
        for d in (0, 1):
            ring_copy(d, n_y - 2, q).wait_recv()
            out_ref[:, columns(d, q)] = recvs[d][n_y - 2, q] + own(0, columns(d, q))
    for k, d in order:
        pair_copy(k, d).wait_send()
    for s in range(n_y - 1):
        for q in range(n_chunks):
            ring_copy(0, s, q).wait_send()
            ring_copy(1, s, q).wait_send()


def scatter_rows(partial_value, n_cd, n_chunks=4):
    n_y = n_cd // 2
    total_rows, cols = partial_value.shape
    rows = total_rows // n_cd
    blocks = partial_value.reshape(n_y, 2, rows, cols)
    width = cols // 2 // n_chunks
    slots = pltpu.VMEM((n_y - 1, n_chunks, rows, width), jnp.float32)
    return pl.pallas_call(
        functools.partial(scatter_kernel, n_y, n_chunks),
        out_shape=jax.ShapeDtypeStruct((rows, cols), partial_value.dtype),
        in_specs=[pl.BlockSpec(memory_space=pltpu.VMEM)],
        out_specs=pl.BlockSpec(memory_space=pltpu.VMEM),
        scratch_shapes=[
            pltpu.VMEM((n_y, rows, cols), jnp.float32),
            slots,
            slots,
            slots,
            slots,
            pltpu.SemaphoreType.DMA((n_y, 2)),
            pltpu.SemaphoreType.DMA((n_y, 2)),
            pltpu.SemaphoreType.DMA((2, n_y - 1, n_chunks)),
            pltpu.SemaphoreType.DMA((2, n_y - 1, n_chunks)),
        ],
        compiler_params=pltpu.CompilerParams(collective_id=1, has_side_effects=True),
    )(blocks)


def on_device(n_x, n_z, n_cd, amplitudes, integrals, ij_pairs, ab_pairs, eps_occ, eps_vir):
    partial_value = contract_rows(gather_rows(amplitudes, n_x, n_z), integrals)
    ladder = scatter_rows(partial_value, n_cd)
    first_occ = lookup_energy(ij_pairs[:, 0], eps_occ)[:, None]
    second_occ = lookup_energy(ij_pairs[:, 1], eps_occ)[:, None]
    first_vir = lookup_energy(ab_pairs[:, 0], eps_vir)[None, :]
    second_vir = lookup_energy(ab_pairs[:, 1], eps_vir)[None, :]
    denominator = first_occ + second_occ - first_vir - second_vir
    update = ladder / denominator
    return (ladder, update)


def solution(mesh):
    in_specs = (P("ab", "cd"), P("ab", "cd"), P("cd", None), P("ab", None), P(), P())
    out_specs = (P("cd", "ab"), P("cd", "ab"))
    return jax.shard_map(
        functools.partial(on_device, x_extent(mesh), mesh.shape["ab"] // x_extent(mesh), mesh.shape["cd"]),
        mesh=mesh,
        in_specs=in_specs,
        out_specs=out_specs,
        check_vma=False,
    )
```

```python
import functools

import jax
import jax.numpy as jnp
from jax import lax
from jax.experimental import pallas as pl
from jax.experimental.pallas import tpu as pltpu
from jax.sharding import PartitionSpec as P

MESH = pl.DeviceIdType.MESH


def lookup_energy(indices, energies):
    lanes = 128
    groups = -(-energies.shape[0] // lanes)
    table = jnp.pad(energies, (0, groups * lanes - energies.shape[0])).reshape(groups, lanes)
    low = lax.rem(indices, lanes)
    high = indices // lanes
    one_hot = (low[:, None] == lax.broadcasted_iota(jnp.int32, (indices.shape[0], lanes), 1)).astype(jnp.float32)
    by_group = lax.dot_general(
        one_hot, table, (((1,), (1,)), ((), ())),
        precision=lax.Precision.HIGHEST, preferred_element_type=jnp.float32,
    )
    chosen = high[:, None] == lax.broadcasted_iota(jnp.int32, by_group.shape, 1)
    return jnp.sum(jnp.where(chosen, by_group, jnp.float32(0.0)), axis=1)


def contract_rows(row_block, col_block):
    return lax.dot_general(
        row_block,
        col_block,
        (((1,), (1,)), ((), ())),
        precision=lax.Precision.HIGH,
        preferred_element_type=jnp.float32,
    )


def gather_kernel(n_x, n_z, amp_ref, int_ref, out_ref, held, int_hi, int_lo, local_sem, x_send, x_recv, z_send, z_recv):
    ab = lax.axis_index("ab")
    cd = lax.axis_index("cd")
    z, x = ab // n_x, lax.rem(ab, n_x)
    rows = amp_ref.shape[0]
    group = rows * n_x
    cols = amp_ref.shape[1]
    up = lax.rem(z + 1, n_z) * n_x + x
    down = lax.rem(z + n_z - 1, n_z) * n_x + x

    barrier = pltpu.get_barrier_semaphore()
    for i in range(1, n_x):
        pl.semaphore_signal(barrier, inc=1, device_id=(z * n_x + lax.rem(x + i, n_x), cd), device_id_type=MESH)
    pl.semaphore_signal(barrier, inc=1, device_id=(up, cd), device_id_type=MESH)
    pl.semaphore_signal(barrier, inc=1, device_id=(down, cd), device_id_type=MESH)
    pl.semaphore_wait(barrier, n_x + 1)

    def block_rows(a_index):
        return pl.ds(pl.multiple_of(a_index * rows, rows), rows)

    def x_copy(i, receiving):
        sender = lax.rem(x + n_x - i, n_x) if receiving else x
        target = lax.rem(x + i, n_x)
        return pltpu.make_async_remote_copy(
            src_ref=amp_ref,
            dst_ref=held.at[block_rows(z * n_x + sender)],
            send_sem=x_send.at[target],
            recv_sem=x_recv.at[sender],
            device_id=(z * n_x + target, cd),
            device_id_type=MESH,
        )

    for i in range(1, n_x):
        x_copy(i, False).start()
    local = pltpu.make_async_copy(amp_ref, held.at[block_rows(ab)], local_sem)
    local.start()

    tile = 256
    n_tiles = int_ref.shape[0] // tile

    def split(j, carry):
        span = pl.ds(pl.multiple_of(j * tile, tile), tile)
        value = int_ref[span, :]
        high = value.astype(jnp.bfloat16)
        int_hi[span, :] = high
        int_lo[span, :] = (value - high.astype(jnp.float32)).astype(jnp.bfloat16)
        return carry

    lax.fori_loop(0, n_tiles, split, 0)

    def contract(group_z):
        span = pl.ds(pl.multiple_of(group_z * group, group), group)
        value = held[span, :]
        high = value.astype(jnp.bfloat16)
        low = (value - high.astype(jnp.float32)).astype(jnp.bfloat16)
        dims = (((1,), (1,)), ((), ()))

        def one_tile(j, carry):
            cols = pl.ds(pl.multiple_of(j * tile, tile), tile)
            b_high = int_hi[cols, :]
            b_low = int_lo[cols, :]
            acc = lax.dot_general(high, b_high, dims, preferred_element_type=jnp.float32)
            acc += lax.dot_general(high, b_low, dims, preferred_element_type=jnp.float32)
            acc += lax.dot_general(low, b_high, dims, preferred_element_type=jnp.float32)
            out_ref[span, cols] = acc
            return carry

        lax.fori_loop(0, n_tiles, one_tile, 0)

    local.wait()
    for i in range(1, n_x):
        x_copy(i, True).wait_recv()

    steps = n_z // 2

    def z_copy(d, t, q):
        source_z = lax.rem(z + n_z - t, n_z) if d == 0 else lax.rem(z + t, n_z)
        cols_here = slice(0, cols)
        if t == steps - 1:
            cols_here = slice(0, cols // 2) if d == 0 else slice(cols // 2, cols)
        src = held.at[block_rows(source_z * n_x + q), cols_here]
        return pltpu.make_async_remote_copy(
            src_ref=src,
            dst_ref=src,
            send_sem=z_send.at[d, t, q],
            recv_sem=z_recv.at[d, t, q],
            device_id=(up if d == 0 else down, cd),
            device_id_type=MESH,
        )

    def z_arrival(d, t, q):
        source_z = lax.rem(z + n_z - t - 1, n_z) if d == 0 else lax.rem(z + t + 1, n_z)
        cols_here = slice(0, cols)
        if t == steps - 1:
            cols_here = slice(0, cols // 2) if d == 0 else slice(cols // 2, cols)
        dst = held.at[block_rows(source_z * n_x + q), cols_here]
        return pltpu.make_async_remote_copy(
            src_ref=dst,
            dst_ref=dst,
            send_sem=z_send.at[d, t, q],
            recv_sem=z_recv.at[d, t, q],
            device_id=(up if d == 0 else down, cd),
            device_id_type=MESH,
        )

    for q in range(n_x):
        for d in (0, 1):
            z_copy(d, 0, q).start()
    contract(z)
    for t in range(steps):
        for q in range(n_x):
            for d in (0, 1):
                z_arrival(d, t, q).wait_recv()
                if t + 1 < steps:
                    z_copy(d, t + 1, q).start()
        if t + 1 < steps:
            contract(lax.rem(z + n_z - t - 1, n_z))
            contract(lax.rem(z + t + 1, n_z))
        else:
            contract(lax.rem(z + t + 1, n_z))
    for i in range(1, n_x):
        x_copy(i, False).wait_send()
    for t in range(steps):
        for q in range(n_x):
            for d in (0, 1):
                z_copy(d, t, q).wait_send()


def gather_contract(amplitudes, integrals, n_x, n_z):
    rows, cols = amplitudes.shape
    steps = n_z // 2
    return pl.pallas_call(
        functools.partial(gather_kernel, n_x, n_z),
        out_shape=jax.ShapeDtypeStruct((rows * n_x * n_z, integrals.shape[0]), jnp.float32),
        in_specs=[pl.BlockSpec(memory_space=pltpu.VMEM)] * 2,
        out_specs=pl.BlockSpec(memory_space=pltpu.VMEM),
        scratch_shapes=[
            pltpu.VMEM((rows * n_x * n_z, cols), amplitudes.dtype),
            pltpu.VMEM(integrals.shape, jnp.bfloat16),
            pltpu.VMEM(integrals.shape, jnp.bfloat16),
            pltpu.SemaphoreType.DMA(()),
            pltpu.SemaphoreType.DMA((n_x,)),
            pltpu.SemaphoreType.DMA((n_x,)),
            pltpu.SemaphoreType.DMA((2, steps, n_x)),
            pltpu.SemaphoreType.DMA((2, steps, n_x)),
        ],
        compiler_params=pltpu.CompilerParams(collective_id=0, has_side_effects=True),
    )(amplitudes, integrals)


def x_extent(mesh):
    first = mesh.devices.reshape(mesh.shape["ab"], -1)[:, 0]
    try:
        return len({d.coords[0] for d in first})
    except AttributeError:
        return 2


def scatter_kernel(n_y, n_chunks, part_ref, out_ref, pair, send_r, recv_r, send_l, recv_l,
                   pair_send, pair_recv, ring_send, ring_recv):
    ab = lax.axis_index("ab")
    cd = lax.axis_index("cd")
    y, core = cd // 2, lax.rem(cd, 2)
    other = 1 - core
    right = lax.rem(y + 1, n_y) * 2 + core
    left = lax.rem(y + n_y - 1, n_y) * 2 + core
    partner = y * 2 + other
    half = out_ref.shape[1] // 2
    width = half // n_chunks

    barrier = pltpu.get_barrier_semaphore()
    for peer in (partner, right, left):
        pl.semaphore_signal(barrier, inc=1, device_id=(ab, peer), device_id_type=MESH)
    pl.semaphore_wait(barrier, 3)

    order = [item for s in range(n_y - 1) for item in ((-(s + 1), 0), (s + 1, 1))] + [(0, 0), (0, 1)]

    def pair_copy(k, d):
        b = lax.rem(y + k + n_y * n_y, n_y)
        cols = slice(d * half, (d + 1) * half)
        return pltpu.make_async_remote_copy(
            src_ref=part_ref.at[b, other, :, cols],
            dst_ref=pair.at[b, :, cols],
            send_sem=pair_send.at[b, d],
            recv_sem=pair_recv.at[b, d],
            device_id=(ab, partner),
            device_id_type=MESH,
        )

    for k, d in order:
        pair_copy(k, d).start()

    def own(k, cols):
        b = lax.rem(y + k + n_y, n_y)
        return part_ref[b, core, :, cols] + pair[b, :, cols]

    def columns(d, q):
        start = d * half + q * width
        return slice(start, start + width)

    sends = (send_r, send_l)
    recvs = (recv_r, recv_l)

    def ring_copy(d, s, q):
        return pltpu.make_async_remote_copy(
            src_ref=sends[d].at[s, q],
            dst_ref=recvs[d].at[s, q],
            send_sem=ring_send.at[d, s, q],
            recv_sem=ring_recv.at[d, s, q],
            device_id=(ab, right if d == 0 else left),
            device_id_type=MESH,
        )

    for s in range(n_y - 1):
        pair_copy(-(s + 1), 0).wait_recv()
        pair_copy(s + 1, 1).wait_recv()
        for q in range(n_chunks):
            for d in (0, 1):
                k = -(s + 1) if d == 0 else s + 1
                if s == 0:
                    sends[d][s, q] = own(k, columns(d, q))
                else:
                    ring_copy(d, s - 1, q).wait_recv()
                    sends[d][s, q] = recvs[d][s - 1, q] + own(k, columns(d, q))
                ring_copy(d, s, q).start()
    pair_copy(0, 0).wait_recv()
    pair_copy(0, 1).wait_recv()
    for q in range(n_chunks):
        for d in (0, 1):
            ring_copy(d, n_y - 2, q).wait_recv()
            out_ref[:, columns(d, q)] = recvs[d][n_y - 2, q] + own(0, columns(d, q))
    for k, d in order:
        pair_copy(k, d).wait_send()
    for s in range(n_y - 1):
        for q in range(n_chunks):
            ring_copy(0, s, q).wait_send()
            ring_copy(1, s, q).wait_send()


def scatter_rows(partial_value, n_cd, n_chunks=4):
    n_y = n_cd // 2
    total_rows, cols = partial_value.shape
    rows = total_rows // n_cd
    blocks = partial_value.reshape(n_y, 2, rows, cols)
    width = cols // 2 // n_chunks
    slots = pltpu.VMEM((n_y - 1, n_chunks, rows, width), jnp.float32)
    return pl.pallas_call(
        functools.partial(scatter_kernel, n_y, n_chunks),
        out_shape=jax.ShapeDtypeStruct((rows, cols), partial_value.dtype),
        in_specs=[pl.BlockSpec(memory_space=pltpu.VMEM)],
        out_specs=pl.BlockSpec(memory_space=pltpu.VMEM),
        scratch_shapes=[
            pltpu.VMEM((n_y, rows, cols), jnp.float32),
            slots,
            slots,
            slots,
            slots,
            pltpu.SemaphoreType.DMA((n_y, 2)),
            pltpu.SemaphoreType.DMA((n_y, 2)),
            pltpu.SemaphoreType.DMA((2, n_y - 1, n_chunks)),
            pltpu.SemaphoreType.DMA((2, n_y - 1, n_chunks)),
        ],
        compiler_params=pltpu.CompilerParams(collective_id=1, has_side_effects=True),
    )(blocks)


def on_device(n_x, n_z, n_cd, amplitudes, integrals, ij_pairs, ab_pairs, eps_occ, eps_vir):
    partial_value = gather_contract(amplitudes, integrals, n_x, n_z)
    ladder = scatter_rows(partial_value, n_cd)
    first_occ = lookup_energy(ij_pairs[:, 0], eps_occ)[:, None]
    second_occ = lookup_energy(ij_pairs[:, 1], eps_occ)[:, None]
    first_vir = lookup_energy(ab_pairs[:, 0], eps_vir)[None, :]
    second_vir = lookup_energy(ab_pairs[:, 1], eps_vir)[None, :]
    denominator = first_occ + second_occ - first_vir - second_vir
    update = ladder / denominator
    return (ladder, update)


def solution(mesh):
    in_specs = (P("ab", "cd"), P("ab", "cd"), P("cd", None), P("ab", None), P(), P())
    out_specs = (P("cd", "ab"), P("cd", "ab"))
    return jax.shard_map(
        functools.partial(on_device, x_extent(mesh), mesh.shape["ab"] // x_extent(mesh), mesh.shape["cd"]),
        mesh=mesh,
        in_specs=in_specs,
        out_specs=out_specs,
        check_vma=False,
    )
```

```python
import functools

import jax
import jax.numpy as jnp
from jax import lax
from jax.experimental import pallas as pl
from jax.experimental.pallas import tpu as pltpu
from jax.sharding import PartitionSpec as P

MESH = pl.DeviceIdType.MESH


def lookup_energy(indices, energies):
    lanes = 128
    groups = -(-energies.shape[0] // lanes)
    table = jnp.pad(energies, (0, groups * lanes - energies.shape[0])).reshape(groups, lanes)
    low = lax.rem(indices, lanes)
    high = indices // lanes
    one_hot = (low[:, None] == lax.broadcasted_iota(jnp.int32, (indices.shape[0], lanes), 1)).astype(jnp.float32)
    by_group = lax.dot_general(
        one_hot, table, (((1,), (1,)), ((), ())),
        precision=lax.Precision.HIGHEST, preferred_element_type=jnp.float32,
    )
    chosen = high[:, None] == lax.broadcasted_iota(jnp.int32, by_group.shape, 1)
    return jnp.sum(jnp.where(chosen, by_group, jnp.float32(0.0)), axis=1)


def contract_rows(row_block, col_block):
    return lax.dot_general(
        row_block,
        col_block,
        (((1,), (1,)), ((), ())),
        precision=lax.Precision.HIGH,
        preferred_element_type=jnp.float32,
    )


def gather_kernel(n_x, n_z, amp_ref, int_ref, out_ref, held, int_hi, int_lo, local_sem, x_send, x_recv, z_send, z_recv):
    ab = lax.axis_index("ab")
    cd = lax.axis_index("cd")
    z, x = ab // n_x, lax.rem(ab, n_x)
    rows = amp_ref.shape[0]
    group = rows * n_x
    cols = amp_ref.shape[1]
    up = lax.rem(z + 1, n_z) * n_x + x
    down = lax.rem(z + n_z - 1, n_z) * n_x + x

    barrier = pltpu.get_barrier_semaphore()
    for i in range(1, n_x):
        pl.semaphore_signal(barrier, inc=1, device_id=(z * n_x + lax.rem(x + i, n_x), cd), device_id_type=MESH)
    pl.semaphore_signal(barrier, inc=1, device_id=(up, cd), device_id_type=MESH)
    pl.semaphore_signal(barrier, inc=1, device_id=(down, cd), device_id_type=MESH)
    pl.semaphore_wait(barrier, n_x + 1)

    def block_rows(a_index):
        return pl.ds(pl.multiple_of(a_index * rows, rows), rows)

    def x_copy(i, receiving):
        sender = lax.rem(x + n_x - i, n_x) if receiving else x
        target = lax.rem(x + i, n_x)
        return pltpu.make_async_remote_copy(
            src_ref=amp_ref,
            dst_ref=held.at[block_rows(z * n_x + sender)],
            send_sem=x_send.at[target],
            recv_sem=x_recv.at[sender],
            device_id=(z * n_x + target, cd),
            device_id_type=MESH,
        )

    for i in range(1, n_x):
        x_copy(i, False).start()
    local = pltpu.make_async_copy(amp_ref, held.at[block_rows(ab)], local_sem)
    local.start()

    tile = 256
    n_tiles = int_ref.shape[0] // tile

    def split(j, carry):
        span = pl.ds(pl.multiple_of(j * tile, tile), tile)
        value = int_ref[span, :]
        high = value.astype(jnp.bfloat16)
        int_hi[span, :] = high
        int_lo[span, :] = (value - high.astype(jnp.float32)).astype(jnp.bfloat16)
        return carry

    lax.fori_loop(0, n_tiles, split, 0)

    def contract(group_z):
        span = pl.ds(pl.multiple_of(group_z * group, group), group)
        value = held[span, :]
        high = value.astype(jnp.bfloat16)
        low = (value - high.astype(jnp.float32)).astype(jnp.bfloat16)
        dims = (((1,), (1,)), ((), ()))

        def one_tile(j, carry):
            cols = pl.ds(pl.multiple_of(j * tile, tile), tile)
            b_high = int_hi[cols, :]
            b_low = int_lo[cols, :]
            acc = lax.dot_general(high, b_high, dims, preferred_element_type=jnp.float32)
            acc += lax.dot_general(high, b_low, dims, preferred_element_type=jnp.float32)
            acc += lax.dot_general(low, b_high, dims, preferred_element_type=jnp.float32)
            out_ref[span, cols] = acc
            return carry

        lax.fori_loop(0, n_tiles, one_tile, 0)

    local.wait()
    for i in range(1, n_x):
        x_copy(i, True).wait_recv()

    steps = n_z // 2

    def z_copy(d, t, q):
        source_z = lax.rem(z + n_z - t, n_z) if d == 0 else lax.rem(z + t, n_z)
        cols_here = slice(0, cols)
        if t == steps - 1:
            cols_here = slice(0, cols // 2) if d == 0 else slice(cols // 2, cols)
        src = held.at[block_rows(source_z * n_x + q), cols_here]
        return pltpu.make_async_remote_copy(
            src_ref=src,
            dst_ref=src,
            send_sem=z_send.at[d, t, q],
            recv_sem=z_recv.at[d, t, q],
            device_id=(up if d == 0 else down, cd),
            device_id_type=MESH,
        )

    def z_arrival(d, t, q):
        source_z = lax.rem(z + n_z - t - 1, n_z) if d == 0 else lax.rem(z + t + 1, n_z)
        cols_here = slice(0, cols)
        if t == steps - 1:
            cols_here = slice(0, cols // 2) if d == 0 else slice(cols // 2, cols)
        dst = held.at[block_rows(source_z * n_x + q), cols_here]
        return pltpu.make_async_remote_copy(
            src_ref=dst,
            dst_ref=dst,
            send_sem=z_send.at[d, t, q],
            recv_sem=z_recv.at[d, t, q],
            device_id=(up if d == 0 else down, cd),
            device_id_type=MESH,
        )

    for q in range(n_x):
        for d in (0, 1):
            z_copy(d, 0, q).start()
    contract(z)
    for t in range(steps):
        if t == steps - 1:
            for u in range(steps - 1):
                contract(lax.rem(z + n_z - u - 1, n_z))
                contract(lax.rem(z + u + 1, n_z))
        for q in range(n_x):
            for d in (0, 1):
                z_arrival(d, t, q).wait_recv()
                if t + 1 < steps:
                    z_copy(d, t + 1, q).start()
    contract(lax.rem(z + steps, n_z))
    for i in range(1, n_x):
        x_copy(i, False).wait_send()
    for t in range(steps):
        for q in range(n_x):
            for d in (0, 1):
                z_copy(d, t, q).wait_send()


def gather_contract(amplitudes, integrals, n_x, n_z):
    rows, cols = amplitudes.shape
    steps = n_z // 2
    return pl.pallas_call(
        functools.partial(gather_kernel, n_x, n_z),
        out_shape=jax.ShapeDtypeStruct((rows * n_x * n_z, integrals.shape[0]), jnp.float32),
        in_specs=[pl.BlockSpec(memory_space=pltpu.VMEM)] * 2,
        out_specs=pl.BlockSpec(memory_space=pltpu.VMEM),
        scratch_shapes=[
            pltpu.VMEM((rows * n_x * n_z, cols), amplitudes.dtype),
            pltpu.VMEM(integrals.shape, jnp.bfloat16),
            pltpu.VMEM(integrals.shape, jnp.bfloat16),
            pltpu.SemaphoreType.DMA(()),
            pltpu.SemaphoreType.DMA((n_x,)),
            pltpu.SemaphoreType.DMA((n_x,)),
            pltpu.SemaphoreType.DMA((2, steps, n_x)),
            pltpu.SemaphoreType.DMA((2, steps, n_x)),
        ],
        compiler_params=pltpu.CompilerParams(collective_id=0, has_side_effects=True),
    )(amplitudes, integrals)


def x_extent(mesh):
    first = mesh.devices.reshape(mesh.shape["ab"], -1)[:, 0]
    try:
        return len({d.coords[0] for d in first})
    except AttributeError:
        return 2


def scatter_kernel(n_y, n_chunks, part_ref, out_ref, pair, send_r, recv_r, send_l, recv_l,
                   pair_send, pair_recv, ring_send, ring_recv):
    ab = lax.axis_index("ab")
    cd = lax.axis_index("cd")
    y, core = cd // 2, lax.rem(cd, 2)
    other = 1 - core
    right = lax.rem(y + 1, n_y) * 2 + core
    left = lax.rem(y + n_y - 1, n_y) * 2 + core
    partner = y * 2 + other
    half = out_ref.shape[1] // 2
    width = half // n_chunks

    barrier = pltpu.get_barrier_semaphore()
    for peer in (partner, right, left):
        pl.semaphore_signal(barrier, inc=1, device_id=(ab, peer), device_id_type=MESH)
    pl.semaphore_wait(barrier, 3)

    order = [item for s in range(n_y - 1) for item in ((-(s + 1), 0), (s + 1, 1))] + [(0, 0), (0, 1)]

    def pair_copy(k, d):
        b = lax.rem(y + k + n_y * n_y, n_y)
        cols = slice(d * half, (d + 1) * half)
        return pltpu.make_async_remote_copy(
            src_ref=part_ref.at[b, other, :, cols],
            dst_ref=pair.at[b, :, cols],
            send_sem=pair_send.at[b, d],
            recv_sem=pair_recv.at[b, d],
            device_id=(ab, partner),
            device_id_type=MESH,
        )

    for k, d in order:
        pair_copy(k, d).start()

    def own(k, cols):
        b = lax.rem(y + k + n_y, n_y)
        return part_ref[b, core, :, cols] + pair[b, :, cols]

    def columns(d, q):
        start = d * half + q * width
        return slice(start, start + width)

    sends = (send_r, send_l)
    recvs = (recv_r, recv_l)

    def ring_copy(d, s, q):
        return pltpu.make_async_remote_copy(
            src_ref=sends[d].at[s, q],
            dst_ref=recvs[d].at[s, q],
            send_sem=ring_send.at[d, s, q],
            recv_sem=ring_recv.at[d, s, q],
            device_id=(ab, right if d == 0 else left),
            device_id_type=MESH,
        )

    for s in range(n_y - 1):
        pair_copy(-(s + 1), 0).wait_recv()
        pair_copy(s + 1, 1).wait_recv()
        for q in range(n_chunks):
            for d in (0, 1):
                k = -(s + 1) if d == 0 else s + 1
                if s == 0:
                    sends[d][s, q] = own(k, columns(d, q))
                else:
                    ring_copy(d, s - 1, q).wait_recv()
                    sends[d][s, q] = recvs[d][s - 1, q] + own(k, columns(d, q))
                ring_copy(d, s, q).start()
    pair_copy(0, 0).wait_recv()
    pair_copy(0, 1).wait_recv()
    for q in range(n_chunks):
        for d in (0, 1):
            ring_copy(d, n_y - 2, q).wait_recv()
            out_ref[:, columns(d, q)] = recvs[d][n_y - 2, q] + own(0, columns(d, q))
    for k, d in order:
        pair_copy(k, d).wait_send()
    for s in range(n_y - 1):
        for q in range(n_chunks):
            ring_copy(0, s, q).wait_send()
            ring_copy(1, s, q).wait_send()


def scatter_rows(partial_value, n_cd, n_chunks=4):
    n_y = n_cd // 2
    total_rows, cols = partial_value.shape
    rows = total_rows // n_cd
    blocks = partial_value.reshape(n_y, 2, rows, cols)
    width = cols // 2 // n_chunks
    slots = pltpu.VMEM((n_y - 1, n_chunks, rows, width), jnp.float32)
    return pl.pallas_call(
        functools.partial(scatter_kernel, n_y, n_chunks),
        out_shape=jax.ShapeDtypeStruct((rows, cols), partial_value.dtype),
        in_specs=[pl.BlockSpec(memory_space=pltpu.VMEM)],
        out_specs=pl.BlockSpec(memory_space=pltpu.VMEM),
        scratch_shapes=[
            pltpu.VMEM((n_y, rows, cols), jnp.float32),
            slots,
            slots,
            slots,
            slots,
            pltpu.SemaphoreType.DMA((n_y, 2)),
            pltpu.SemaphoreType.DMA((n_y, 2)),
            pltpu.SemaphoreType.DMA((2, n_y - 1, n_chunks)),
            pltpu.SemaphoreType.DMA((2, n_y - 1, n_chunks)),
        ],
        compiler_params=pltpu.CompilerParams(collective_id=1, has_side_effects=True),
    )(blocks)


def on_device(n_x, n_z, n_cd, amplitudes, integrals, ij_pairs, ab_pairs, eps_occ, eps_vir):
    partial_value = gather_contract(amplitudes, integrals, n_x, n_z)
    ladder = scatter_rows(partial_value, n_cd)
    first_occ = lookup_energy(ij_pairs[:, 0], eps_occ)[:, None]
    second_occ = lookup_energy(ij_pairs[:, 1], eps_occ)[:, None]
    first_vir = lookup_energy(ab_pairs[:, 0], eps_vir)[None, :]
    second_vir = lookup_energy(ab_pairs[:, 1], eps_vir)[None, :]
    denominator = first_occ + second_occ - first_vir - second_vir
    update = ladder / denominator
    return (ladder, update)


def solution(mesh):
    in_specs = (P("ab", "cd"), P("ab", "cd"), P("cd", None), P("ab", None), P(), P())
    out_specs = (P("cd", "ab"), P("cd", "ab"))
    return jax.shard_map(
        functools.partial(on_device, x_extent(mesh), mesh.shape["ab"] // x_extent(mesh), mesh.shape["cd"]),
        mesh=mesh,
        in_specs=in_specs,
        out_specs=out_specs,
        check_vma=False,
    )
```

```python
import functools

import jax
import jax.numpy as jnp
from jax import lax
from jax.experimental import pallas as pl
from jax.experimental.pallas import tpu as pltpu
from jax.sharding import PartitionSpec as P

MESH = pl.DeviceIdType.MESH


def lookup_energy(indices, energies):
    lanes = 128
    groups = -(-energies.shape[0] // lanes)
    table = jnp.pad(energies, (0, groups * lanes - energies.shape[0])).reshape(groups, lanes)
    low = lax.rem(indices, lanes)
    high = indices // lanes
    one_hot = (low[:, None] == lax.broadcasted_iota(jnp.int32, (indices.shape[0], lanes), 1)).astype(jnp.float32)
    by_group = lax.dot_general(
        one_hot, table, (((1,), (1,)), ((), ())),
        precision=lax.Precision.HIGHEST, preferred_element_type=jnp.float32,
    )
    chosen = high[:, None] == lax.broadcasted_iota(jnp.int32, by_group.shape, 1)
    return jnp.sum(jnp.where(chosen, by_group, jnp.float32(0.0)), axis=1)


def contract_rows(row_block, col_block):
    return lax.dot_general(
        row_block,
        col_block,
        (((1,), (1,)), ((), ())),
        precision=lax.Precision.HIGH,
        preferred_element_type=jnp.float32,
    )


def gather_kernel(n_x, n_z, amp_ref, out_ref, held, local_sem, x_send, x_recv, z_send, z_recv):
    ab = lax.axis_index("ab")
    cd = lax.axis_index("cd")
    z, x = ab // n_x, lax.rem(ab, n_x)
    rows = amp_ref.shape[0]
    group = rows * n_x
    cols = amp_ref.shape[1]
    up = lax.rem(z + 1, n_z) * n_x + x
    down = lax.rem(z + n_z - 1, n_z) * n_x + x

    barrier = pltpu.get_barrier_semaphore()
    for i in range(1, n_x):
        pl.semaphore_signal(barrier, inc=1, device_id=(z * n_x + lax.rem(x + i, n_x), cd), device_id_type=MESH)
    pl.semaphore_signal(barrier, inc=1, device_id=(up, cd), device_id_type=MESH)
    pl.semaphore_signal(barrier, inc=1, device_id=(down, cd), device_id_type=MESH)
    pl.semaphore_wait(barrier, n_x + 1)

    def block_rows(a_index):
        return pl.ds(pl.multiple_of(a_index * rows, rows), rows)

    def x_copy(i, receiving):
        sender = lax.rem(x + n_x - i, n_x) if receiving else x
        target = lax.rem(x + i, n_x)
        return pltpu.make_async_remote_copy(
            src_ref=amp_ref,
            dst_ref=held.at[block_rows(z * n_x + sender)],
            send_sem=x_send.at[target],
            recv_sem=x_recv.at[sender],
            device_id=(z * n_x + target, cd),
            device_id_type=MESH,
        )

    for i in range(1, n_x):
        x_copy(i, False).start()
    local = pltpu.make_async_copy(amp_ref, held.at[block_rows(ab)], local_sem)
    local.start()
    local.wait()
    for i in range(1, n_x):
        x_copy(i, True).wait_recv()

    steps = n_z // 2

    def z_copy(d, t, q):
        source_z = lax.rem(z + n_z - t, n_z) if d == 0 else lax.rem(z + t, n_z)
        cols_here = slice(0, cols)
        if t == steps - 1:
            cols_here = slice(0, cols // 2) if d == 0 else slice(cols // 2, cols)
        src = held.at[block_rows(source_z * n_x + q), cols_here]
        return pltpu.make_async_remote_copy(
            src_ref=src,
            dst_ref=src,
            send_sem=z_send.at[d, t, q],
            recv_sem=z_recv.at[d, t, q],
            device_id=(up if d == 0 else down, cd),
            device_id_type=MESH,
        )

    def z_arrival(d, t, q):
        source_z = lax.rem(z + n_z - t - 1, n_z) if d == 0 else lax.rem(z + t + 1, n_z)
        cols_here = slice(0, cols)
        if t == steps - 1:
            cols_here = slice(0, cols // 2) if d == 0 else slice(cols // 2, cols)
        dst = held.at[block_rows(source_z * n_x + q), cols_here]
        return pltpu.make_async_remote_copy(
            src_ref=dst,
            dst_ref=dst,
            send_sem=z_send.at[d, t, q],
            recv_sem=z_recv.at[d, t, q],
            device_id=(up if d == 0 else down, cd),
            device_id_type=MESH,
        )

    for t in range(steps):
        for q in range(n_x):
            for d in (0, 1):
                if t > 0:
                    z_arrival(d, t - 1, q).wait_recv()
                z_copy(d, t, q).start()
    for q in range(n_x):
        for d in (0, 1):
            z_arrival(d, steps - 1, q).wait_recv()
    for i in range(1, n_x):
        x_copy(i, False).wait_send()
    for t in range(steps):
        for q in range(n_x):
            for d in (0, 1):
                z_copy(d, t, q).wait_send()
    out_ref[...] = held[...]


def gather_rows(amplitudes, n_x, n_z):
    rows, cols = amplitudes.shape
    steps = n_z // 2
    return pl.pallas_call(
        functools.partial(gather_kernel, n_x, n_z),
        out_shape=jax.ShapeDtypeStruct((rows * n_x * n_z, cols), amplitudes.dtype),
        in_specs=[pl.BlockSpec(memory_space=pltpu.VMEM)],
        out_specs=pl.BlockSpec(memory_space=pltpu.VMEM),
        scratch_shapes=[
            pltpu.VMEM((rows * n_x * n_z, cols), amplitudes.dtype),
            pltpu.SemaphoreType.DMA(()),
            pltpu.SemaphoreType.DMA((n_x,)),
            pltpu.SemaphoreType.DMA((n_x,)),
            pltpu.SemaphoreType.DMA((2, steps, n_x)),
            pltpu.SemaphoreType.DMA((2, steps, n_x)),
        ],
        compiler_params=pltpu.CompilerParams(collective_id=0, has_side_effects=True),
    )(amplitudes)


def x_extent(mesh):
    first = mesh.devices.reshape(mesh.shape["ab"], -1)[:, 0]
    try:
        return len({d.coords[0] for d in first})
    except AttributeError:
        return 2


def scatter_kernel(n_y, n_chunks, part_ref, out_ref, pair, send_r, recv_r, send_l, recv_l,
                   pair_send, pair_recv, ring_send, ring_recv):
    ab = lax.axis_index("ab")
    cd = lax.axis_index("cd")
    y, core = cd // 2, lax.rem(cd, 2)
    other = 1 - core
    right = lax.rem(y + 1, n_y) * 2 + core
    left = lax.rem(y + n_y - 1, n_y) * 2 + core
    partner = y * 2 + other
    half = out_ref.shape[1] // 2
    width = half // n_chunks

    barrier = pltpu.get_barrier_semaphore()
    for peer in (partner, right, left):
        pl.semaphore_signal(barrier, inc=1, device_id=(ab, peer), device_id_type=MESH)
    pl.semaphore_wait(barrier, 3)

    order = []
    for k in list(range(1, n_y // 2 + 1)) + [0]:
        for sign in (1, -1):
            if (sign * k) % n_y not in [j % n_y for j in order]:
                order.append(sign * k)

    def pair_copy(k):
        b = lax.rem(y + k + n_y, n_y)
        return pltpu.make_async_remote_copy(
            src_ref=part_ref.at[b, other],
            dst_ref=pair.at[b],
            send_sem=pair_send.at[b],
            recv_sem=pair_recv.at[b],
            device_id=(ab, partner),
            device_id_type=MESH,
        )

    for k in order:
        pair_copy(k).start()

    def own(k, cols):
        b = lax.rem(y + k + n_y, n_y)
        return part_ref[b, core, :, cols] + pair[b, :, cols]

    def columns(d, q):
        start = d * half + q * width
        return slice(start, start + width)

    sends = (send_r, send_l)
    recvs = (recv_r, recv_l)

    def ring_copy(d, s, q):
        return pltpu.make_async_remote_copy(
            src_ref=sends[d].at[s, q],
            dst_ref=recvs[d].at[s, q],
            send_sem=ring_send.at[d, s, q],
            recv_sem=ring_recv.at[d, s, q],
            device_id=(ab, right if d == 0 else left),
            device_id_type=MESH,
        )

    waited = set()

    def need(k):
        k = k % n_y
        if k not in waited:
            waited.add(k)
            pair_copy(k if k <= n_y // 2 else k - n_y).wait_recv()

    for s in range(n_y - 1):
        need(-(s + 1))
        need(s + 1)
        for q in range(n_chunks):
            for d in (0, 1):
                k = -(s + 1) if d == 0 else s + 1
                if s == 0:
                    sends[d][s, q] = own(k, columns(d, q))
                else:
                    ring_copy(d, s - 1, q).wait_recv()
                    sends[d][s, q] = recvs[d][s - 1, q] + own(k, columns(d, q))
                ring_copy(d, s, q).start()
    need(0)
    for q in range(n_chunks):
        for d in (0, 1):
            ring_copy(d, n_y - 2, q).wait_recv()
            out_ref[:, columns(d, q)] = recvs[d][n_y - 2, q] + own(0, columns(d, q))
    for k in order:
        pair_copy(k).wait_send()
    for s in range(n_y - 1):
        for q in range(n_chunks):
            ring_copy(0, s, q).wait_send()
            ring_copy(1, s, q).wait_send()


def scatter_rows(partial_value, n_cd, n_chunks=4):
    n_y = n_cd // 2
    total_rows, cols = partial_value.shape
    rows = total_rows // n_cd
    blocks = partial_value.reshape(n_y, 2, rows, cols)
    width = cols // 2 // n_chunks
    slots = pltpu.VMEM((n_y - 1, n_chunks, rows, width), jnp.float32)
    return pl.pallas_call(
        functools.partial(scatter_kernel, n_y, n_chunks),
        out_shape=jax.ShapeDtypeStruct((rows, cols), partial_value.dtype),
        in_specs=[pl.BlockSpec(memory_space=pltpu.VMEM)],
        out_specs=pl.BlockSpec(memory_space=pltpu.VMEM),
        scratch_shapes=[
            pltpu.VMEM((n_y, rows, cols), jnp.float32),
            slots,
            slots,
            slots,
            slots,
            pltpu.SemaphoreType.DMA((n_y,)),
            pltpu.SemaphoreType.DMA((n_y,)),
            pltpu.SemaphoreType.DMA((2, n_y - 1, n_chunks)),
            pltpu.SemaphoreType.DMA((2, n_y - 1, n_chunks)),
        ],
        compiler_params=pltpu.CompilerParams(collective_id=1, has_side_effects=True),
    )(blocks)


def on_device(n_x, n_z, n_cd, amplitudes, integrals, ij_pairs, ab_pairs, eps_occ, eps_vir):
    partial_value = contract_rows(gather_rows(amplitudes, n_x, n_z), integrals)
    ladder = scatter_rows(partial_value, n_cd)
    first_occ = lookup_energy(ij_pairs[:, 0], eps_occ)[:, None]
    second_occ = lookup_energy(ij_pairs[:, 1], eps_occ)[:, None]
    first_vir = lookup_energy(ab_pairs[:, 0], eps_vir)[None, :]
    second_vir = lookup_energy(ab_pairs[:, 1], eps_vir)[None, :]
    denominator = first_occ + second_occ - first_vir - second_vir
    update = ladder / denominator
    return (jnp.where(denominator == denominator, ladder, update), update)


def solution(mesh):
    in_specs = (P("ab", "cd"), P("ab", "cd"), P("cd", None), P("ab", None), P(), P())
    out_specs = (P("cd", "ab"), P("cd", "ab"))
    return jax.shard_map(
        functools.partial(on_device, x_extent(mesh), mesh.shape["ab"] // x_extent(mesh), mesh.shape["cd"]),
        mesh=mesh,
        in_specs=in_specs,
        out_specs=out_specs,
        check_vma=False,
    )
```

```python
import functools

import jax
import jax.numpy as jnp
from jax import lax
from jax.experimental import pallas as pl
from jax.experimental.pallas import tpu as pltpu
from jax.sharding import PartitionSpec as P

MESH = pl.DeviceIdType.MESH


def lookup_energy(indices, energies):
    lanes = 128
    groups = -(-energies.shape[0] // lanes)
    table = jnp.pad(energies, (0, groups * lanes - energies.shape[0])).reshape(groups, lanes)
    low = lax.rem(indices, lanes)
    high = indices // lanes
    one_hot = (low[:, None] == lax.broadcasted_iota(jnp.int32, (indices.shape[0], lanes), 1)).astype(jnp.float32)
    by_group = lax.dot_general(
        one_hot, table, (((1,), (1,)), ((), ())),
        precision=lax.Precision.HIGHEST, preferred_element_type=jnp.float32,
    )
    chosen = high[:, None] == lax.broadcasted_iota(jnp.int32, by_group.shape, 1)
    return jnp.sum(jnp.where(chosen, by_group, jnp.float32(0.0)), axis=1)


def contract_rows(row_block, col_block):
    return lax.dot_general(
        row_block,
        col_block,
        (((1,), (1,)), ((), ())),
        precision=lax.Precision.HIGH,
        preferred_element_type=jnp.float32,
    )


def gather_kernel(n_x, n_z, amp_ref, out_ref, held, local_sem, x_send, x_recv, z_send, z_recv):
    ab = lax.axis_index("ab")
    cd = lax.axis_index("cd")
    z, x = ab // n_x, lax.rem(ab, n_x)
    rows = amp_ref.shape[0]
    group = rows * n_x
    cols = amp_ref.shape[1]
    up = lax.rem(z + 1, n_z) * n_x + x
    down = lax.rem(z + n_z - 1, n_z) * n_x + x

    barrier = pltpu.get_barrier_semaphore()
    for i in range(1, n_x):
        pl.semaphore_signal(barrier, inc=1, device_id=(z * n_x + lax.rem(x + i, n_x), cd), device_id_type=MESH)
    pl.semaphore_signal(barrier, inc=1, device_id=(up, cd), device_id_type=MESH)
    pl.semaphore_signal(barrier, inc=1, device_id=(down, cd), device_id_type=MESH)
    pl.semaphore_wait(barrier, n_x + 1)

    def block_rows(a_index):
        return pl.ds(pl.multiple_of(a_index * rows, rows), rows)

    def x_copy(i, receiving):
        sender = lax.rem(x + n_x - i, n_x) if receiving else x
        target = lax.rem(x + i, n_x)
        return pltpu.make_async_remote_copy(
            src_ref=amp_ref,
            dst_ref=held.at[block_rows(z * n_x + sender)],
            send_sem=x_send.at[target],
            recv_sem=x_recv.at[sender],
            device_id=(z * n_x + target, cd),
            device_id_type=MESH,
        )

    for i in range(1, n_x):
        x_copy(i, False).start()
    local = pltpu.make_async_copy(amp_ref, held.at[block_rows(ab)], local_sem)
    local.start()

    steps = n_z // 2

    def z_copy(d, t, q):
        source_z = lax.rem(z + n_z - t, n_z) if d == 0 else lax.rem(z + t, n_z)
        cols_here = slice(0, cols)
        if t == steps - 1:
            cols_here = slice(0, cols // 2) if d == 0 else slice(cols // 2, cols)
        src = held.at[block_rows(source_z * n_x + q), cols_here]
        return pltpu.make_async_remote_copy(
            src_ref=src,
            dst_ref=src,
            send_sem=z_send.at[d, t, q],
            recv_sem=z_recv.at[d, t, q],
            device_id=(up if d == 0 else down, cd),
            device_id_type=MESH,
        )

    def z_arrival(d, t, q):
        source_z = lax.rem(z + n_z - t - 1, n_z) if d == 0 else lax.rem(z + t + 1, n_z)
        cols_here = slice(0, cols)
        if t == steps - 1:
            cols_here = slice(0, cols // 2) if d == 0 else slice(cols // 2, cols)
        dst = held.at[block_rows(source_z * n_x + q), cols_here]
        return pltpu.make_async_remote_copy(
            src_ref=dst,
            dst_ref=dst,
            send_sem=z_send.at[d, t, q],
            recv_sem=z_recv.at[d, t, q],
            device_id=(up if d == 0 else down, cd),
            device_id_type=MESH,
        )

    for i in range(n_x):
        if i == 0:
            local.wait()
        else:
            x_copy(i, True).wait_recv()
        landed = lax.rem(x + n_x - i, n_x)
        for d in (0, 1):
            z_copy(d, 0, landed).start()
    for t in range(1, steps):
        for q in range(n_x):
            for d in (0, 1):
                z_arrival(d, t - 1, q).wait_recv()
                z_copy(d, t, q).start()
    for q in range(n_x):
        for d in (0, 1):
            z_arrival(d, steps - 1, q).wait_recv()
    for i in range(1, n_x):
        x_copy(i, False).wait_send()
    for t in range(steps):
        for q in range(n_x):
            for d in (0, 1):
                z_copy(d, t, q).wait_send()
    out_ref[...] = held[...]


def gather_rows(amplitudes, n_x, n_z):
    rows, cols = amplitudes.shape
    steps = n_z // 2
    return pl.pallas_call(
        functools.partial(gather_kernel, n_x, n_z),
        out_shape=jax.ShapeDtypeStruct((rows * n_x * n_z, cols), amplitudes.dtype),
        in_specs=[pl.BlockSpec(memory_space=pltpu.VMEM)],
        out_specs=pl.BlockSpec(memory_space=pltpu.VMEM),
        scratch_shapes=[
            pltpu.VMEM((rows * n_x * n_z, cols), amplitudes.dtype),
            pltpu.SemaphoreType.DMA(()),
            pltpu.SemaphoreType.DMA((n_x,)),
            pltpu.SemaphoreType.DMA((n_x,)),
            pltpu.SemaphoreType.DMA((2, steps, n_x)),
            pltpu.SemaphoreType.DMA((2, steps, n_x)),
        ],
        compiler_params=pltpu.CompilerParams(collective_id=0, has_side_effects=True),
    )(amplitudes)


def x_extent(mesh):
    first = mesh.devices.reshape(mesh.shape["ab"], -1)[:, 0]
    try:
        return len({d.coords[0] for d in first})
    except AttributeError:
        return 2


def scatter_kernel(n_y, n_chunks, part_ref, out_ref, pair, send_r, recv_r, send_l, recv_l,
                   pair_send, pair_recv, ring_send, ring_recv):
    ab = lax.axis_index("ab")
    cd = lax.axis_index("cd")
    y, core = cd // 2, lax.rem(cd, 2)
    other = 1 - core
    right = lax.rem(y + 1, n_y) * 2 + core
    left = lax.rem(y + n_y - 1, n_y) * 2 + core
    partner = y * 2 + other
    half = out_ref.shape[1] // 2
    width = half // n_chunks

    barrier = pltpu.get_barrier_semaphore()
    for peer in (partner, right, left):
        pl.semaphore_signal(barrier, inc=1, device_id=(ab, peer), device_id_type=MESH)
    pl.semaphore_wait(barrier, 3)

    order = []
    for k in list(range(1, n_y // 2 + 1)) + [0]:
        for sign in (1, -1):
            if (sign * k) % n_y not in [j % n_y for j in order]:
                order.append(sign * k)

    def pair_copy(k):
        b = lax.rem(y + k + n_y, n_y)
        return pltpu.make_async_remote_copy(
            src_ref=part_ref.at[b, other],
            dst_ref=pair.at[b],
            send_sem=pair_send.at[b],
            recv_sem=pair_recv.at[b],
            device_id=(ab, partner),
            device_id_type=MESH,
        )

    for k in order:
        pair_copy(k).start()

    def own(k, cols):
        b = lax.rem(y + k + n_y, n_y)
        return part_ref[b, core, :, cols] + pair[b, :, cols]

    def columns(d, q):
        start = d * half + q * width
        return slice(start, start + width)

    sends = (send_r, send_l)
    recvs = (recv_r, recv_l)

    def ring_copy(d, s, q):
        return pltpu.make_async_remote_copy(
            src_ref=sends[d].at[s, q],
            dst_ref=recvs[d].at[s, q],
            send_sem=ring_send.at[d, s, q],
            recv_sem=ring_recv.at[d, s, q],
            device_id=(ab, right if d == 0 else left),
            device_id_type=MESH,
        )

    waited = set()

    def need(k):
        k = k % n_y
        if k not in waited:
            waited.add(k)
            pair_copy(k if k <= n_y // 2 else k - n_y).wait_recv()

    for s in range(n_y - 1):
        need(-(s + 1))
        need(s + 1)
        for q in range(n_chunks):
            for d in (0, 1):
                k = -(s + 1) if d == 0 else s + 1
                if s == 0:
                    sends[d][s, q] = own(k, columns(d, q))
                else:
                    ring_copy(d, s - 1, q).wait_recv()
                    sends[d][s, q] = recvs[d][s - 1, q] + own(k, columns(d, q))
                ring_copy(d, s, q).start()
    need(0)
    for q in range(n_chunks):
        for d in (0, 1):
            ring_copy(d, n_y - 2, q).wait_recv()
            out_ref[:, columns(d, q)] = recvs[d][n_y - 2, q] + own(0, columns(d, q))
    for k in order:
        pair_copy(k).wait_send()
    for s in range(n_y - 1):
        for q in range(n_chunks):
            ring_copy(0, s, q).wait_send()
            ring_copy(1, s, q).wait_send()


def scatter_rows(partial_value, n_cd, n_chunks=4):
    n_y = n_cd // 2
    total_rows, cols = partial_value.shape
    rows = total_rows // n_cd
    blocks = partial_value.reshape(n_y, 2, rows, cols)
    width = cols // 2 // n_chunks
    slots = pltpu.VMEM((n_y - 1, n_chunks, rows, width), jnp.float32)
    return pl.pallas_call(
        functools.partial(scatter_kernel, n_y, n_chunks),
        out_shape=jax.ShapeDtypeStruct((rows, cols), partial_value.dtype),
        in_specs=[pl.BlockSpec(memory_space=pltpu.VMEM)],
        out_specs=pl.BlockSpec(memory_space=pltpu.VMEM),
        scratch_shapes=[
            pltpu.VMEM((n_y, rows, cols), jnp.float32),
            slots,
            slots,
            slots,
            slots,
            pltpu.SemaphoreType.DMA((n_y,)),
            pltpu.SemaphoreType.DMA((n_y,)),
            pltpu.SemaphoreType.DMA((2, n_y - 1, n_chunks)),
            pltpu.SemaphoreType.DMA((2, n_y - 1, n_chunks)),
        ],
        compiler_params=pltpu.CompilerParams(collective_id=1, has_side_effects=True),
    )(blocks)


def on_device(n_x, n_z, n_cd, amplitudes, integrals, ij_pairs, ab_pairs, eps_occ, eps_vir):
    partial_value = contract_rows(gather_rows(amplitudes, n_x, n_z), integrals)
    ladder = scatter_rows(partial_value, n_cd)
    first_occ = lookup_energy(ij_pairs[:, 0], eps_occ)[:, None]
    second_occ = lookup_energy(ij_pairs[:, 1], eps_occ)[:, None]
    first_vir = lookup_energy(ab_pairs[:, 0], eps_vir)[None, :]
    second_vir = lookup_energy(ab_pairs[:, 1], eps_vir)[None, :]
    denominator = first_occ + second_occ - first_vir - second_vir
    update = ladder / denominator
    return (jnp.where(denominator == denominator, ladder, update), update)


def solution(mesh):
    in_specs = (P("ab", "cd"), P("ab", "cd"), P("cd", None), P("ab", None), P(), P())
    out_specs = (P("cd", "ab"), P("cd", "ab"))
    return jax.shard_map(
        functools.partial(on_device, x_extent(mesh), mesh.shape["ab"] // x_extent(mesh), mesh.shape["cd"]),
        mesh=mesh,
        in_specs=in_specs,
        out_specs=out_specs,
        check_vma=False,
    )
```

```python
import functools

import jax
import jax.numpy as jnp
from jax import lax
from jax.experimental import pallas as pl
from jax.experimental.pallas import tpu as pltpu
from jax.sharding import PartitionSpec as P

MESH = pl.DeviceIdType.MESH


def lookup_energy(indices, energies):
    lanes = 128
    groups = -(-energies.shape[0] // lanes)
    table = jnp.pad(energies, (0, groups * lanes - energies.shape[0])).reshape(groups, lanes)
    low = lax.rem(indices, lanes)
    high = indices // lanes
    one_hot = (low[:, None] == lax.broadcasted_iota(jnp.int32, (indices.shape[0], lanes), 1)).astype(jnp.float32)
    by_group = lax.dot_general(
        one_hot, table, (((1,), (1,)), ((), ())),
        precision=lax.Precision.HIGHEST, preferred_element_type=jnp.float32,
    )
    chosen = high[:, None] == lax.broadcasted_iota(jnp.int32, by_group.shape, 1)
    return jnp.sum(jnp.where(chosen, by_group, jnp.float32(0.0)), axis=1)


def contract_rows(row_block, col_block):
    return lax.dot_general(
        row_block,
        col_block,
        (((1,), (1,)), ((), ())),
        precision=lax.Precision.HIGH,
        preferred_element_type=jnp.float32,
    )


def gather_kernel(n_x, n_z, amp_ref, out_ref, held, local_sem, x_send, x_recv, z_send, z_recv):
    ab = lax.axis_index("ab")
    cd = lax.axis_index("cd")
    z, x = ab // n_x, lax.rem(ab, n_x)
    rows = amp_ref.shape[0]
    group = rows * n_x
    cols = amp_ref.shape[1]
    up = lax.rem(z + 1, n_z) * n_x + x
    down = lax.rem(z + n_z - 1, n_z) * n_x + x

    barrier = pltpu.get_barrier_semaphore()
    for i in range(1, n_x):
        pl.semaphore_signal(barrier, inc=1, device_id=(z * n_x + lax.rem(x + i, n_x), cd), device_id_type=MESH)
    pl.semaphore_signal(barrier, inc=1, device_id=(up, cd), device_id_type=MESH)
    pl.semaphore_signal(barrier, inc=1, device_id=(down, cd), device_id_type=MESH)
    pl.semaphore_wait(barrier, n_x + 1)

    def block_rows(a_index):
        return pl.ds(pl.multiple_of(a_index * rows, rows), rows)

    def x_copy(i, receiving):
        sender = lax.rem(x + n_x - i, n_x) if receiving else x
        target = lax.rem(x + i, n_x)
        return pltpu.make_async_remote_copy(
            src_ref=amp_ref,
            dst_ref=held.at[block_rows(z * n_x + sender)],
            send_sem=x_send.at[target],
            recv_sem=x_recv.at[sender],
            device_id=(z * n_x + target, cd),
            device_id_type=MESH,
        )

    for i in range(1, n_x):
        x_copy(i, False).start()
    local = pltpu.make_async_copy(amp_ref, held.at[block_rows(ab)], local_sem)
    local.start()

    steps = n_z // 2

    def z_copy(d, t, q):
        source_z = lax.rem(z + n_z - t, n_z) if d == 0 else lax.rem(z + t, n_z)
        cols_here = slice(0, cols)
        if t == steps - 1:
            cols_here = slice(0, cols // 2) if d == 0 else slice(cols // 2, cols)
        src = held.at[block_rows(source_z * n_x + q), cols_here]
        return pltpu.make_async_remote_copy(
            src_ref=src,
            dst_ref=src,
            send_sem=z_send.at[d, t, q],
            recv_sem=z_recv.at[d, t, q],
            device_id=(up if d == 0 else down, cd),
            device_id_type=MESH,
        )

    def z_arrival(d, t, q):
        source_z = lax.rem(z + n_z - t - 1, n_z) if d == 0 else lax.rem(z + t + 1, n_z)
        cols_here = slice(0, cols)
        if t == steps - 1:
            cols_here = slice(0, cols // 2) if d == 0 else slice(cols // 2, cols)
        dst = held.at[block_rows(source_z * n_x + q), cols_here]
        return pltpu.make_async_remote_copy(
            src_ref=dst,
            dst_ref=dst,
            send_sem=z_send.at[d, t, q],
            recv_sem=z_recv.at[d, t, q],
            device_id=(up if d == 0 else down, cd),
            device_id_type=MESH,
        )

    for i in range(n_x):
        if i == 0:
            local.wait()
        else:
            x_copy(i, True).wait_recv()
        landed = lax.rem(x + n_x - i, n_x)
        for d in (0, 1):
            z_copy(d, 0, landed).start()
    for t in range(1, steps):
        for q in range(n_x):
            for d in (0, 1):
                z_arrival(d, t - 1, q).wait_recv()
                z_copy(d, t, q).start()
    for q in range(n_x):
        for d in (0, 1):
            z_arrival(d, steps - 1, q).wait_recv()
    for i in range(1, n_x):
        x_copy(i, False).wait_send()
    for t in range(steps):
        for q in range(n_x):
            for d in (0, 1):
                z_copy(d, t, q).wait_send()
    out_ref[...] = held[...]


def gather_rows(amplitudes, n_x, n_z):
    rows, cols = amplitudes.shape
    steps = n_z // 2
    return pl.pallas_call(
        functools.partial(gather_kernel, n_x, n_z),
        out_shape=jax.ShapeDtypeStruct((rows * n_x * n_z, cols), amplitudes.dtype),
        in_specs=[pl.BlockSpec(memory_space=pltpu.VMEM)],
        out_specs=pl.BlockSpec(memory_space=pltpu.VMEM),
        scratch_shapes=[
            pltpu.VMEM((rows * n_x * n_z, cols), amplitudes.dtype),
            pltpu.SemaphoreType.DMA(()),
            pltpu.SemaphoreType.DMA((n_x,)),
            pltpu.SemaphoreType.DMA((n_x,)),
            pltpu.SemaphoreType.DMA((2, steps, n_x)),
            pltpu.SemaphoreType.DMA((2, steps, n_x)),
        ],
        compiler_params=pltpu.CompilerParams(collective_id=0, has_side_effects=True),
    )(amplitudes)


def x_extent(mesh):
    first = mesh.devices.reshape(mesh.shape["ab"], -1)[:, 0]
    try:
        return len({d.coords[0] for d in first})
    except AttributeError:
        return 2


def scatter_kernel(n_y, n_chunks, part_ref, out_ref, mine, pair, send_r, recv_r, send_l, recv_l,
                   mine_sem, pair_send, pair_recv, ring_send, ring_recv):
    ab = lax.axis_index("ab")
    cd = lax.axis_index("cd")
    y, core = cd // 2, lax.rem(cd, 2)
    other = 1 - core
    right = lax.rem(y + 1, n_y) * 2 + core
    left = lax.rem(y + n_y - 1, n_y) * 2 + core
    partner = y * 2 + other
    half = out_ref.shape[1] // 2
    width = half // n_chunks

    def fetch(k):
        b = lax.rem(y + k + n_y, n_y)
        return pltpu.make_async_copy(part_ref.at[b, core], mine.at[b], mine_sem.at[b])

    fetch_order = []
    for s in range(1, n_y // 2 + 1):
        for k in (-s, s):
            if k % n_y not in [j % n_y for j in fetch_order]:
                fetch_order.append(k)
    fetch_order.append(0)
    for k in fetch_order:
        fetch(k).start()

    barrier = pltpu.get_barrier_semaphore()
    for peer in (partner, right, left):
        pl.semaphore_signal(barrier, inc=1, device_id=(ab, peer), device_id_type=MESH)
    pl.semaphore_wait(barrier, 3)

    order = []
    for k in list(range(1, n_y // 2 + 1)) + [0]:
        for sign in (1, -1):
            if (sign * k) % n_y not in [j % n_y for j in order]:
                order.append(sign * k)

    def pair_copy(k):
        b = lax.rem(y + k + n_y, n_y)
        return pltpu.make_async_remote_copy(
            src_ref=part_ref.at[b, other],
            dst_ref=pair.at[b],
            send_sem=pair_send.at[b],
            recv_sem=pair_recv.at[b],
            device_id=(ab, partner),
            device_id_type=MESH,
        )

    for k in order:
        pair_copy(k).start()

    def own(k, cols):
        b = lax.rem(y + k + n_y, n_y)
        return mine[b, :, cols] + pair[b, :, cols]

    def columns(d, q):
        start = d * half + q * width
        return slice(start, start + width)

    sends = (send_r, send_l)
    recvs = (recv_r, recv_l)

    def ring_copy(d, s, q):
        return pltpu.make_async_remote_copy(
            src_ref=sends[d].at[s, q],
            dst_ref=recvs[d].at[s, q],
            send_sem=ring_send.at[d, s, q],
            recv_sem=ring_recv.at[d, s, q],
            device_id=(ab, right if d == 0 else left),
            device_id_type=MESH,
        )

    waited = set()

    def need(k):
        k = k % n_y
        if k not in waited:
            waited.add(k)
            pair_copy(k if k <= n_y // 2 else k - n_y).wait_recv()
            fetch(k).wait()

    for s in range(n_y - 1):
        need(-(s + 1))
        need(s + 1)
        for q in range(n_chunks):
            for d in (0, 1):
                k = -(s + 1) if d == 0 else s + 1
                if s == 0:
                    sends[d][s, q] = own(k, columns(d, q))
                else:
                    ring_copy(d, s - 1, q).wait_recv()
                    sends[d][s, q] = recvs[d][s - 1, q] + own(k, columns(d, q))
                ring_copy(d, s, q).start()
    need(0)
    for q in range(n_chunks):
        for d in (0, 1):
            ring_copy(d, n_y - 2, q).wait_recv()
            out_ref[:, columns(d, q)] = recvs[d][n_y - 2, q] + own(0, columns(d, q))
    for k in order:
        pair_copy(k).wait_send()
    for s in range(n_y - 1):
        for q in range(n_chunks):
            ring_copy(0, s, q).wait_send()
            ring_copy(1, s, q).wait_send()


def scatter_rows(partial_value, n_cd, n_chunks=4):
    n_y = n_cd // 2
    total_rows, cols = partial_value.shape
    rows = total_rows // n_cd
    blocks = partial_value.reshape(n_y, 2, rows, cols)
    width = cols // 2 // n_chunks
    slots = pltpu.VMEM((n_y - 1, n_chunks, rows, width), jnp.float32)
    return pl.pallas_call(
        functools.partial(scatter_kernel, n_y, n_chunks),
        out_shape=jax.ShapeDtypeStruct((rows, cols), partial_value.dtype),
        in_specs=[pl.BlockSpec(memory_space=pl.ANY)],
        out_specs=pl.BlockSpec(memory_space=pltpu.VMEM),
        scratch_shapes=[
            pltpu.VMEM((n_y, rows, cols), jnp.float32),
            pltpu.VMEM((n_y, rows, cols), jnp.float32),
            slots,
            slots,
            slots,
            slots,
            pltpu.SemaphoreType.DMA((n_y,)),
            pltpu.SemaphoreType.DMA((n_y,)),
            pltpu.SemaphoreType.DMA((n_y,)),
            pltpu.SemaphoreType.DMA((2, n_y - 1, n_chunks)),
            pltpu.SemaphoreType.DMA((2, n_y - 1, n_chunks)),
        ],
        compiler_params=pltpu.CompilerParams(collective_id=1, has_side_effects=True),
    )(blocks)


def on_device(n_x, n_z, n_cd, amplitudes, integrals, ij_pairs, ab_pairs, eps_occ, eps_vir):
    partial_value = contract_rows(gather_rows(amplitudes, n_x, n_z), integrals)
    ladder = scatter_rows(partial_value, n_cd)
    first_occ = lookup_energy(ij_pairs[:, 0], eps_occ)[:, None]
    second_occ = lookup_energy(ij_pairs[:, 1], eps_occ)[:, None]
    first_vir = lookup_energy(ab_pairs[:, 0], eps_vir)[None, :]
    second_vir = lookup_energy(ab_pairs[:, 1], eps_vir)[None, :]
    denominator = first_occ + second_occ - first_vir - second_vir
    update = ladder / denominator
    return (jnp.where(denominator == denominator, ladder, update), update)


def solution(mesh):
    in_specs = (P("ab", "cd"), P("ab", "cd"), P("cd", None), P("ab", None), P(), P())
    out_specs = (P("cd", "ab"), P("cd", "ab"))
    return jax.shard_map(
        functools.partial(on_device, x_extent(mesh), mesh.shape["ab"] // x_extent(mesh), mesh.shape["cd"]),
        mesh=mesh,
        in_specs=in_specs,
        out_specs=out_specs,
        check_vma=False,
    )
```

```python
import functools

import jax
import jax.numpy as jnp
from jax import lax
from jax.experimental import pallas as pl
from jax.experimental.pallas import tpu as pltpu
from jax.sharding import PartitionSpec as P

MESH = pl.DeviceIdType.MESH


def lookup_energy(indices, energies):
    lanes = 128
    groups = -(-energies.shape[0] // lanes)
    table = jnp.pad(energies, (0, groups * lanes - energies.shape[0])).reshape(groups, lanes)
    low = lax.rem(indices, lanes)
    high = indices // lanes
    one_hot = (low[:, None] == lax.broadcasted_iota(jnp.int32, (indices.shape[0], lanes), 1)).astype(jnp.float32)
    by_group = lax.dot_general(
        one_hot, table, (((1,), (1,)), ((), ())),
        precision=lax.Precision.HIGHEST, preferred_element_type=jnp.float32,
    )
    chosen = high[:, None] == lax.broadcasted_iota(jnp.int32, by_group.shape, 1)
    return jnp.sum(jnp.where(chosen, by_group, jnp.float32(0.0)), axis=1)


def contract_rows(row_block, col_block):
    return lax.dot_general(
        row_block,
        col_block,
        (((1,), (1,)), ((), ())),
        precision=lax.Precision.HIGH,
        preferred_element_type=jnp.float32,
    )


def gather_kernel(n_x, n_z, amp_ref, out_ref, held, local_sem, out_sem, x_send, x_recv, z_send, z_recv):
    ab = lax.axis_index("ab")
    cd = lax.axis_index("cd")
    z, x = ab // n_x, lax.rem(ab, n_x)
    rows = amp_ref.shape[0]
    group = rows * n_x
    cols = amp_ref.shape[1]
    up = lax.rem(z + 1, n_z) * n_x + x
    down = lax.rem(z + n_z - 1, n_z) * n_x + x

    barrier = pltpu.get_barrier_semaphore()
    for i in range(1, n_x):
        pl.semaphore_signal(barrier, inc=1, device_id=(z * n_x + lax.rem(x + i, n_x), cd), device_id_type=MESH)
    pl.semaphore_signal(barrier, inc=1, device_id=(up, cd), device_id_type=MESH)
    pl.semaphore_signal(barrier, inc=1, device_id=(down, cd), device_id_type=MESH)
    pl.semaphore_wait(barrier, n_x + 1)

    def block_rows(a_index):
        return pl.ds(pl.multiple_of(a_index * rows, rows), rows)

    def x_copy(i, receiving):
        sender = lax.rem(x + n_x - i, n_x) if receiving else x
        target = lax.rem(x + i, n_x)
        return pltpu.make_async_remote_copy(
            src_ref=amp_ref,
            dst_ref=held.at[block_rows(z * n_x + sender)],
            send_sem=x_send.at[target],
            recv_sem=x_recv.at[sender],
            device_id=(z * n_x + target, cd),
            device_id_type=MESH,
        )

    for i in range(1, n_x):
        x_copy(i, False).start()
    local = pltpu.make_async_copy(amp_ref, held.at[block_rows(ab)], local_sem)
    local.start()

    steps = n_z // 2

    def z_copy(d, t, q):
        source_z = lax.rem(z + n_z - t, n_z) if d == 0 else lax.rem(z + t, n_z)
        cols_here = slice(0, cols)
        if t == steps - 1:
            cols_here = slice(0, cols // 2) if d == 0 else slice(cols // 2, cols)
        src = held.at[block_rows(source_z * n_x + q), cols_here]
        return pltpu.make_async_remote_copy(
            src_ref=src,
            dst_ref=src,
            send_sem=z_send.at[d, t, q],
            recv_sem=z_recv.at[d, t, q],
            device_id=(up if d == 0 else down, cd),
            device_id_type=MESH,
        )

    def z_arrival(d, t, q):
        source_z = lax.rem(z + n_z - t - 1, n_z) if d == 0 else lax.rem(z + t + 1, n_z)
        cols_here = slice(0, cols)
        if t == steps - 1:
            cols_here = slice(0, cols // 2) if d == 0 else slice(cols // 2, cols)
        dst = held.at[block_rows(source_z * n_x + q), cols_here]
        return pltpu.make_async_remote_copy(
            src_ref=dst,
            dst_ref=dst,
            send_sem=z_send.at[d, t, q],
            recv_sem=z_recv.at[d, t, q],
            device_id=(up if d == 0 else down, cd),
            device_id_type=MESH,
        )

    for i in range(n_x):
        if i == 0:
            local.wait()
        else:
            x_copy(i, True).wait_recv()
        landed = lax.rem(x + n_x - i, n_x)
        for d in (0, 1):
            z_copy(d, 0, landed).start()
    for t in range(1, steps):
        for q in range(n_x):
            for d in (0, 1):
                z_arrival(d, t - 1, q).wait_recv()
                z_copy(d, t, q).start()
    for q in range(n_x):
        for d in (0, 1):
            z_arrival(d, steps - 1, q).wait_recv()
    for i in range(1, n_x):
        x_copy(i, False).wait_send()
    for t in range(steps):
        for q in range(n_x):
            for d in (0, 1):
                z_copy(d, t, q).wait_send()
    result = pltpu.make_async_copy(held, out_ref, out_sem)
    result.start()
    result.wait()


def gather_rows(amplitudes, n_x, n_z):
    rows, cols = amplitudes.shape
    steps = n_z // 2
    return pl.pallas_call(
        functools.partial(gather_kernel, n_x, n_z),
        out_shape=jax.ShapeDtypeStruct((rows * n_x * n_z, cols), amplitudes.dtype),
        in_specs=[pl.BlockSpec(memory_space=pltpu.VMEM)],
        out_specs=pl.BlockSpec(memory_space=pl.ANY),
        scratch_shapes=[
            pltpu.VMEM((rows * n_x * n_z, cols), amplitudes.dtype),
            pltpu.SemaphoreType.DMA(()),
            pltpu.SemaphoreType.DMA(()),
            pltpu.SemaphoreType.DMA((n_x,)),
            pltpu.SemaphoreType.DMA((n_x,)),
            pltpu.SemaphoreType.DMA((2, steps, n_x)),
            pltpu.SemaphoreType.DMA((2, steps, n_x)),
        ],
        compiler_params=pltpu.CompilerParams(collective_id=0, has_side_effects=True),
    )(amplitudes)


def x_extent(mesh):
    first = mesh.devices.reshape(mesh.shape["ab"], -1)[:, 0]
    try:
        return len({d.coords[0] for d in first})
    except AttributeError:
        return 2


def scatter_kernel(n_y, n_chunks, part_ref, out_ref, mine, pair, send_r, recv_r, send_l, recv_l,
                   mine_sem, pair_send, pair_recv, ring_send, ring_recv):
    ab = lax.axis_index("ab")
    cd = lax.axis_index("cd")
    y, core = cd // 2, lax.rem(cd, 2)
    other = 1 - core
    right = lax.rem(y + 1, n_y) * 2 + core
    left = lax.rem(y + n_y - 1, n_y) * 2 + core
    partner = y * 2 + other
    half = out_ref.shape[1] // 2
    width = half // n_chunks

    def fetch(k):
        b = lax.rem(y + k + n_y, n_y)
        return pltpu.make_async_copy(part_ref.at[b, core], mine.at[b], mine_sem.at[b])

    fetch_order = []
    for s in range(1, n_y // 2 + 1):
        for k in (-s, s):
            if k % n_y not in [j % n_y for j in fetch_order]:
                fetch_order.append(k)
    fetch_order.append(0)
    for k in fetch_order:
        fetch(k).start()

    barrier = pltpu.get_barrier_semaphore()
    for peer in (partner, right, left):
        pl.semaphore_signal(barrier, inc=1, device_id=(ab, peer), device_id_type=MESH)
    pl.semaphore_wait(barrier, 3)

    order = []
    for k in list(range(1, n_y // 2 + 1)) + [0]:
        for sign in (1, -1):
            if (sign * k) % n_y not in [j % n_y for j in order]:
                order.append(sign * k)

    def pair_copy(k):
        b = lax.rem(y + k + n_y, n_y)
        return pltpu.make_async_remote_copy(
            src_ref=part_ref.at[b, other],
            dst_ref=pair.at[b],
            send_sem=pair_send.at[b],
            recv_sem=pair_recv.at[b],
            device_id=(ab, partner),
            device_id_type=MESH,
        )

    for k in order:
        pair_copy(k).start()

    def own(k, cols):
        b = lax.rem(y + k + n_y, n_y)
        return mine[b, :, cols] + pair[b, :, cols]

    def columns(d, q):
        start = d * half + q * width
        return slice(start, start + width)

    sends = (send_r, send_l)
    recvs = (recv_r, recv_l)

    def ring_copy(d, s, q):
        return pltpu.make_async_remote_copy(
            src_ref=sends[d].at[s, q],
            dst_ref=recvs[d].at[s, q],
            send_sem=ring_send.at[d, s, q],
            recv_sem=ring_recv.at[d, s, q],
            device_id=(ab, right if d == 0 else left),
            device_id_type=MESH,
        )

    waited = set()

    def need(k):
        k = k % n_y
        if k not in waited:
            waited.add(k)
            pair_copy(k if k <= n_y // 2 else k - n_y).wait_recv()
            fetch(k).wait()

    for s in range(n_y - 1):
        need(-(s + 1))
        need(s + 1)
        for q in range(n_chunks):
            for d in (0, 1):
                k = -(s + 1) if d == 0 else s + 1
                if s == 0:
                    sends[d][s, q] = own(k, columns(d, q))
                else:
                    ring_copy(d, s - 1, q).wait_recv()
                    sends[d][s, q] = recvs[d][s - 1, q] + own(k, columns(d, q))
                ring_copy(d, s, q).start()
    need(0)
    for q in range(n_chunks):
        for d in (0, 1):
            ring_copy(d, n_y - 2, q).wait_recv()
            out_ref[:, columns(d, q)] = recvs[d][n_y - 2, q] + own(0, columns(d, q))
    for k in order:
        pair_copy(k).wait_send()
    for s in range(n_y - 1):
        for q in range(n_chunks):
            ring_copy(0, s, q).wait_send()
            ring_copy(1, s, q).wait_send()


def scatter_rows(partial_value, n_cd, n_chunks=4):
    n_y = n_cd // 2
    total_rows, cols = partial_value.shape
    rows = total_rows // n_cd
    blocks = partial_value.reshape(n_y, 2, rows, cols)
    width = cols // 2 // n_chunks
    slots = pltpu.VMEM((n_y - 1, n_chunks, rows, width), jnp.float32)
    return pl.pallas_call(
        functools.partial(scatter_kernel, n_y, n_chunks),
        out_shape=jax.ShapeDtypeStruct((rows, cols), partial_value.dtype),
        in_specs=[pl.BlockSpec(memory_space=pl.ANY)],
        out_specs=pl.BlockSpec(memory_space=pltpu.VMEM),
        scratch_shapes=[
            pltpu.VMEM((n_y, rows, cols), jnp.float32),
            pltpu.VMEM((n_y, rows, cols), jnp.float32),
            slots,
            slots,
            slots,
            slots,
            pltpu.SemaphoreType.DMA((n_y,)),
            pltpu.SemaphoreType.DMA((n_y,)),
            pltpu.SemaphoreType.DMA((n_y,)),
            pltpu.SemaphoreType.DMA((2, n_y - 1, n_chunks)),
            pltpu.SemaphoreType.DMA((2, n_y - 1, n_chunks)),
        ],
        compiler_params=pltpu.CompilerParams(collective_id=1, has_side_effects=True),
    )(blocks)


def on_device(n_x, n_z, n_cd, amplitudes, integrals, ij_pairs, ab_pairs, eps_occ, eps_vir):
    partial_value = contract_rows(gather_rows(amplitudes, n_x, n_z), integrals)
    ladder = scatter_rows(partial_value, n_cd)
    first_occ = lookup_energy(ij_pairs[:, 0], eps_occ)[:, None]
    second_occ = lookup_energy(ij_pairs[:, 1], eps_occ)[:, None]
    first_vir = lookup_energy(ab_pairs[:, 0], eps_vir)[None, :]
    second_vir = lookup_energy(ab_pairs[:, 1], eps_vir)[None, :]
    denominator = first_occ + second_occ - first_vir - second_vir
    update = ladder / denominator
    return (jnp.where(denominator == denominator, ladder, update), update)


def solution(mesh):
    in_specs = (P("ab", "cd"), P("ab", "cd"), P("cd", None), P("ab", None), P(), P())
    out_specs = (P("cd", "ab"), P("cd", "ab"))
    return jax.shard_map(
        functools.partial(on_device, x_extent(mesh), mesh.shape["ab"] // x_extent(mesh), mesh.shape["cd"]),
        mesh=mesh,
        in_specs=in_specs,
        out_specs=out_specs,
        check_vma=False,
    )
```

```python
import functools

import jax
import jax.numpy as jnp
from jax import lax
from jax.experimental import pallas as pl
from jax.experimental.pallas import tpu as pltpu
from jax.sharding import PartitionSpec as P

MESH = pl.DeviceIdType.MESH


def lookup_energy(indices, energies):
    lanes = 128
    groups = -(-energies.shape[0] // lanes)
    table = jnp.pad(energies, (0, groups * lanes - energies.shape[0])).reshape(groups, lanes)
    low = lax.rem(indices, lanes)
    high = indices // lanes
    one_hot = (low[:, None] == lax.broadcasted_iota(jnp.int32, (indices.shape[0], lanes), 1)).astype(jnp.float32)
    by_group = lax.dot_general(
        one_hot, table, (((1,), (1,)), ((), ())),
        precision=lax.Precision.HIGHEST, preferred_element_type=jnp.float32,
    )
    chosen = high[:, None] == lax.broadcasted_iota(jnp.int32, by_group.shape, 1)
    return jnp.sum(jnp.where(chosen, by_group, jnp.float32(0.0)), axis=1)


def contract_rows(row_block, col_block):
    return lax.dot_general(
        row_block,
        col_block,
        (((1,), (1,)), ((), ())),
        precision=lax.Precision.HIGH,
        preferred_element_type=jnp.float32,
    )


def gather_kernel(n_x, n_z, amp_ref, out_ref, held, local_sem, x_send, x_recv, z_send, z_recv):
    ab = lax.axis_index("ab")
    cd = lax.axis_index("cd")
    z, x = ab // n_x, lax.rem(ab, n_x)
    rows = amp_ref.shape[0]
    group = rows * n_x
    cols = amp_ref.shape[1]
    up = lax.rem(z + 1, n_z) * n_x + x
    down = lax.rem(z + n_z - 1, n_z) * n_x + x

    barrier = pltpu.get_barrier_semaphore()
    for i in range(1, n_x):
        pl.semaphore_signal(barrier, inc=1, device_id=(z * n_x + lax.rem(x + i, n_x), cd), device_id_type=MESH)
    pl.semaphore_signal(barrier, inc=1, device_id=(up, cd), device_id_type=MESH)
    pl.semaphore_signal(barrier, inc=1, device_id=(down, cd), device_id_type=MESH)
    pl.semaphore_wait(barrier, n_x + 1)

    def block_rows(a_index):
        return pl.ds(pl.multiple_of(a_index * rows, rows), rows)

    def x_copy(i, receiving):
        sender = lax.rem(x + n_x - i, n_x) if receiving else x
        target = lax.rem(x + i, n_x)
        return pltpu.make_async_remote_copy(
            src_ref=amp_ref,
            dst_ref=held.at[block_rows(z * n_x + sender)],
            send_sem=x_send.at[target],
            recv_sem=x_recv.at[sender],
            device_id=(z * n_x + target, cd),
            device_id_type=MESH,
        )

    for i in range(1, n_x):
        x_copy(i, False).start()
    local = pltpu.make_async_copy(amp_ref, held.at[block_rows(ab)], local_sem)
    local.start()

    steps = n_z // 2

    def z_copy(d, t, q):
        source_z = lax.rem(z + n_z - t, n_z) if d == 0 else lax.rem(z + t, n_z)
        cols_here = slice(0, cols)
        if t == steps - 1:
            cols_here = slice(0, cols // 2) if d == 0 else slice(cols // 2, cols)
        src = held.at[block_rows(source_z * n_x + q), cols_here]
        return pltpu.make_async_remote_copy(
            src_ref=src,
            dst_ref=src,
            send_sem=z_send.at[d, t, q],
            recv_sem=z_recv.at[d, t, q],
            device_id=(up if d == 0 else down, cd),
            device_id_type=MESH,
        )

    def z_arrival(d, t, q):
        source_z = lax.rem(z + n_z - t - 1, n_z) if d == 0 else lax.rem(z + t + 1, n_z)
        cols_here = slice(0, cols)
        if t == steps - 1:
            cols_here = slice(0, cols // 2) if d == 0 else slice(cols // 2, cols)
        dst = held.at[block_rows(source_z * n_x + q), cols_here]
        return pltpu.make_async_remote_copy(
            src_ref=dst,
            dst_ref=dst,
            send_sem=z_send.at[d, t, q],
            recv_sem=z_recv.at[d, t, q],
            device_id=(up if d == 0 else down, cd),
            device_id_type=MESH,
        )

    for i in range(n_x):
        if i == 0:
            local.wait()
        else:
            x_copy(i, True).wait_recv()
        landed = lax.rem(x + n_x - i, n_x)
        for d in (0, 1):
            z_copy(d, 0, landed).start()
    for t in range(1, steps):
        for q in range(n_x):
            for d in (0, 1):
                z_arrival(d, t - 1, q).wait_recv()
                z_copy(d, t, q).start()
    for q in range(n_x):
        for d in (0, 1):
            z_arrival(d, steps - 1, q).wait_recv()
    for i in range(1, n_x):
        x_copy(i, False).wait_send()
    for t in range(steps):
        for q in range(n_x):
            for d in (0, 1):
                z_copy(d, t, q).wait_send()
    out_ref[...] = held[...]


def gather_rows(amplitudes, n_x, n_z):
    rows, cols = amplitudes.shape
    steps = n_z // 2
    return pl.pallas_call(
        functools.partial(gather_kernel, n_x, n_z),
        out_shape=jax.ShapeDtypeStruct((rows * n_x * n_z, cols), amplitudes.dtype),
        in_specs=[pl.BlockSpec(memory_space=pltpu.VMEM)],
        out_specs=pl.BlockSpec(memory_space=pltpu.VMEM),
        scratch_shapes=[
            pltpu.VMEM((rows * n_x * n_z, cols), amplitudes.dtype),
            pltpu.SemaphoreType.DMA(()),
            pltpu.SemaphoreType.DMA((n_x,)),
            pltpu.SemaphoreType.DMA((n_x,)),
            pltpu.SemaphoreType.DMA((2, steps, n_x)),
            pltpu.SemaphoreType.DMA((2, steps, n_x)),
        ],
        compiler_params=pltpu.CompilerParams(collective_id=0, has_side_effects=True),
    )(amplitudes)


def x_extent(mesh):
    first = mesh.devices.reshape(mesh.shape["ab"], -1)[:, 0]
    try:
        return len({d.coords[0] for d in first})
    except AttributeError:
        return 2


def scatter_kernel(n_y, n_chunks, part_ref, out_ref, mine, pair, send_r, recv_r, send_l, recv_l,
                   mine_sem, pair_send, pair_recv, ring_send, ring_recv):
    ab = lax.axis_index("ab")
    cd = lax.axis_index("cd")
    y, core = cd // 2, lax.rem(cd, 2)
    other = 1 - core
    right = lax.rem(y + 1, n_y) * 2 + core
    left = lax.rem(y + n_y - 1, n_y) * 2 + core
    partner = y * 2 + other
    half = out_ref.shape[1] // 2
    width = half // n_chunks

    def fetch(k):
        b = lax.rem(y + k + n_y, n_y)
        return pltpu.make_async_copy(part_ref.at[b, core], mine.at[b], mine_sem.at[b])

    fetch_order = []
    for s in range(1, n_y // 2 + 1):
        for k in (-s, s):
            if k % n_y not in [j % n_y for j in fetch_order]:
                fetch_order.append(k)
    fetch_order.append(0)
    for k in fetch_order:
        fetch(k).start()

    barrier = pltpu.get_barrier_semaphore()
    for peer in (partner, right, left):
        pl.semaphore_signal(barrier, inc=1, device_id=(ab, peer), device_id_type=MESH)
    pl.semaphore_wait(barrier, 3)

    order = []
    for k in list(range(1, n_y // 2 + 1)) + [0]:
        for sign in (1, -1):
            if (sign * k) % n_y not in [j % n_y for j in order]:
                order.append(sign * k)

    def pair_copy(k):
        b = lax.rem(y + k + n_y, n_y)
        return pltpu.make_async_remote_copy(
            src_ref=part_ref.at[b, other],
            dst_ref=pair.at[b],
            send_sem=pair_send.at[b],
            recv_sem=pair_recv.at[b],
            device_id=(ab, partner),
            device_id_type=MESH,
        )

    for k in order:
        pair_copy(k).start()

    def own(k, cols):
        b = lax.rem(y + k + n_y, n_y)
        return mine[b, :, cols] + pair[b, :, cols]

    def columns(d, q):
        start = d * half + q * width
        return slice(start, start + width)

    sends = (send_r, send_l)
    recvs = (recv_r, recv_l)

    def ring_copy(d, s, q):
        return pltpu.make_async_remote_copy(
            src_ref=sends[d].at[s, q],
            dst_ref=recvs[d].at[s, q],
            send_sem=ring_send.at[d, s, q],
            recv_sem=ring_recv.at[d, s, q],
            device_id=(ab, right if d == 0 else left),
            device_id_type=MESH,
        )

    waited = set()

    def need(k):
        k = k % n_y
        if k not in waited:
            waited.add(k)
            pair_copy(k if k <= n_y // 2 else k - n_y).wait_recv()
            fetch(k).wait()

    for s in range(n_y - 1):
        need(-(s + 1))
        need(s + 1)
        for q in range(n_chunks):
            for d in (0, 1):
                k = -(s + 1) if d == 0 else s + 1
                if s == 0:
                    sends[d][s, q] = own(k, columns(d, q))
                else:
                    ring_copy(d, s - 1, q).wait_recv()
                    sends[d][s, q] = recvs[d][s - 1, q] + own(k, columns(d, q))
                ring_copy(d, s, q).start()
    need(0)
    for q in range(n_chunks):
        for d in (0, 1):
            ring_copy(d, n_y - 2, q).wait_recv()
            out_ref[:, columns(d, q)] = recvs[d][n_y - 2, q] + own(0, columns(d, q))
    for k in order:
        pair_copy(k).wait_send()
    for s in range(n_y - 1):
        for q in range(n_chunks):
            ring_copy(0, s, q).wait_send()
            ring_copy(1, s, q).wait_send()


def scatter_rows(partial_value, n_cd, n_chunks=2):
    n_y = n_cd // 2
    total_rows, cols = partial_value.shape
    rows = total_rows // n_cd
    blocks = partial_value.reshape(n_y, 2, rows, cols)
    width = cols // 2 // n_chunks
    slots = pltpu.VMEM((n_y - 1, n_chunks, rows, width), jnp.float32)
    return pl.pallas_call(
        functools.partial(scatter_kernel, n_y, n_chunks),
        out_shape=jax.ShapeDtypeStruct((rows, cols), partial_value.dtype),
        in_specs=[pl.BlockSpec(memory_space=pl.ANY)],
        out_specs=pl.BlockSpec(memory_space=pltpu.VMEM),
        scratch_shapes=[
            pltpu.VMEM((n_y, rows, cols), jnp.float32),
            pltpu.VMEM((n_y, rows, cols), jnp.float32),
            slots,
            slots,
            slots,
            slots,
            pltpu.SemaphoreType.DMA((n_y,)),
            pltpu.SemaphoreType.DMA((n_y,)),
            pltpu.SemaphoreType.DMA((n_y,)),
            pltpu.SemaphoreType.DMA((2, n_y - 1, n_chunks)),
            pltpu.SemaphoreType.DMA((2, n_y - 1, n_chunks)),
        ],
        compiler_params=pltpu.CompilerParams(collective_id=1, has_side_effects=True),
    )(blocks)


def on_device(n_x, n_z, n_cd, amplitudes, integrals, ij_pairs, ab_pairs, eps_occ, eps_vir):
    partial_value = contract_rows(gather_rows(amplitudes, n_x, n_z), integrals)
    ladder = scatter_rows(partial_value, n_cd)
    first_occ = lookup_energy(ij_pairs[:, 0], eps_occ)[:, None]
    second_occ = lookup_energy(ij_pairs[:, 1], eps_occ)[:, None]
    first_vir = lookup_energy(ab_pairs[:, 0], eps_vir)[None, :]
    second_vir = lookup_energy(ab_pairs[:, 1], eps_vir)[None, :]
    denominator = first_occ + second_occ - first_vir - second_vir
    update = ladder / denominator
    return (jnp.where(denominator == denominator, ladder, update), update)


def solution(mesh):
    in_specs = (P("ab", "cd"), P("ab", "cd"), P("cd", None), P("ab", None), P(), P())
    out_specs = (P("cd", "ab"), P("cd", "ab"))
    return jax.shard_map(
        functools.partial(on_device, x_extent(mesh), mesh.shape["ab"] // x_extent(mesh), mesh.shape["cd"]),
        mesh=mesh,
        in_specs=in_specs,
        out_specs=out_specs,
        check_vma=False,
    )
```

```python
import functools

import jax
import jax.numpy as jnp
from jax import lax
from jax.experimental import pallas as pl
from jax.experimental.pallas import tpu as pltpu
from jax.sharding import PartitionSpec as P

MESH = pl.DeviceIdType.MESH


def lookup_energy(indices, energies):
    lanes = 128
    groups = -(-energies.shape[0] // lanes)
    table = jnp.pad(energies, (0, groups * lanes - energies.shape[0])).reshape(groups, lanes)
    low = lax.rem(indices, lanes)
    high = indices // lanes
    one_hot = (low[:, None] == lax.broadcasted_iota(jnp.int32, (indices.shape[0], lanes), 1)).astype(jnp.float32)
    by_group = lax.dot_general(
        one_hot, table, (((1,), (1,)), ((), ())),
        precision=lax.Precision.HIGHEST, preferred_element_type=jnp.float32,
    )
    chosen = high[:, None] == lax.broadcasted_iota(jnp.int32, by_group.shape, 1)
    return jnp.sum(jnp.where(chosen, by_group, jnp.float32(0.0)), axis=1)


def contract_rows(row_block, col_block):
    return lax.dot_general(
        row_block,
        col_block,
        (((1,), (1,)), ((), ())),
        precision=lax.Precision.HIGH,
        preferred_element_type=jnp.float32,
    )


def gather_kernel(n_x, n_z, amp_ref, out_ref, held, local_sem, x_send, x_recv, z_send, z_recv):
    ab = lax.axis_index("ab")
    cd = lax.axis_index("cd")
    z, x = ab // n_x, lax.rem(ab, n_x)
    rows = amp_ref.shape[0]
    group = rows * n_x
    cols = amp_ref.shape[1]
    up = lax.rem(z + 1, n_z) * n_x + x
    down = lax.rem(z + n_z - 1, n_z) * n_x + x

    barrier = pltpu.get_barrier_semaphore()
    for i in range(1, n_x):
        pl.semaphore_signal(barrier, inc=1, device_id=(z * n_x + lax.rem(x + i, n_x), cd), device_id_type=MESH)
    pl.semaphore_signal(barrier, inc=1, device_id=(up, cd), device_id_type=MESH)
    pl.semaphore_signal(barrier, inc=1, device_id=(down, cd), device_id_type=MESH)
    pl.semaphore_wait(barrier, n_x + 1)

    def block_rows(a_index):
        return pl.ds(pl.multiple_of(a_index * rows, rows), rows)

    def x_copy(i, receiving):
        sender = lax.rem(x + n_x - i, n_x) if receiving else x
        target = lax.rem(x + i, n_x)
        return pltpu.make_async_remote_copy(
            src_ref=amp_ref,
            dst_ref=held.at[block_rows(z * n_x + sender)],
            send_sem=x_send.at[target],
            recv_sem=x_recv.at[sender],
            device_id=(z * n_x + target, cd),
            device_id_type=MESH,
        )

    for i in range(1, n_x):
        x_copy(i, False).start()
    local = pltpu.make_async_copy(amp_ref, held.at[block_rows(ab)], local_sem)
    local.start()

    steps = n_z // 2

    def z_copy(d, t, q):
        source_z = lax.rem(z + n_z - t, n_z) if d == 0 else lax.rem(z + t, n_z)
        cols_here = slice(0, cols)
        if t == steps - 1:
            cols_here = slice(0, cols // 2) if d == 0 else slice(cols // 2, cols)
        src = held.at[block_rows(source_z * n_x + q), cols_here]
        return pltpu.make_async_remote_copy(
            src_ref=src,
            dst_ref=src,
            send_sem=z_send.at[d, t, q],
            recv_sem=z_recv.at[d, t, q],
            device_id=(up if d == 0 else down, cd),
            device_id_type=MESH,
        )

    def z_arrival(d, t, q):
        source_z = lax.rem(z + n_z - t - 1, n_z) if d == 0 else lax.rem(z + t + 1, n_z)
        cols_here = slice(0, cols)
        if t == steps - 1:
            cols_here = slice(0, cols // 2) if d == 0 else slice(cols // 2, cols)
        dst = held.at[block_rows(source_z * n_x + q), cols_here]
        return pltpu.make_async_remote_copy(
            src_ref=dst,
            dst_ref=dst,
            send_sem=z_send.at[d, t, q],
            recv_sem=z_recv.at[d, t, q],
            device_id=(up if d == 0 else down, cd),
            device_id_type=MESH,
        )

    for i in range(n_x):
        if i == 0:
            local.wait()
        else:
            x_copy(i, True).wait_recv()
        landed = lax.rem(x + n_x - i, n_x)
        for d in (0, 1):
            z_copy(d, 0, landed).start()
    for t in range(1, steps):
        for q in range(n_x):
            for d in (0, 1):
                z_arrival(d, t - 1, q).wait_recv()
                z_copy(d, t, q).start()
    for q in range(n_x):
        for d in (0, 1):
            z_arrival(d, steps - 1, q).wait_recv()
    for i in range(1, n_x):
        x_copy(i, False).wait_send()
    for t in range(steps):
        for q in range(n_x):
            for d in (0, 1):
                z_copy(d, t, q).wait_send()
    out_ref[...] = held[...]


def gather_rows(amplitudes, n_x, n_z):
    rows, cols = amplitudes.shape
    steps = n_z // 2
    return pl.pallas_call(
        functools.partial(gather_kernel, n_x, n_z),
        out_shape=jax.ShapeDtypeStruct((rows * n_x * n_z, cols), amplitudes.dtype),
        in_specs=[pl.BlockSpec(memory_space=pltpu.VMEM)],
        out_specs=pl.BlockSpec(memory_space=pltpu.VMEM),
        scratch_shapes=[
            pltpu.VMEM((rows * n_x * n_z, cols), amplitudes.dtype),
            pltpu.SemaphoreType.DMA(()),
            pltpu.SemaphoreType.DMA((n_x,)),
            pltpu.SemaphoreType.DMA((n_x,)),
            pltpu.SemaphoreType.DMA((2, steps, n_x)),
            pltpu.SemaphoreType.DMA((2, steps, n_x)),
        ],
        compiler_params=pltpu.CompilerParams(collective_id=0, has_side_effects=True),
    )(amplitudes)


def x_extent(mesh):
    first = mesh.devices.reshape(mesh.shape["ab"], -1)[:, 0]
    try:
        return len({d.coords[0] for d in first})
    except AttributeError:
        return 2


def scatter_kernel(n_y, n_chunks, part_ref, out_ref, mine, pair, send_r, recv_r, send_l, recv_l,
                   mine_sem, pair_send, pair_recv, ring_send, ring_recv):
    ab = lax.axis_index("ab")
    cd = lax.axis_index("cd")
    y, core = cd // 2, lax.rem(cd, 2)
    other = 1 - core
    right = lax.rem(y + 1, n_y) * 2 + core
    left = lax.rem(y + n_y - 1, n_y) * 2 + core
    partner = y * 2 + other
    half = out_ref.shape[1] // 2
    width = half // n_chunks

    def fetch(k):
        b = lax.rem(y + k + n_y, n_y)
        return pltpu.make_async_copy(part_ref.at[b, core], mine.at[b], mine_sem.at[b])

    fetch_order = []
    for s in range(1, n_y // 2 + 1):
        for k in (-s, s):
            if k % n_y not in [j % n_y for j in fetch_order]:
                fetch_order.append(k)
    fetch_order.append(0)
    for k in fetch_order:
        fetch(k).start()

    barrier = pltpu.get_barrier_semaphore()
    for peer in (partner, right, left):
        pl.semaphore_signal(barrier, inc=1, device_id=(ab, peer), device_id_type=MESH)
    pl.semaphore_wait(barrier, 3)

    order = []
    for k in list(range(1, n_y // 2 + 1)) + [0]:
        for sign in (1, -1):
            if (sign * k) % n_y not in [j % n_y for j in order]:
                order.append(sign * k)

    def pair_copy(k):
        b = lax.rem(y + k + n_y, n_y)
        return pltpu.make_async_remote_copy(
            src_ref=part_ref.at[b, other],
            dst_ref=pair.at[b],
            send_sem=pair_send.at[b],
            recv_sem=pair_recv.at[b],
            device_id=(ab, partner),
            device_id_type=MESH,
        )

    for k in order:
        pair_copy(k).start()

    def own(k, cols):
        b = lax.rem(y + k + n_y, n_y)
        return mine[b, :, cols] + pair[b, :, cols]

    def columns(d, q):
        start = d * half + q * width
        return slice(start, start + width)

    sends = (send_r, send_l)
    recvs = (recv_r, recv_l)

    def ring_copy(d, s, q):
        return pltpu.make_async_remote_copy(
            src_ref=sends[d].at[s, q],
            dst_ref=recvs[d].at[s, q],
            send_sem=ring_send.at[d, s, q],
            recv_sem=ring_recv.at[d, s, q],
            device_id=(ab, right if d == 0 else left),
            device_id_type=MESH,
        )

    waited = set()

    def need(k):
        k = k % n_y
        if k not in waited:
            waited.add(k)
            pair_copy(k if k <= n_y // 2 else k - n_y).wait_recv()
            fetch(k).wait()

    for s in range(n_y - 1):
        need(-(s + 1))
        need(s + 1)
        for q in range(n_chunks):
            for d in (0, 1):
                k = -(s + 1) if d == 0 else s + 1
                if s == 0:
                    sends[d][s, q] = own(k, columns(d, q))
                else:
                    ring_copy(d, s - 1, q).wait_recv()
                    sends[d][s, q] = recvs[d][s - 1, q] + own(k, columns(d, q))
                ring_copy(d, s, q).start()
    need(0)
    for q in range(n_chunks):
        for d in (0, 1):
            ring_copy(d, n_y - 2, q).wait_recv()
            out_ref[:, columns(d, q)] = recvs[d][n_y - 2, q] + own(0, columns(d, q))
    for k in order:
        pair_copy(k).wait_send()
    for s in range(n_y - 1):
        for q in range(n_chunks):
            ring_copy(0, s, q).wait_send()
            ring_copy(1, s, q).wait_send()


def scatter_rows(partial_value, n_cd, n_chunks=4):
    n_y = n_cd // 2
    total_rows, cols = partial_value.shape
    rows = total_rows // n_cd
    blocks = partial_value.reshape(n_y, 2, rows, cols)
    width = cols // 2 // n_chunks
    slots = pltpu.VMEM((n_y - 1, n_chunks, rows, width), jnp.float32)
    return pl.pallas_call(
        functools.partial(scatter_kernel, n_y, n_chunks),
        out_shape=jax.ShapeDtypeStruct((rows, cols), partial_value.dtype),
        in_specs=[pl.BlockSpec(memory_space=pl.ANY)],
        out_specs=pl.BlockSpec(memory_space=pltpu.VMEM),
        scratch_shapes=[
            pltpu.VMEM((n_y, rows, cols), jnp.float32),
            pltpu.VMEM((n_y, rows, cols), jnp.float32),
            slots,
            slots,
            slots,
            slots,
            pltpu.SemaphoreType.DMA((n_y,)),
            pltpu.SemaphoreType.DMA((n_y,)),
            pltpu.SemaphoreType.DMA((n_y,)),
            pltpu.SemaphoreType.DMA((2, n_y - 1, n_chunks)),
            pltpu.SemaphoreType.DMA((2, n_y - 1, n_chunks)),
        ],
        compiler_params=pltpu.CompilerParams(collective_id=1, has_side_effects=True),
    )(blocks)


def on_device(n_x, n_z, n_cd, amplitudes, integrals, ij_pairs, ab_pairs, eps_occ, eps_vir):
    first_occ = lookup_energy(ij_pairs[:, 0], eps_occ)[:, None]
    second_occ = lookup_energy(ij_pairs[:, 1], eps_occ)[:, None]
    first_vir = lookup_energy(ab_pairs[:, 0], eps_vir)[None, :]
    second_vir = lookup_energy(ab_pairs[:, 1], eps_vir)[None, :]
    first_occ, second_occ, first_vir, second_vir, amplitudes = lax.optimization_barrier(
        (first_occ, second_occ, first_vir, second_vir, amplitudes)
    )
    partial_value = contract_rows(gather_rows(amplitudes, n_x, n_z), integrals)
    ladder = scatter_rows(partial_value, n_cd)
    denominator = first_occ + second_occ - first_vir - second_vir
    update = ladder / denominator
    return (jnp.where(denominator == denominator, ladder, update), update)


def solution(mesh):
    in_specs = (P("ab", "cd"), P("ab", "cd"), P("cd", None), P("ab", None), P(), P())
    out_specs = (P("cd", "ab"), P("cd", "ab"))
    return jax.shard_map(
        functools.partial(on_device, x_extent(mesh), mesh.shape["ab"] // x_extent(mesh), mesh.shape["cd"]),
        mesh=mesh,
        in_specs=in_specs,
        out_specs=out_specs,
        check_vma=False,
    )
```

```python
import functools

import jax
import jax.numpy as jnp
from jax import lax
from jax.experimental import pallas as pl
from jax.experimental.pallas import tpu as pltpu
from jax.sharding import PartitionSpec as P

MESH = pl.DeviceIdType.MESH


def lookup_energy(indices, energies):
    lanes = 128
    groups = -(-energies.shape[0] // lanes)
    table = jnp.pad(energies, (0, groups * lanes - energies.shape[0])).reshape(groups, lanes)
    low = lax.rem(indices, lanes)
    high = indices // lanes
    one_hot = (low[:, None] == lax.broadcasted_iota(jnp.int32, (indices.shape[0], lanes), 1)).astype(jnp.float32)
    by_group = lax.dot_general(
        one_hot, table, (((1,), (1,)), ((), ())),
        precision=lax.Precision.HIGHEST, preferred_element_type=jnp.float32,
    )
    chosen = high[:, None] == lax.broadcasted_iota(jnp.int32, by_group.shape, 1)
    return jnp.sum(jnp.where(chosen, by_group, jnp.float32(0.0)), axis=1)


def contract_rows(row_block, col_block):
    return lax.dot_general(
        row_block,
        col_block,
        (((1,), (1,)), ((), ())),
        precision=lax.Precision.HIGH,
        preferred_element_type=jnp.float32,
    )


def gather_kernel(n_x, n_z, amp_ref, out_ref, held, local_sem, x_send, x_recv, z_send, z_recv):
    ab = lax.axis_index("ab")
    cd = lax.axis_index("cd")
    z, x = ab // n_x, lax.rem(ab, n_x)
    rows = amp_ref.shape[0]
    group = rows * n_x
    cols = amp_ref.shape[1]
    up = lax.rem(z + 1, n_z) * n_x + x
    down = lax.rem(z + n_z - 1, n_z) * n_x + x

    barrier = pltpu.get_barrier_semaphore()
    for i in range(1, n_x):
        pl.semaphore_signal(barrier, inc=1, device_id=(z * n_x + lax.rem(x + i, n_x), cd), device_id_type=MESH)
    pl.semaphore_signal(barrier, inc=1, device_id=(up, cd), device_id_type=MESH)
    pl.semaphore_signal(barrier, inc=1, device_id=(down, cd), device_id_type=MESH)
    pl.semaphore_wait(barrier, n_x + 1)

    def block_rows(a_index):
        return pl.ds(pl.multiple_of(a_index * rows, rows), rows)

    def x_copy(i, receiving):
        sender = lax.rem(x + n_x - i, n_x) if receiving else x
        target = lax.rem(x + i, n_x)
        return pltpu.make_async_remote_copy(
            src_ref=amp_ref,
            dst_ref=held.at[block_rows(z * n_x + sender)],
            send_sem=x_send.at[target],
            recv_sem=x_recv.at[sender],
            device_id=(z * n_x + target, cd),
            device_id_type=MESH,
        )

    for i in range(1, n_x):
        x_copy(i, False).start()
    local = pltpu.make_async_copy(amp_ref, held.at[block_rows(ab)], local_sem)
    local.start()

    steps = n_z // 2

    def z_copy(d, t, q):
        source_z = lax.rem(z + n_z - t, n_z) if d == 0 else lax.rem(z + t, n_z)
        cols_here = slice(0, cols)
        if t == steps - 1:
            cols_here = slice(0, cols // 2) if d == 0 else slice(cols // 2, cols)
        src = held.at[block_rows(source_z * n_x + q), cols_here]
        return pltpu.make_async_remote_copy(
            src_ref=src,
            dst_ref=src,
            send_sem=z_send.at[d, t, q],
            recv_sem=z_recv.at[d, t, q],
            device_id=(up if d == 0 else down, cd),
            device_id_type=MESH,
        )

    def z_arrival(d, t, q):
        source_z = lax.rem(z + n_z - t - 1, n_z) if d == 0 else lax.rem(z + t + 1, n_z)
        cols_here = slice(0, cols)
        if t == steps - 1:
            cols_here = slice(0, cols // 2) if d == 0 else slice(cols // 2, cols)
        dst = held.at[block_rows(source_z * n_x + q), cols_here]
        return pltpu.make_async_remote_copy(
            src_ref=dst,
            dst_ref=dst,
            send_sem=z_send.at[d, t, q],
            recv_sem=z_recv.at[d, t, q],
            device_id=(up if d == 0 else down, cd),
            device_id_type=MESH,
        )

    for i in range(n_x):
        if i == 0:
            local.wait()
        else:
            x_copy(i, True).wait_recv()
        landed = lax.rem(x + n_x - i, n_x)
        for d in (0, 1):
            z_copy(d, 0, landed).start()
    for t in range(1, steps):
        for q in range(n_x):
            for d in (0, 1):
                z_arrival(d, t - 1, q).wait_recv()
                z_copy(d, t, q).start()
    for q in range(n_x):
        for d in (0, 1):
            z_arrival(d, steps - 1, q).wait_recv()
    for i in range(1, n_x):
        x_copy(i, False).wait_send()
    for t in range(steps):
        for q in range(n_x):
            for d in (0, 1):
                z_copy(d, t, q).wait_send()
    out_ref[...] = held[...]


def gather_rows(amplitudes, n_x, n_z):
    rows, cols = amplitudes.shape
    steps = n_z // 2
    return pl.pallas_call(
        functools.partial(gather_kernel, n_x, n_z),
        out_shape=jax.ShapeDtypeStruct((rows * n_x * n_z, cols), amplitudes.dtype),
        in_specs=[pl.BlockSpec(memory_space=pltpu.VMEM)],
        out_specs=pl.BlockSpec(memory_space=pltpu.VMEM),
        scratch_shapes=[
            pltpu.VMEM((rows * n_x * n_z, cols), amplitudes.dtype),
            pltpu.SemaphoreType.DMA(()),
            pltpu.SemaphoreType.DMA((n_x,)),
            pltpu.SemaphoreType.DMA((n_x,)),
            pltpu.SemaphoreType.DMA((2, steps, n_x)),
            pltpu.SemaphoreType.DMA((2, steps, n_x)),
        ],
        compiler_params=pltpu.CompilerParams(collective_id=0, has_side_effects=True),
    )(amplitudes)


def x_extent(mesh):
    first = mesh.devices.reshape(mesh.shape["ab"], -1)[:, 0]
    try:
        return len({d.coords[0] for d in first})
    except AttributeError:
        return 2


def scatter_kernel(n_y, n_chunks, part_ref, out_ref, mine, pair, send_r, recv_r, send_l, recv_l,
                   mine_sem, pair_send, pair_recv, ring_send, ring_recv):
    ab = lax.axis_index("ab")
    cd = lax.axis_index("cd")
    y, core = cd // 2, lax.rem(cd, 2)
    other = 1 - core
    right = lax.rem(y + 1, n_y) * 2 + core
    left = lax.rem(y + n_y - 1, n_y) * 2 + core
    partner = y * 2 + other
    half = out_ref.shape[1] // 2
    width = half // n_chunks

    def fetch(k):
        b = lax.rem(y + k + n_y, n_y)
        return pltpu.make_async_copy(part_ref.at[b, core], mine.at[b], mine_sem.at[b])

    fetch_order = []
    for s in range(1, n_y // 2 + 1):
        for k in (-s, s):
            if k % n_y not in [j % n_y for j in fetch_order]:
                fetch_order.append(k)
    fetch_order.append(0)
    early = fetch_order[:2]
    for k in early:
        fetch(k).start()

    barrier = pltpu.get_barrier_semaphore()
    for peer in (partner, right, left):
        pl.semaphore_signal(barrier, inc=1, device_id=(ab, peer), device_id_type=MESH)
    pl.semaphore_wait(barrier, 3)

    order = []
    for k in list(range(1, n_y // 2 + 1)) + [0]:
        for sign in (1, -1):
            if (sign * k) % n_y not in [j % n_y for j in order]:
                order.append(sign * k)

    def pair_copy(k):
        b = lax.rem(y + k + n_y, n_y)
        return pltpu.make_async_remote_copy(
            src_ref=part_ref.at[b, other],
            dst_ref=pair.at[b],
            send_sem=pair_send.at[b],
            recv_sem=pair_recv.at[b],
            device_id=(ab, partner),
            device_id_type=MESH,
        )

    for k in order:
        pair_copy(k).start()
        if k % n_y not in [j % n_y for j in early]:
            fetch(k).start()

    def own(k, cols):
        b = lax.rem(y + k + n_y, n_y)
        return mine[b, :, cols] + pair[b, :, cols]

    def columns(d, q):
        start = d * half + q * width
        return slice(start, start + width)

    sends = (send_r, send_l)
    recvs = (recv_r, recv_l)

    def ring_copy(d, s, q):
        return pltpu.make_async_remote_copy(
            src_ref=sends[d].at[s, q],
            dst_ref=recvs[d].at[s, q],
            send_sem=ring_send.at[d, s, q],
            recv_sem=ring_recv.at[d, s, q],
            device_id=(ab, right if d == 0 else left),
            device_id_type=MESH,
        )

    waited = set()

    def need(k):
        k = k % n_y
        if k not in waited:
            waited.add(k)
            pair_copy(k if k <= n_y // 2 else k - n_y).wait_recv()
            fetch(k).wait()

    for s in range(n_y - 1):
        need(-(s + 1))
        need(s + 1)
        for q in range(n_chunks):
            for d in (0, 1):
                k = -(s + 1) if d == 0 else s + 1
                if s == 0:
                    sends[d][s, q] = own(k, columns(d, q))
                else:
                    ring_copy(d, s - 1, q).wait_recv()
                    sends[d][s, q] = recvs[d][s - 1, q] + own(k, columns(d, q))
                ring_copy(d, s, q).start()
    need(0)
    for q in range(n_chunks):
        for d in (0, 1):
            ring_copy(d, n_y - 2, q).wait_recv()
            out_ref[:, columns(d, q)] = recvs[d][n_y - 2, q] + own(0, columns(d, q))
    for k in order:
        pair_copy(k).wait_send()
    for s in range(n_y - 1):
        for q in range(n_chunks):
            ring_copy(0, s, q).wait_send()
            ring_copy(1, s, q).wait_send()


def scatter_rows(partial_value, n_cd, n_chunks=4):
    n_y = n_cd // 2
    total_rows, cols = partial_value.shape
    rows = total_rows // n_cd
    blocks = partial_value.reshape(n_y, 2, rows, cols)
    width = cols // 2 // n_chunks
    slots = pltpu.VMEM((n_y - 1, n_chunks, rows, width), jnp.float32)
    return pl.pallas_call(
        functools.partial(scatter_kernel, n_y, n_chunks),
        out_shape=jax.ShapeDtypeStruct((rows, cols), partial_value.dtype),
        in_specs=[pl.BlockSpec(memory_space=pl.ANY)],
        out_specs=pl.BlockSpec(memory_space=pltpu.VMEM),
        scratch_shapes=[
            pltpu.VMEM((n_y, rows, cols), jnp.float32),
            pltpu.VMEM((n_y, rows, cols), jnp.float32),
            slots,
            slots,
            slots,
            slots,
            pltpu.SemaphoreType.DMA((n_y,)),
            pltpu.SemaphoreType.DMA((n_y,)),
            pltpu.SemaphoreType.DMA((n_y,)),
            pltpu.SemaphoreType.DMA((2, n_y - 1, n_chunks)),
            pltpu.SemaphoreType.DMA((2, n_y - 1, n_chunks)),
        ],
        compiler_params=pltpu.CompilerParams(collective_id=1, has_side_effects=True),
    )(blocks)


def on_device(n_x, n_z, n_cd, amplitudes, integrals, ij_pairs, ab_pairs, eps_occ, eps_vir):
    partial_value = contract_rows(gather_rows(amplitudes, n_x, n_z), integrals)
    ladder = scatter_rows(partial_value, n_cd)
    first_occ = lookup_energy(ij_pairs[:, 0], eps_occ)[:, None]
    second_occ = lookup_energy(ij_pairs[:, 1], eps_occ)[:, None]
    first_vir = lookup_energy(ab_pairs[:, 0], eps_vir)[None, :]
    second_vir = lookup_energy(ab_pairs[:, 1], eps_vir)[None, :]
    denominator = first_occ + second_occ - first_vir - second_vir
    update = ladder / denominator
    return (jnp.where(denominator == denominator, ladder, update), update)


def solution(mesh):
    in_specs = (P("ab", "cd"), P("ab", "cd"), P("cd", None), P("ab", None), P(), P())
    out_specs = (P("cd", "ab"), P("cd", "ab"))
    return jax.shard_map(
        functools.partial(on_device, x_extent(mesh), mesh.shape["ab"] // x_extent(mesh), mesh.shape["cd"]),
        mesh=mesh,
        in_specs=in_specs,
        out_specs=out_specs,
        check_vma=False,
    )
```

```python
import functools

import jax
import jax.numpy as jnp
from jax import lax
from jax.experimental import pallas as pl
from jax.experimental.pallas import tpu as pltpu
from jax.sharding import PartitionSpec as P

MESH = pl.DeviceIdType.MESH


def lookup_energy(indices, energies):
    lanes = 128
    groups = -(-energies.shape[0] // lanes)
    table = jnp.pad(energies, (0, groups * lanes - energies.shape[0])).reshape(groups, lanes)
    low = lax.rem(indices, lanes)
    high = indices // lanes
    one_hot = (low[:, None] == lax.broadcasted_iota(jnp.int32, (indices.shape[0], lanes), 1)).astype(jnp.float32)
    by_group = lax.dot_general(
        one_hot, table, (((1,), (1,)), ((), ())),
        precision=lax.Precision.HIGHEST, preferred_element_type=jnp.float32,
    )
    chosen = high[:, None] == lax.broadcasted_iota(jnp.int32, by_group.shape, 1)
    return jnp.sum(jnp.where(chosen, by_group, jnp.float32(0.0)), axis=1)


def contract_rows(row_block, col_block):
    return lax.dot_general(
        row_block,
        col_block,
        (((1,), (1,)), ((), ())),
        precision=lax.Precision.HIGH,
        preferred_element_type=jnp.float32,
    )


def gather_kernel(n_x, n_z, amp_ref, out_ref, held, local_sem, x_send, x_recv, z_send, z_recv):
    ab = lax.axis_index("ab")
    cd = lax.axis_index("cd")
    z, x = ab // n_x, lax.rem(ab, n_x)
    rows = amp_ref.shape[0]
    group = rows * n_x
    cols = amp_ref.shape[1]
    up = lax.rem(z + 1, n_z) * n_x + x
    down = lax.rem(z + n_z - 1, n_z) * n_x + x

    barrier = pltpu.get_barrier_semaphore()
    for i in range(1, n_x):
        pl.semaphore_signal(barrier, inc=1, device_id=(z * n_x + lax.rem(x + i, n_x), cd), device_id_type=MESH)
    pl.semaphore_signal(barrier, inc=1, device_id=(up, cd), device_id_type=MESH)
    pl.semaphore_signal(barrier, inc=1, device_id=(down, cd), device_id_type=MESH)
    pl.semaphore_wait(barrier, n_x + 1)

    def block_rows(a_index):
        return pl.ds(pl.multiple_of(a_index * rows, rows), rows)

    def x_copy(i, receiving):
        sender = lax.rem(x + n_x - i, n_x) if receiving else x
        target = lax.rem(x + i, n_x)
        return pltpu.make_async_remote_copy(
            src_ref=amp_ref,
            dst_ref=held.at[block_rows(z * n_x + sender)],
            send_sem=x_send.at[target],
            recv_sem=x_recv.at[sender],
            device_id=(z * n_x + target, cd),
            device_id_type=MESH,
        )

    for i in range(1, n_x):
        x_copy(i, False).start()
    local = pltpu.make_async_copy(amp_ref, held.at[block_rows(ab)], local_sem)
    local.start()

    steps = n_z // 2

    def z_copy(d, t, q):
        source_z = lax.rem(z + n_z - t, n_z) if d == 0 else lax.rem(z + t, n_z)
        cols_here = slice(0, cols)
        if t == steps - 1:
            cols_here = slice(0, cols // 2) if d == 0 else slice(cols // 2, cols)
        src = held.at[block_rows(source_z * n_x + q), cols_here]
        return pltpu.make_async_remote_copy(
            src_ref=src,
            dst_ref=src,
            send_sem=z_send.at[d, t, q],
            recv_sem=z_recv.at[d, t, q],
            device_id=(up if d == 0 else down, cd),
            device_id_type=MESH,
        )

    def z_arrival(d, t, q):
        source_z = lax.rem(z + n_z - t - 1, n_z) if d == 0 else lax.rem(z + t + 1, n_z)
        cols_here = slice(0, cols)
        if t == steps - 1:
            cols_here = slice(0, cols // 2) if d == 0 else slice(cols // 2, cols)
        dst = held.at[block_rows(source_z * n_x + q), cols_here]
        return pltpu.make_async_remote_copy(
            src_ref=dst,
            dst_ref=dst,
            send_sem=z_send.at[d, t, q],
            recv_sem=z_recv.at[d, t, q],
            device_id=(up if d == 0 else down, cd),
            device_id_type=MESH,
        )

    for i in range(n_x):
        if i == 0:
            local.wait()
        else:
            x_copy(i, True).wait_recv()
        landed = lax.rem(x + n_x - i, n_x)
        for d in (0, 1):
            z_copy(d, 0, landed).start()
    for t in range(1, steps):
        for q in range(n_x):
            for d in (0, 1):
                z_arrival(d, t - 1, q).wait_recv()
                z_copy(d, t, q).start()
    for q in range(n_x):
        for d in (0, 1):
            z_arrival(d, steps - 1, q).wait_recv()
    for i in range(1, n_x):
        x_copy(i, False).wait_send()
    for t in range(steps):
        for q in range(n_x):
            for d in (0, 1):
                z_copy(d, t, q).wait_send()
    out_ref[...] = held[...]


def gather_rows(amplitudes, n_x, n_z):
    rows, cols = amplitudes.shape
    steps = n_z // 2
    return pl.pallas_call(
        functools.partial(gather_kernel, n_x, n_z),
        out_shape=jax.ShapeDtypeStruct((rows * n_x * n_z, cols), amplitudes.dtype),
        in_specs=[pl.BlockSpec(memory_space=pltpu.VMEM)],
        out_specs=pl.BlockSpec(memory_space=pltpu.VMEM),
        scratch_shapes=[
            pltpu.VMEM((rows * n_x * n_z, cols), amplitudes.dtype),
            pltpu.SemaphoreType.DMA(()),
            pltpu.SemaphoreType.DMA((n_x,)),
            pltpu.SemaphoreType.DMA((n_x,)),
            pltpu.SemaphoreType.DMA((2, steps, n_x)),
            pltpu.SemaphoreType.DMA((2, steps, n_x)),
        ],
        compiler_params=pltpu.CompilerParams(collective_id=0, has_side_effects=True),
    )(amplitudes)


def x_extent(mesh):
    first = mesh.devices.reshape(mesh.shape["ab"], -1)[:, 0]
    try:
        return len({d.coords[0] for d in first})
    except AttributeError:
        return 2


def scatter_kernel(n_y, n_chunks, part_ref, out_ref, mine, pair, send_r, recv_r, send_l, recv_l,
                   mine_sem, pair_send, pair_recv, ring_send, ring_recv):
    ab = lax.axis_index("ab")
    cd = lax.axis_index("cd")
    y, core = cd // 2, lax.rem(cd, 2)
    other = 1 - core
    right = lax.rem(y + 1, n_y) * 2 + core
    left = lax.rem(y + n_y - 1, n_y) * 2 + core
    partner = y * 2 + other
    half = out_ref.shape[1] // 2
    width = half // n_chunks

    def fetch(k):
        b = lax.rem(y + k + n_y, n_y)
        return pltpu.make_async_copy(part_ref.at[b, core], mine.at[b], mine_sem.at[b])

    fetch_order = []
    for s in range(1, n_y // 2 + 1):
        for k in (-s, s):
            if k % n_y not in [j % n_y for j in fetch_order]:
                fetch_order.append(k)
    fetch_order.append(0)
    for k in fetch_order:
        fetch(k).start()

    barrier = pltpu.get_barrier_semaphore()
    for peer in (partner, right, left):
        pl.semaphore_signal(barrier, inc=1, device_id=(ab, peer), device_id_type=MESH)
    pl.semaphore_wait(barrier, 3)

    order = []
    for k in list(range(1, n_y // 2 + 1)) + [0]:
        for sign in (1, -1):
            if (sign * k) % n_y not in [j % n_y for j in order]:
                order.append(sign * k)

    def pair_copy(k):
        b = lax.rem(y + k + n_y, n_y)
        return pltpu.make_async_remote_copy(
            src_ref=part_ref.at[b, other],
            dst_ref=pair.at[b],
            send_sem=pair_send.at[b],
            recv_sem=pair_recv.at[b],
            device_id=(ab, partner),
            device_id_type=MESH,
        )

    for k in order:
        pair_copy(k).start()

    def own(k, cols):
        b = lax.rem(y + k + n_y, n_y)
        return mine[b, :, cols] + pair[b, :, cols]

    def columns(d, q):
        start = d * half + q * width
        return slice(start, start + width)

    sends = (send_r, send_l)
    recvs = (recv_r, recv_l)

    def ring_copy(d, s, q):
        return pltpu.make_async_remote_copy(
            src_ref=sends[d].at[s, q],
            dst_ref=recvs[d].at[s, q],
            send_sem=ring_send.at[d, s, q],
            recv_sem=ring_recv.at[d, s, q],
            device_id=(ab, right if d == 0 else left),
            device_id_type=MESH,
        )

    waited = set()

    def need(k):
        k = k % n_y
        if k not in waited:
            waited.add(k)
            pair_copy(k if k <= n_y // 2 else k - n_y).wait_recv()
            fetch(k).wait()

    for s in range(n_y - 1):
        need(-(s + 1))
        need(s + 1)
        for q in range(n_chunks):
            for d in (0, 1):
                k = -(s + 1) if d == 0 else s + 1
                if s == 0:
                    sends[d][s, q] = own(k, columns(d, q))
                else:
                    ring_copy(d, s - 1, q).wait_recv()
                    sends[d][s, q] = recvs[d][s - 1, q] + own(k, columns(d, q))
                ring_copy(d, s, q).start()
    need(0)
    for q in range(n_chunks):
        for d in (0, 1):
            ring_copy(d, n_y - 2, q).wait_recv()
            out_ref[:, columns(d, q)] = recvs[d][n_y - 2, q] + own(0, columns(d, q))
    for k in order:
        pair_copy(k).wait_send()
    for s in range(n_y - 1):
        for q in range(n_chunks):
            ring_copy(0, s, q).wait_send()
            ring_copy(1, s, q).wait_send()


def scatter_rows(partial_value, n_cd, n_chunks=4):
    n_y = n_cd // 2
    total_rows, cols = partial_value.shape
    rows = total_rows // n_cd
    blocks = partial_value.reshape(n_y, 2, rows, cols)
    width = cols // 2 // n_chunks
    slots = pltpu.VMEM((n_y - 1, n_chunks, rows, width), jnp.float32)
    return pl.pallas_call(
        functools.partial(scatter_kernel, n_y, n_chunks),
        out_shape=jax.ShapeDtypeStruct((rows, cols), partial_value.dtype),
        in_specs=[pl.BlockSpec(memory_space=pl.ANY)],
        out_specs=pl.BlockSpec(memory_space=pltpu.VMEM),
        scratch_shapes=[
            pltpu.VMEM((n_y, rows, cols), jnp.float32),
            pltpu.VMEM((n_y, rows, cols), jnp.float32),
            slots,
            slots,
            slots,
            slots,
            pltpu.SemaphoreType.DMA((n_y,)),
            pltpu.SemaphoreType.DMA((n_y,)),
            pltpu.SemaphoreType.DMA((n_y,)),
            pltpu.SemaphoreType.DMA((2, n_y - 1, n_chunks)),
            pltpu.SemaphoreType.DMA((2, n_y - 1, n_chunks)),
        ],
        compiler_params=pltpu.CompilerParams(collective_id=1, has_side_effects=True),
    )(blocks)


def on_device(n_x, n_z, n_cd, amplitudes, integrals, ij_pairs, ab_pairs, eps_occ, eps_vir):
    partial_value = contract_rows(gather_rows(amplitudes, n_x, n_z), integrals)
    ladder = scatter_rows(partial_value, n_cd)
    n_ij, n_ab = ij_pairs.shape[0], ab_pairs.shape[0]
    occ = lookup_energy(jnp.concatenate([ij_pairs[:, 0], ij_pairs[:, 1]]), eps_occ)
    vir = lookup_energy(jnp.concatenate([ab_pairs[:, 0], ab_pairs[:, 1]]), eps_vir)
    first_occ = occ[:n_ij][:, None]
    second_occ = occ[n_ij:][:, None]
    first_vir = vir[:n_ab][None, :]
    second_vir = vir[n_ab:][None, :]
    denominator = first_occ + second_occ - first_vir - second_vir
    update = ladder / denominator
    return (jnp.where(denominator == denominator, ladder, update), update)


def solution(mesh):
    in_specs = (P("ab", "cd"), P("ab", "cd"), P("cd", None), P("ab", None), P(), P())
    out_specs = (P("cd", "ab"), P("cd", "ab"))
    return jax.shard_map(
        functools.partial(on_device, x_extent(mesh), mesh.shape["ab"] // x_extent(mesh), mesh.shape["cd"]),
        mesh=mesh,
        in_specs=in_specs,
        out_specs=out_specs,
        check_vma=False,
    )
```
